32 devices in a mesh: gx: 2 (over x), gy: 4 (over y, core), gz: 4 (over z).
Axes of the slice: x: 2, y: 2, z: 4, core: 2. Of those that a mesh axis runs over, the one named last changes fastest.
Arguments:
- node_feat: bfloat16 [16, 32, 32, 128], P('gx', 'gy', 'gz'), may hold values from -6 to 6
- edge_feat: bfloat16 [4, 16, 32, 32, 128], P(None, 'gx', 'gy', 'gz'), may hold values from -6 to 6
- copies: int32 [16, 32, 32], P('gx', 'gy', 'gz'), may hold values from 1 to 8
- offsets: int32 [4, 3], replicated, may hold values from -1 to 1
- w_edge_in: bfloat16 [384, 128], replicated, may hold values from -0.3125 to 0.3125
- w_edge_out: bfloat16 [128, 128], replicated, may hold values from -0.5 to 0.5
- w_node_in: bfloat16 [256, 128], replicated, may hold values from -0.375 to 0.375
- w_node_out: bfloat16 [128, 128], replicated, may hold values from -0.5 to 0.5
- node_cot: bfloat16 [16, 32, 32, 128], P('gx', 'gy', 'gz'), may hold values from -6 to 6
Outputs:
- node_grad: bfloat16 [16, 32, 32, 128], P('gx', 'gy', 'gz')
- edge_grad: bfloat16 [4, 16, 32, 32, 128], P(None, 'gx', 'gy', 'gz')
- grad_edge_in: float32 [384, 128], replicated
- grad_edge_out: float32 [128, 128], replicated
- grad_node_in: float32 [256, 128], replicated
- grad_node_out: float32 [128, 128], replicated
The draws below stay inside these ranges and needn't reach their ends.
Inputs may be any that keep to these rules, and one draw needn't show every extreme that they name: `offsets`: each row is one lattice offset, its three entries along the first, second and third dimension.
All inputs are finite; a program needn't handle non-finite values.
Results may differ from the reference program's by a relative error of at most 0.0068.
Values sent between devices are 32-bit elements; how exact they have to be, the bound alone decides.
A program may use at most 64 MiB of HBM per device.

```python
import math
import jax
import jax.numpy as jnp
from jax import lax

WIDTH = 128
KINDS = 4
BRICK = 8
NX = 16
NY = 32
NZ = 32
N_GX = 2
N_GY = 4
N_GZ = 4


def place_ends(values, rng, low, high):
    longest = values.shape.index(max(values.shape))
    spots = []
    for shift in (0, 1):
        where = [jax.random.randint(jax.random.fold_in(rng, axis), (), 0, length) for axis, length in enumerate(values.shape)]
        where[longest] = (where[longest] + shift) % values.shape[longest]
        spots.append(tuple(where))
    return values.at[spots[0]].set(low).at[spots[1]].set(high)


def block_levels(own_key, extent, shards, least, top_value):
    level, own = 1.0, jax.random.fold_in(own_key, 6)
    for dim, blocks in shards:
        heights = jnp.exp(jax.random.uniform(jax.random.fold_in(own, dim), (blocks,), jnp.float32, least / len(shards), top_value / len(shards)))
        level = level * jnp.repeat(heights, extent[dim] // blocks).reshape([-1 if axis == dim else 1 for axis in range(len(extent))])
    return level


def bell_draw(rng, dims, scale, most, cuts=(), held_as=jnp.bfloat16):
    values = jax.random.normal(rng, dims, jnp.float32) * scale
    if len(cuts) > 0:
        values = block_levels(rng, dims, cuts, -0.22, 0.18) * values
    return jnp.clip(values, min=-most, max=most).astype(held_as)


def setup_inputs(seed: int = 0) -> dict:
    keys = jax.random.split(jax.random.key(seed), 10)
    node_feat = bell_draw(keys[0], (NX, NY, NZ, WIDTH), 1.0, 6.0, ((0, 2), (1, 4), (2, 4)))
    edge_feat = bell_draw(keys[1], (KINDS, NX, NY, NZ, WIDTH), 1.0, 6.0, ((1, 2), (2, 4), (3, 4)))
    copies = place_ends(jax.random.randint(keys[2], (NX, NY, NZ), 1, 9), jax.random.fold_in(keys[2], 1), 1, 8).astype(jnp.int32)
    offsets = place_ends(jax.random.randint(keys[3], (KINDS, 3), -1, 2), jax.random.fold_in(keys[3], 1), -1, 1).astype(jnp.int32)
    w_edge_in = bell_draw(keys[4], (3 * WIDTH, WIDTH), (3 * WIDTH) ** -0.5, 0.3125)
    w_edge_out = bell_draw(keys[5], (WIDTH, WIDTH), WIDTH ** -0.5, 0.5)
    w_node_in = bell_draw(keys[6], (2 * WIDTH, WIDTH), (2 * WIDTH) ** -0.5, 0.375)
    w_node_out = bell_draw(keys[7], (WIDTH, WIDTH), WIDTH ** -0.5, 0.5)
    node_cot = bell_draw(keys[8], (NX, NY, NZ, WIDTH), 1.0, 6.0, ((0, 2), (1, 4), (2, 4)))
    return dict(node_feat=node_feat, edge_feat=edge_feat, copies=copies, offsets=offsets, w_edge_in=w_edge_in, w_edge_out=w_edge_out, w_node_in=w_node_in, w_node_out=w_node_out, node_cot=node_cot)


def neighbour_valid(offset, brick):
    coords = jnp.arange(brick, dtype=jnp.int32)
    inside = [(coords + offset[which] >= 0) & (coords + offset[which] < brick) for which in range(3)]
    joined = inside[0][:, None, None] & inside[1][None, :, None] & inside[2][None, None, :]
    return joined.astype(jnp.float32).reshape(brick * brick * brick, 1)

def moved_view(field, corner):
    padded = jnp.pad(field, ((1, 1), (1, 1), (1, 1), (0, 0)))
    start = (1 + corner).astype(jnp.int32)
    return lax.dynamic_slice(padded, (start[0], start[1], start[2], jnp.int32(0)), field.shape)

def silu_slope(preact):
    sigma = jax.nn.sigmoid(preact)
    return sigma * (1.0 + preact * (1.0 - sigma))

def outer_product(left, right):
    return lax.dot_general(left, right, (((0,), (0,)), ((), ())), preferred_element_type=jnp.float32)

def edge_preact(sender, receiver, feature, w_edge_in, width):
    total = jnp.dot(sender, w_edge_in[:width], preferred_element_type=jnp.float32)
    total = total + jnp.dot(receiver, w_edge_in[width:2 * width], preferred_element_type=jnp.float32)
    return total + jnp.dot(feature, w_edge_in[2 * width:], preferred_element_type=jnp.float32)

def edge_messages(nodes, edges, offsets, w_edge_in, w_edge_out):
    brick = nodes.shape[0]
    width = nodes.shape[3]
    count = brick * brick * brick
    receiver = nodes.reshape(count, width)
    total = jnp.zeros((count, width), jnp.float32)
    preacts = []
    hiddens = []
    for kind_index in range(edges.shape[0]):
        offset = offsets[kind_index]
        sender = moved_view(nodes, offset).reshape(count, width)
        preact = edge_preact(sender, receiver, edges[kind_index].reshape(count, width), w_edge_in, width)
        hidden = jax.nn.silu(preact).astype(jnp.bfloat16)
        message = jnp.dot(hidden, w_edge_out, preferred_element_type=jnp.float32)
        total = total + neighbour_valid(offset, brick) * message
        preacts.append(preact)
        hiddens.append(hidden)
    return (total.reshape(nodes.shape), jnp.stack(preacts), jnp.stack(hiddens))

def node_backward(nodes, summed, copies, node_cot, w_node_in, w_node_out):
    width = nodes.shape[3]
    count = nodes.shape[0] * nodes.shape[1] * nodes.shape[2]
    receiver = nodes.reshape(count, width)
    scale = copies.reshape(count, 1).astype(jnp.float32)
    gathered = (summed.reshape(count, width) / scale).astype(jnp.bfloat16)
    preact = jnp.dot(receiver, w_node_in[:width], preferred_element_type=jnp.float32)
    preact = preact + jnp.dot(gathered, w_node_in[width:], preferred_element_type=jnp.float32)
    hidden = jax.nn.silu(preact).astype(jnp.bfloat16)
    upstream = node_cot.reshape(count, width)
    grad_out = outer_product(hidden, upstream)
    slope = (jnp.dot(upstream, w_node_out.T, preferred_element_type=jnp.float32) * silu_slope(preact)).astype(jnp.bfloat16)
    grad_in = jnp.concatenate([outer_product(receiver, slope), outer_product(gathered, slope)], axis=0)
    to_nodes = jnp.dot(slope, w_node_in[:width].T, preferred_element_type=jnp.float32)
    to_agg = jnp.dot(slope, w_node_in[width:].T, preferred_element_type=jnp.float32) / scale
    return (to_nodes.reshape(nodes.shape), to_agg.reshape(nodes.shape), grad_in, grad_out)

def edge_backward(nodes, edges, offsets, incoming, w_edge_in, w_edge_out, preacts, hiddens):
    brick = nodes.shape[0]
    width = nodes.shape[3]
    count = brick * brick * brick
    receiver = nodes.reshape(count, width)
    arriving = incoming.reshape(count, width)
    grad_in = jnp.zeros((3 * width, width), jnp.float32)
    grad_out = jnp.zeros((width, width), jnp.float32)
    to_nodes = jnp.zeros((count, width), jnp.float32)
    sent_back = jnp.zeros(nodes.shape, jnp.float32)
    edge_grads = []
    for kind_index in range(edges.shape[0]):
        offset = offsets[kind_index]
        sender = moved_view(nodes, offset).reshape(count, width)
        feature = edges[kind_index].reshape(count, width)
        message_cot = (neighbour_valid(offset, brick) * arriving).astype(jnp.bfloat16)
        grad_out = grad_out + outer_product(hiddens[kind_index], message_cot)
        slope = jnp.dot(message_cot, w_edge_out.T, preferred_element_type=jnp.float32) * silu_slope(preacts[kind_index])
        slope = slope.astype(jnp.bfloat16)
        grad_in = grad_in + jnp.concatenate([outer_product(sender, slope), outer_product(receiver, slope), outer_product(feature, slope)], axis=0)
        to_nodes = to_nodes + jnp.dot(slope, w_edge_in[width:2 * width].T, preferred_element_type=jnp.float32)
        from_sender = jnp.dot(slope, w_edge_in[:width].T, preferred_element_type=jnp.float32).reshape(nodes.shape)
        sent_back = sent_back + moved_view(from_sender, -offset)
        edge_grads.append(jnp.dot(slope, w_edge_in[2 * width:].T, preferred_element_type=jnp.float32).astype(jnp.bfloat16).reshape(nodes.shape))
    return (to_nodes.reshape(nodes.shape) + sent_back, jnp.stack(edge_grads), grad_in, grad_out)

def clip_all(grads):
    squares = sum((jnp.sum(single * single) for single in grads))
    entries = sum((single.size for single in grads))
    factor = math.sqrt(entries) / jnp.sqrt(squares)
    return tuple((single * factor for single in grads))

def to_bricks(array):
    rest = array.shape[3:]
    shaped = array.reshape((N_GX, BRICK, N_GY, BRICK, N_GZ, BRICK) + rest)
    order = (0, 2, 4, 1, 3, 5) + tuple(range(6, 6 + len(rest)))
    return jnp.transpose(shaped, order).reshape((N_GX * N_GY * N_GZ, BRICK, BRICK, BRICK) + rest)

def from_bricks(array):
    rest = array.shape[4:]
    shaped = array.reshape((N_GX, N_GY, N_GZ, BRICK, BRICK, BRICK) + rest)
    order = (0, 3, 1, 4, 2, 5) + tuple(range(6, 6 + len(rest)))
    return jnp.transpose(shaped, order).reshape((N_GX * BRICK, N_GY * BRICK, N_GZ * BRICK) + rest)

def shift_blocks(block, brick_axis, forward):
    length = block.shape[brick_axis]
    empty = jnp.zeros_like(lax.slice_in_dim(block, 0, 1, axis=brick_axis))
    if forward:
        return jnp.concatenate([empty, lax.slice_in_dim(block, 0, length - 1, axis=brick_axis)], axis=brick_axis)
    return jnp.concatenate([lax.slice_in_dim(block, 1, length, axis=brick_axis), empty], axis=brick_axis)

def assemble_all(stacked):
    grid = stacked.reshape((N_GX, N_GY, N_GZ, BRICK, BRICK, BRICK) + stacked.shape[4:])
    for brick_axis in range(3):
        local_axis = brick_axis + 3
        lower = lax.slice_in_dim(grid, 0, 1, axis=local_axis)
        upper = lax.slice_in_dim(grid, BRICK - 1, BRICK, axis=local_axis)
        middle = lax.slice_in_dim(grid, 1, BRICK - 1, axis=local_axis)
        new_lower = lower + shift_blocks(upper, brick_axis, True)
        new_upper = upper + shift_blocks(lower, brick_axis, False)
        grid = jnp.concatenate([new_lower, middle, new_upper], axis=local_axis)
    return grid.reshape(stacked.shape)

def reference(node_feat, edge_feat, copies, offsets, w_edge_in, w_edge_out, w_node_in, w_node_out, node_cot):
    width = node_feat.shape[3]
    nodes_b = to_bricks(node_feat)
    edges_b = jnp.moveaxis(to_bricks(jnp.moveaxis(edge_feat, 0, 3)), 4, 1)
    copies_b = to_bricks(copies)
    cot_b = to_bricks(node_cot)

    def forward_one(items):
        return edge_messages(items[0], items[1], offsets, w_edge_in, w_edge_out)[0]
    local_sum = lax.map(forward_one, (nodes_b, edges_b))
    summed = assemble_all(local_sum)

    def node_step(carry, items):
        to_nodes, to_agg, grad_in, grad_out = node_backward(items[0], items[1], items[2], items[3], w_node_in, w_node_out)
        return ((carry[0] + grad_in, carry[1] + grad_out), (to_nodes, to_agg))
    start_node = (jnp.zeros((2 * width, width), jnp.float32), jnp.zeros((width, width), jnp.float32))
    node_grads, node_outputs = lax.scan(node_step, start_node, (nodes_b, summed, copies_b, cot_b))
    node_part, agg_part = node_outputs
    incoming = assemble_all(agg_part)

    def edge_step(carry, items):
        nodes, edges, arriving = items
        unused, preacts, hiddens = edge_messages(nodes, edges, offsets, w_edge_in, w_edge_out)
        to_nodes, edge_grads, grad_in, grad_out = edge_backward(nodes, edges, offsets, arriving, w_edge_in, w_edge_out, preacts, hiddens)
        return ((carry[0] + grad_in, carry[1] + grad_out), (to_nodes, edge_grads))
    start_edge = (jnp.zeros((3 * width, width), jnp.float32), jnp.zeros((width, width), jnp.float32))
    edge_grads_w, edge_outputs = lax.scan(edge_step, start_edge, (nodes_b, edges_b, incoming))
    edge_part, edge_grad_b = edge_outputs
    local = cot_b.astype(jnp.float32) + node_part + edge_part
    node_grad = from_bricks(assemble_all(local)).astype(jnp.bfloat16)
    edge_grad = jnp.moveaxis(from_bricks(jnp.moveaxis(edge_grad_b, 1, 4)), 3, 0)
    clipped = clip_all((edge_grads_w[0], edge_grads_w[1], node_grads[0], node_grads[1]))
    return (node_grad, edge_grad, clipped[0], clipped[1], clipped[2], clipped[3])
```

```python
import functools
import math

import jax
import jax.numpy as jnp
from jax import lax
from jax.experimental import pallas as pl
from jax.experimental.pallas import tpu as pltpu
from jax.sharding import PartitionSpec as P

F32 = jnp.float32
BF16 = jnp.bfloat16
VMEM_MAIN = 28 * 2**20
VMEM_FINISH = 8 * 2**20
AXES = ("gx", "gy", "gz")
MESH = pl.DeviceIdType.MESH
DIRS = [
    (dx, dy, dz)
    for dx in (-1, 0, 1)
    for dy in (-1, 0, 1)
    for dz in (-1, 0, 1)
    if (dx, dy, dz) != (0, 0, 0)
]
DIRS.sort(key=lambda d: -sum(map(abs, d)))


def dot(left, right):
    return jnp.dot(left, right, preferred_element_type=F32)


def dot_t(left, right):
    return lax.dot_general(left, right, (((1,), (1,)), ((), ())), preferred_element_type=F32)


def outer(left, right):
    return lax.dot_general(left, right, (((0,), (0,)), ((), ())), preferred_element_type=F32)


def rim_layout(brick):
    spots, base = {}, 0
    for d in DIRS:
        steps = sum(map(abs, d))
        rows = max(brick ** (3 - steps), 8)
        spots[d] = (base, rows)
        base += rows
    return spots, base


def rim_place(d, sign, brick):
    return [None if s == 0 else (brick - 1 if s * sign > 0 else 0) for s in d]


def rim_slices(d, sign, brick):
    x, y, z = rim_place(d, sign, brick)
    face = brick * brick
    if z is None:
        if y is None:
            return [pl.ds(x * face, face)]
        if x is None:
            return [pl.ds(i * face + y * brick, brick) for i in range(brick)]
        return [pl.ds(x * face + y * brick, brick)]
    if x is None and y is None:
        return [pl.ds(z, face, stride=brick)]
    if y is None:
        return [pl.ds(x * face + z, brick, stride=brick)]
    if x is None:
        return [pl.ds(y * brick + z, brick, stride=face)]
    return [pl.ds(x * face + y * brick + z, 1)]


def rim_load(ref, d, sign, brick):
    parts = [ref[s, :] for s in rim_slices(d, sign, brick)]
    if len(parts) > 1:
        return jnp.concatenate(parts, axis=0)
    if parts[0].shape[0] < 8:
        return jnp.broadcast_to(parts[0], (8, parts[0].shape[1]))
    return parts[0]


def rim_add(ref, d, brick, values):
    slices = rim_slices(d, -1, brick)
    for i, s in enumerate(slices):
        rows = s.size
        ref[s, :] = ref[s, :] + values[i * rows : (i + 1) * rows]


def split(size):
    return 2 if size % 2 == 0 else 1


def kernel(
    sizes,
    offs_hbm, node_hbm, edge_hbm, cop_hbm, wei_hbm, weo_hbm, wni_hbm, wno_hbm, cot_hbm,
    o_node, o_edge, gn, ge,
    offs, node_ref, edges, cop_ref, wei, weo, wni, wno, cot_ref, pad_a, pad_s, sl,
    field, quant, hst, hrc, est, erc,
    ng, eg, cbn, cbe, rbn, rbe, exn, exe,
    in_sem, hs_sem, hr_sem, es_sem, er_sem, cs_s, cs_r, rs_s, rs_r, ex_s, ex_r, ag_s, ag_r, fw_s, fw_r,
):
    width = node_ref.shape[1]
    count = node_ref.shape[0]
    kinds = offs.shape[0]
    brick = pad_a.shape[2]
    cube = (brick, brick, brick, width)
    pos = {a: lax.axis_index(a) for a in AXES}
    spots, rim = rim_layout(brick)

    def fetch_edge(k):
        rows = pl.ds(k * count, count)
        return edge_hbm.at[rows], edges.at[rows]

    moves = (
        [(offs_hbm, offs), (node_hbm, node_ref), (wei_hbm, wei)]
        + [fetch_edge(k) for k in range(kinds)]
        + [(wni_hbm, wni), (cot_hbm, cot_ref), (wno_hbm, wno), (cop_hbm, cop_ref), (weo_hbm, weo)]
    )
    fetches = [pltpu.make_async_copy(src, dst, in_sem.at[i]) for i, (src, dst) in enumerate(moves)]
    for fetch in fetches:
        fetch.start()

    def exists(d, sign):
        ok = None
        for a, step in zip(AXES, d):
            if step != 0:
                here = pos[a] + sign * step
                one = (here >= 0) & (here < sizes[a])
                ok = one if ok is None else ok & one
        return ok

    def shifted(d, sign):
        return {a: pos[a] + sign * step for a, step in zip(AXES, d)}

    low = {a: split(sizes[a]) for a in AXES}
    high = {a: sizes[a] // low[a] for a in AXES}
    in_low = {a: lax.rem(pos[a], low[a]) for a in AXES}
    in_high = {a: pos[a] // low[a] for a in AXES}
    cores = low["gy"]
    ring = (("gx", "low"), ("gy", "high"), ("gz", "low"))
    parts = {"low": (low, in_low), "high": (high, in_high)}
    members = math.prod(parts[p][0][a] for a, p in ring)
    core = in_low["gy"]
    me = 0
    for a, p in ring:
        me = me * parts[p][0][a] + parts[p][1][a]
    rest = [a for a in ("gx", "gz") if high[a] > 1]

    def joined(lows, highs):
        return {a: highs[a] * low[a] + lows[a] for a in AXES}

    sibling = joined({**in_low, "gy": cores - 1 - core}, in_high)

    def member(rank):
        lows, highs = dict(in_low), dict(in_high)
        for a, p in reversed(ring):
            n = parts[p][0][a]
            (lows if p == "low" else highs)[a] = lax.rem(rank, n)
            rank = rank // n
        return joined(lows, highs)

    def across(a, j):
        return joined(in_low, {**in_high, a: lax.rem(in_high[a] + j, high[a])})

    hst[...] = jnp.zeros_like(hst)
    hrc[...] = jnp.zeros_like(hrc)
    erc[...] = jnp.zeros_like(erc)
    barrier = pltpu.get_barrier_semaphore()

    def greet(place):
        pl.semaphore_signal(barrier, inc=1, device_id=place, device_id_type=MESH)

    waits = jnp.int32(cores - 1 + members - 1 + sum(high[a] - 1 for a in rest))
    for d in DIRS:
        ok = exists(d, 1)
        waits = waits + ok.astype(jnp.int32)

        @pl.when(ok)
        def _(d=d):
            greet(shifted(d, 1))

    if cores > 1:
        greet(sibling)
    for j in range(1, members):
        greet(member(lax.rem(me + j, members)))
    for a in rest:
        for j in range(1, high[a]):
            greet(across(a, j))

    def halo_copy(a, i, d, place):
        rows = pl.ds(*spots[d])
        return pltpu.make_async_remote_copy(
            src_ref=hst.at[a, rows],
            dst_ref=hrc.at[a, rows],
            send_sem=hs_sem.at[a, i],
            recv_sem=hr_sem.at[a, i],
            device_id=place,
            device_id_type=MESH,
        )

    def early_copy(i, d, place):
        rows = pl.ds(*spots[d])
        return pltpu.make_async_remote_copy(
            src_ref=est.at[:, rows],
            dst_ref=erc.at[:, rows],
            send_sem=es_sem.at[i],
            recv_sem=er_sem.at[i],
            device_id=place,
            device_id_type=MESH,
        )

    def each(sign, act):
        for i, d in enumerate(DIRS):

            @pl.when(exists(d, sign))
            def _(i=i, d=d):
                act(i, d, shifted(d, sign))

    def halo_start(a, values):
        field[a] = values
        for d in DIRS:
            hst[a, pl.ds(*spots[d]), :] = rim_load(field.at[a], d, 1, brick)
        each(1, lambda i, d, place: halo_copy(a, i, d, place).start())

    def halo_finish(a):
        each(-1, lambda i, d, place: halo_copy(a, i, d, place).wait_recv())
        for d in DIRS:
            rim_add(field.at[a], d, brick, hrc[a, pl.ds(*spots[d]), :])
        return field[a]

    def rows_at(ref, index, rows):
        return ref.at[pl.ds(pl.multiple_of(index * rows, 8), rows)]

    sums = ((ng, cbn, rbn, exn, gn), (eg, cbe, rbe, exe, ge))

    def core_copy(w):
        buf, got = sums[w][:2]
        return pltpu.make_async_remote_copy(
            src_ref=rows_at(buf, cores - 1 - core, buf.shape[0] // cores),
            dst_ref=got,
            send_sem=cs_s.at[w],
            recv_sem=cs_r.at[w],
            device_id=sibling,
            device_id_type=MESH,
        )

    def core_start(w):
        if cores > 1:
            core_copy(w).start()

    def piece(ref, rank):
        return rows_at(ref, core * members + rank, ref.shape[0] // (cores * members))

    def ring_copy(w, j):
        buf, _, got = sums[w][:3]
        to = lax.rem(me + j, members)
        return pltpu.make_async_remote_copy(
            src_ref=piece(buf, to),
            dst_ref=got.at[j],
            send_sem=rs_s.at[w, j],
            recv_sem=rs_r.at[w, j],
            device_id=member(to),
            device_id_type=MESH,
        )

    def ring_start(w):
        if cores > 1:
            buf, got = sums[w][:2]
            half = rows_at(buf, core, buf.shape[0] // cores)
            core_copy(w).wait_recv()
            half[...] = half[...] + got[...]
        for j in range(1, members):
            ring_copy(w, j).start()

    def ring_finish(w):
        buf, _, got = sums[w][:3]
        total = piece(buf, me)[...]
        for j in range(1, members):
            ring_copy(w, j).wait_recv()
            total = total + got[j]
        return total

    bases = []
    base = 0
    for a in rest:
        bases.append(base)
        base += high[a]

    def ex_copy(w, e, j):
        buf = sums[w][3]
        a = rest[e]
        spot = buf.at[bases[e] + in_high[a]]
        return pltpu.make_async_remote_copy(
            src_ref=spot,
            dst_ref=spot,
            send_sem=ex_s.at[w, bases[e] + j],
            recv_sem=ex_r.at[w, bases[e] + j],
            device_id=across(a, j),
            device_id_type=MESH,
        )

    def ex_start(w, e, total):
        sums[w][3][bases[e] + in_high[rest[e]]] = total
        for j in range(1, high[rest[e]]):
            ex_copy(w, e, j).start()

    def ex_finish(w, e):
        buf = sums[w][3]
        for j in range(1, high[rest[e]]):
            ex_copy(w, e, j).wait_recv()
        total = buf[bases[e]]
        for r in range(1, high[rest[e]]):
            total = total + buf[bases[e] + r]
        return total

    def ex_first(w):
        total = ring_finish(w)
        if len(rest) > 0:
            ex_start(w, 0, total)
        return total

    def ex_all(w, total):
        for e in range(len(rest)):
            total = ex_finish(w, e)
            if e + 1 < len(rest):
                ex_start(w, e + 1, total)
        return total

    def share_copy(w, j):
        spot = piece(sums[w][4], me)
        return pltpu.make_async_remote_copy(
            src_ref=spot,
            dst_ref=spot,
            send_sem=ag_s.at[w, j],
            recv_sem=ag_r.at[w, j],
            device_id=member(lax.rem(me + j, members)),
            device_id_type=MESH,
        )

    def pass_copy(w, j):
        spot = piece(sums[w][4], lax.rem(me + members - j, members))
        return pltpu.make_async_remote_copy(
            src_ref=spot,
            dst_ref=spot,
            send_sem=fw_s.at[w, j],
            recv_sem=fw_r.at[w, j],
            device_id=sibling,
            device_id_type=MESH,
        )

    def share_start(w, total):
        piece(sums[w][4], me)[...] = total
        for j in range(1, members):
            share_copy(w, j).start()
        if cores > 1:
            pass_copy(w, 0).start()

    def share_pass(w):
        for j in range(1, members):
            share_copy(w, j).wait_recv()
            if cores > 1:
                pass_copy(w, j).start()

    pad_a[...] = jnp.zeros_like(pad_a)
    pad_s[...] = jnp.zeros_like(pad_s)
    coords = [lax.broadcasted_iota(jnp.int32, cube, axis) for axis in range(3)]
    for fetch in fetches[:3]:
        fetch.wait()
    node = node_ref[...]
    pad_a[1 : brick + 1, 1 : brick + 1] = dot(node, wei[:width]).reshape(cube)
    received = dot(node, wei[width : 2 * width])
    hidden_sum = None
    for k in range(kinds):
        o = [offs[k, axis] for axis in range(3)]
        sent = pad_a[pl.ds(1 + o[0], brick), pl.ds(1 + o[1], brick)]
        sent = pltpu.roll(sent.reshape(brick * brick, brick, width), lax.rem(brick - o[2], brick), 1)
        fetches[3 + k].wait()
        pre = dot(edges[k * count : (k + 1) * count], wei[2 * width :])
        pre = pre + received + sent.reshape(count, width)
        sigma = 0.5 * jnp.tanh(0.5 * pre) + 0.5
        hidden = pre * sigma
        valid = None
        for axis in range(3):
            here = coords[axis] + o[axis]
            one = (here >= 0) & (here < brick)
            valid = one if valid is None else valid & one
        valid = valid.reshape(count, width)
        sl[k] = jnp.where(valid, sigma + hidden * (1.0 - sigma), 0.0)
        hidden = jnp.where(valid, hidden, 0.0).astype(BF16)
        wide = hidden.astype(F32)
        hidden_sum = wide if hidden_sum is None else hidden_sum + wide
    pl.semaphore_wait(barrier, waits)
    halo_start(0, hidden_sum)

    for fetch in fetches[3 + kinds :]:
        fetch.wait()
    cot = cot_ref[...]
    scale_rows = lax.broadcasted_iota(jnp.int32, (count, brick * brick), 0) // brick
    scale_cols = lax.broadcasted_iota(jnp.int32, (count, brick * brick), 1)
    picked = dot(
        (scale_rows == scale_cols).astype(BF16), cop_ref[...].astype(F32).astype(BF16)
    )
    lane = lax.broadcasted_iota(jnp.int32, (count, brick), 1)
    row = lax.broadcasted_iota(jnp.int32, (count, brick), 0) % brick
    picked = jnp.where(lane == row, picked, 0.0).astype(BF16)
    quant[0] = 1.0 / dot(picked, jnp.ones((brick, width), BF16))
    quant[1] = dot(node, wni[:width])
    quant[2] = dot_t(cot, wno[...])
    for q in range(3):
        for d in DIRS:
            est[q, pl.ds(*spots[d]), :] = rim_load(quant.at[q], d, 1, brick)
    each(1, lambda i, d, place: early_copy(i, d, place).start())

    w_out = weo[...]
    twice = jnp.concatenate([w_out, w_out], axis=0)

    def node_step(summed, inverse, own, upstream):
        gathered = (summed * inverse).astype(BF16)
        pre = own + dot(gathered, wni[width:])
        sigma = 0.5 * jnp.tanh(0.5 * pre) + 0.5
        hidden = pre * sigma
        slope = (upstream * (sigma + hidden * (1.0 - sigma))).astype(BF16)
        return gathered, hidden, slope, dot_t(slope, wni[width:]) * inverse

    total = halo_finish(0)
    big = total.astype(BF16)
    small = (total - big.astype(F32)).astype(BF16)
    summed = dot(jnp.concatenate([big, small], axis=1), twice)
    field[0] = summed
    gathered, hidden, slope, to_agg = node_step(summed, quant[0], quant[1], quant[2])
    field[1] = to_agg
    ng[:width] = outer(node, slope)
    ng[width : 2 * width] = outer(gathered, slope)
    ng[2 * width : 3 * width] = outer(hidden.astype(BF16), cot)
    ng[3 * width :] = outer(big, to_agg.astype(BF16))
    core_start(0)

    beyond = jnp.concatenate([rim_load(field.at[0], d, -1, brick) for d in DIRS], axis=0)
    each(-1, lambda i, d, place: early_copy(i, d, place).wait_recv())
    to_rim = node_step(beyond, erc[0], erc[1], erc[2])[3]
    for d in DIRS:
        start, rows = spots[d]
        rim_add(field.at[1], d, brick, to_rim[start : start + rows])

    arriving = field[1].astype(BF16)
    back = dot_t(arriving, w_out)
    slopes = []
    direct = None
    turned = None
    for k in range(kinds):
        o = [offs[k, axis] for axis in range(3)]
        slope_k = (back * sl[k]).astype(BF16)
        slopes.append(slope_k)
        wide = slope_k.astype(F32)
        direct = wide if direct is None else direct + wide
        pad_s[k, 1 : brick + 1, 1 : brick + 1] = wide.reshape(cube)
        moved = pad_s[k, pl.ds(1 - o[0], brick), pl.ds(1 - o[1], brick)]
        moved = pltpu.roll(moved.reshape(brick * brick, brick, width), lax.rem(brick + o[2], brick), 1)
        turned = moved if turned is None else turned + moved
    turned = turned.reshape(count, width).astype(BF16)
    direct = direct.astype(BF16)
    slope_all = jnp.concatenate(slopes, axis=0)
    ring_start(0)
    eg[:width] = outer(node, turned)
    eg[width : 2 * width] = outer(node, direct)
    eg[2 * width :] = outer(edges[...], slope_all)
    core_start(1)
    local = cot.astype(F32) + dot_t(slope, wni[:width])
    local = local + dot_t(turned, wei[:width]) + dot_t(direct, wei[width : 2 * width])
    ring_start(1)
    halo_start(1, local)
    o_edge[...] = dot_t(slope_all, wei[2 * width :]).astype(BF16)
    first = ex_first(0)
    second = ex_first(1)
    share_start(0, ex_all(0, first))
    share_start(1, ex_all(1, second))
    o_node[...] = halo_finish(1).astype(BF16)
    share_pass(0)
    share_pass(1)
    if cores > 1:
        for w in range(2):
            for j in range(members):
                pass_copy(w, j).wait_recv()

    for a in range(2):
        each(1, lambda i, d, place: halo_copy(a, i, d, place).wait_send())
    each(1, lambda i, d, place: early_copy(i, d, place).wait_send())
    for w in range(2):
        if cores > 1:
            core_copy(w).wait_send()
            for j in range(members):
                pass_copy(w, j).wait_send()
        for j in range(1, members):
            ring_copy(w, j).wait_send()
            share_copy(w, j).wait_send()
        for e in range(len(rest)):
            for j in range(1, high[rest[e]]):
                ex_copy(w, e, j).wait_send()


def finish(node_in, edge_in, gn, ge, o_node, o_edge, o_ei, o_eo, o_ni, o_no, s_ei, s_n, sems):
    width = gn.shape[1]
    moves = [
        pltpu.make_async_copy(edge_in, o_edge, sems.at[0]),
        pltpu.make_async_copy(node_in, o_node, sems.at[1]),
    ]
    for move in moves:
        move.start()
    totals = [ref[...] for ref in (gn, ge)]
    squares = sum(jnp.sum(t * t, axis=0, keepdims=True) for t in totals)
    squares = jnp.sum(squares, axis=1, keepdims=True)
    entries = sum(t.shape[0] for t in totals) * width
    factor = math.sqrt(entries) / jnp.sqrt(squares)
    s_n[...] = totals[0] * factor
    outs = ((s_n.at[: 2 * width], o_ni), (s_n.at[2 * width : 3 * width], o_no), (s_n.at[3 * width :], o_eo), (s_ei, o_ei))
    for i, (src, dst) in enumerate(outs):
        if src is s_ei:
            s_ei[...] = totals[1] * factor
        moves.append(pltpu.make_async_copy(src, dst, sems.at[2 + i]))
        moves[-1].start()
    for move in moves:
        move.wait()


def on_device(
    sizes, node_feat, edge_feat, copies, offsets, w_edge_in, w_edge_out, w_node_in, w_node_out, node_cot
):
    brick = node_feat.shape[0]
    width = node_feat.shape[3]
    kinds = edge_feat.shape[0]
    count = brick**3
    _, rim = rim_layout(brick)
    low = {a: split(sizes[a]) for a in AXES}
    high = {a: sizes[a] // low[a] for a in AXES}
    cores = low["gy"]
    members = low["gx"] * high["gy"] * low["gz"]
    others = max(sum(high[a] for a in ("gx", "gz") if high[a] > 1), 1)
    vmem = pl.BlockSpec(memory_space=pltpu.VMEM)
    hbm = pl.BlockSpec(memory_space=pl.ANY)
    far = pl.BlockSpec(memory_space=pltpu.HBM)
    dma = pltpu.SemaphoreType.DMA
    b, w = brick, width
    rows = (4 * w, 3 * w)
    outs = pl.pallas_call(
        functools.partial(kernel, sizes),
        out_shape=(
            jax.ShapeDtypeStruct((count, w), BF16),
            jax.ShapeDtypeStruct((kinds * count, w), BF16),
            *[jax.ShapeDtypeStruct((r, w), F32) for r in rows],
        ),
        in_specs=[far] * 9,
        out_specs=(vmem, vmem, vmem, vmem),
        scratch_shapes=[
            pltpu.SMEM(offsets.shape, jnp.int32),
            pltpu.VMEM((count, w), BF16),
            pltpu.VMEM((kinds * count, w), BF16),
            pltpu.VMEM((b * b, b), jnp.int32),
            pltpu.VMEM((3 * w, w), BF16),
            pltpu.VMEM((w, w), BF16),
            pltpu.VMEM((2 * w, w), BF16),
            pltpu.VMEM((w, w), BF16),
            pltpu.VMEM((count, w), BF16),
            pltpu.VMEM((b + 2, b + 2, b, w), F32),
            pltpu.VMEM((kinds, b + 2, b + 2, b, w), F32),
            pltpu.VMEM((kinds, count, w), F32),
            pltpu.VMEM((2, count, w), F32),
            pltpu.VMEM((3, count, w), F32),
            pltpu.VMEM((2, rim, w), F32),
            pltpu.VMEM((2, rim, w), F32),
            pltpu.VMEM((3, rim, w), F32),
            pltpu.VMEM((3, rim, w), F32),
            *[pltpu.VMEM((r, w), F32) for r in rows],
            *[pltpu.VMEM((r // cores, w), F32) for r in rows],
            *[pltpu.VMEM((members, r // (cores * members), w), F32) for r in rows],
            *[pltpu.VMEM((others, r // (cores * members), w), F32) for r in rows],
            dma((8 + kinds,)),
            dma((2, len(DIRS))),
            dma((2, len(DIRS))),
            dma((len(DIRS),)),
            dma((len(DIRS),)),
            dma((2,)),
            dma((2,)),
            *[dma((2, n)) for n in (members, members, others, others, members, members, members, members)],
        ],
        compiler_params=pltpu.CompilerParams(
            collective_id=0, has_side_effects=True, vmem_limit_bytes=VMEM_MAIN
        ),
    )(
        pltpu.with_memory_space_constraint(offsets, pltpu.HBM),
        *[
            pltpu.with_memory_space_constraint(array, pltpu.HBM)
            for array in (
                node_feat.reshape(count, w),
                edge_feat.reshape(kinds * count, w),
                copies.reshape(b * b, b),
                w_edge_in,
                w_edge_out,
                w_node_in,
                w_node_out,
                node_cot.reshape(count, w),
            )
        ],
    )
    done = pl.pallas_call(
        finish,
        out_shape=(
            jax.ShapeDtypeStruct((count, w), BF16),
            jax.ShapeDtypeStruct((kinds * count, w), BF16),
            jax.ShapeDtypeStruct((3 * w, w), F32),
            jax.ShapeDtypeStruct((w, w), F32),
            jax.ShapeDtypeStruct((2 * w, w), F32),
            jax.ShapeDtypeStruct((w, w), F32),
        ),
        in_specs=[hbm, hbm, vmem, vmem],
        out_specs=(hbm,) * 6,
        scratch_shapes=[pltpu.VMEM((rows[1], w), F32), pltpu.VMEM((rows[0], w), F32), dma((6,))],
        compiler_params=pltpu.CompilerParams(vmem_limit_bytes=VMEM_FINISH),
    )(*outs)
    return (done[0].reshape(node_feat.shape), done[1].reshape(edge_feat.shape)) + tuple(done[2:])


def solution(mesh):
    sizes = {a: mesh.shape[a] for a in AXES}
    bricks, edges = P("gx", "gy", "gz", None), P(None, "gx", "gy", "gz", None)
    return jax.shard_map(
        functools.partial(on_device, sizes),
        mesh=mesh,
        in_specs=(bricks, edges, P("gx", "gy", "gz"), P(), P(), P(), P(), P(), bricks),
        out_specs=(bricks, edges, P(), P(), P(), P()),
        check_vma=False,
    )
```

```python
import functools
import math

import jax
import jax.numpy as jnp
from jax import lax
from jax.experimental import pallas as pl
from jax.experimental.pallas import tpu as pltpu
from jax.sharding import PartitionSpec as P

F32 = jnp.float32
BF16 = jnp.bfloat16
VMEM_MAIN = 28 * 2**20
VMEM_FINISH = 8 * 2**20
AXES = ("gx", "gy", "gz")
MESH = pl.DeviceIdType.MESH
TILE = 8
PLANS = (
    (True, (("gx", "low"), ("gy", "high"), ("gz", "low")), (("gx", "high"), ("gz", "high")), False),
    (True, (("gx", "low"), ("gy", "high"), ("gz", "low")), (("gx", "high"), ("gz", "high")), False),
)
DIRS = [
    (dx, dy, dz)
    for dx in (-1, 0, 1)
    for dy in (-1, 0, 1)
    for dz in (-1, 0, 1)
    if (dx, dy, dz) != (0, 0, 0)
]
DIRS.sort(key=lambda d: -sum(map(abs, d)))


def dot(left, right):
    return jnp.dot(left, right, preferred_element_type=F32)


def dot_t(left, right):
    return lax.dot_general(left, right, (((1,), (1,)), ((), ())), preferred_element_type=F32)


def outer(left, right):
    return lax.dot_general(left, right, (((0,), (0,)), ((), ())), preferred_element_type=F32)


def rim_layout(brick, times, extra):
    spots, base = {}, 0
    for d in reversed(DIRS):
        rows = times * rim_rows(d, brick) + extra
        spots[d] = (base, rows)
        base += rows
    return spots, base


def rim_rows(d, brick):
    return max(brick ** (3 - sum(map(abs, d))), TILE)


def rim_place(d, sign, brick):
    return [None if s == 0 else (brick - 1 if s * sign > 0 else 0) for s in d]


def rim_slices(d, sign, brick):
    x, y, z = rim_place(d, sign, brick)
    face = brick * brick
    if z is None:
        if y is None:
            return [pl.ds(x * face, face)]
        if x is None:
            return [pl.ds(i * face + y * brick, brick) for i in range(brick)]
        return [pl.ds(x * face + y * brick, brick)]
    if x is None and y is None:
        return [pl.ds(z, face, stride=brick)]
    if y is None:
        return [pl.ds(x * face + z, brick, stride=brick)]
    if x is None:
        return [pl.ds(y * brick + z, brick, stride=face)]
    return [pl.ds(x * face + y * brick + z, 1)]


def rim_load(ref, d, sign, brick):
    parts = [ref[s, :] for s in rim_slices(d, sign, brick)]
    if len(parts) > 1:
        return jnp.concatenate(parts, axis=0)
    if parts[0].shape[0] < 8:
        return jnp.broadcast_to(parts[0], (8, parts[0].shape[1]))
    return parts[0]


def rim_add(ref, d, brick, values):
    slices = rim_slices(d, -1, brick)
    for i, s in enumerate(slices):
        rows = s.size
        ref[s, :] = ref[s, :] + values[i * rows : (i + 1) * rows]


def axis_part(sizes, a, part):
    low = 2 if sizes[a] % 2 == 0 else 1
    return {"all": (1, sizes[a]), "low": (1, low), "high": (low, sizes[a] // low)}[part]


def plan_sizes(sizes, plan):
    pre, ring, rest, _ = plan
    cores = axis_part(sizes, "gy", "low")[1] if pre else 1
    members = math.prod(axis_part(sizes, a, p)[1] for a, p in ring)
    rest = [(a, p) for a, p in rest if axis_part(sizes, a, p)[1] > 1]
    return cores, members, rest


class Group:
    def __init__(self, sizes, pos, axes):
        self.pos, self.axes = pos, [(a, *axis_part(sizes, a, p)) for a, p in axes]
        self.size = math.prod(n for _, _, n in self.axes)
        self.rank = 0
        for a, f, n in self.axes:
            self.rank = self.rank * n + lax.rem(pos[a] // f, n)

    def place(self, rank):
        place = dict(self.pos)
        for a, f, n in reversed(self.axes):
            place[a] = place[a] + (lax.rem(rank, n) - lax.rem(self.pos[a] // f, n)) * f
            rank = rank // n
        return place

    def other(self, j):
        return self.place(lax.rem(self.rank + j, self.size))


def kernel(
    sizes,
    offs_hbm, node_hbm, edge_hbm, cop_hbm, wei_hbm, weo_hbm, wni_hbm, wno_hbm, cot_hbm,
    o_node, o_edge, gn, ge,
    offs, node_ref, edges, cop_ref, wei, weo, wni, wno, cot_ref, pad_a, pad_s, sl,
    field, quant, hst0, hrc0, hst1, hrc1, est, erc, zero, spill0, spill1, spille,
    ng, eg, cbn, cbe, rbn, rbe, exn, exe,
    in_sem, rim_sem, sum_sem, ex_sem,
):
    width = node_ref.shape[1]
    count = node_ref.shape[0]
    kinds = offs.shape[0]
    brick = pad_a.shape[2]
    cube = (brick, brick, brick, width)
    pos = {a: lax.axis_index(a) for a in AXES}
    spots, rim = rim_layout(brick, 1, 0)

    moves = (
        [(cop_hbm, cop_ref), (offs_hbm, offs), (node_hbm, node_ref), (wei_hbm, wei), (edge_hbm, edges)]
        + [(wni_hbm, wni), (cot_hbm, cot_ref), (wno_hbm, wno), (weo_hbm, weo)]
    )
    fetches = [pltpu.make_async_copy(src, dst, in_sem.at[i]) for i, (src, dst) in enumerate(moves)]
    for fetch in fetches:
        fetch.start()

    def exists(d, sign):
        ok = None
        for a, step in zip(AXES, d):
            if step != 0:
                here = pos[a] + sign * step
                one = (here >= 0) & (here < sizes[a])
                ok = one if ok is None else ok & one
        return ok

    def shifted(d, sign):
        return {a: pos[a] + sign * step for a, step in zip(AXES, d)}

    plans = []
    for pre, ring, rest, direct in PLANS:
        rest = plan_sizes(sizes, (pre, ring, rest, direct))[2]
        core = Group(sizes, pos, (("gy", "low"),) if pre else ())
        share = Group(sizes, pos, ((("gy", "low"),) if pre and direct else ()) + ring)
        plans.append((core, Group(sizes, pos, ring), [Group(sizes, pos, (ap,)) for ap in rest], share))

    rims = (
        (hst0, hrc0, spill0, rim_layout(brick, 1, TILE)[0]),
        (hst1, hrc1, spill1, spots),
        (est, erc, spille, rim_layout(brick, 2, 0)[0]),
    )
    zero[...] = jnp.zeros_like(zero)
    for r, (src, dst, spill, layout) in enumerate(rims):
        for d in DIRS:
            start, rows = layout[d]
            back = tuple(-step for step in d)

            @pl.when(jnp.logical_not(exists(d, 1)))
            def _(r=r, dst=dst, spill=spill, start=start, rows=rows, other=layout[back][0]):
                blank = zero.at[pl.ds(0, rows)]
                pltpu.make_async_copy(blank, dst.at[pl.ds(other, rows)], rim_sem.at[r, 1]).start()
                pltpu.make_async_copy(blank, spill.at[pl.ds(start, rows)], rim_sem.at[r, 0]).start()

    barrier = pltpu.get_barrier_semaphore()

    def greet(place):
        pl.semaphore_signal(barrier, inc=1, device_id=place, device_id_type=MESH)

    waits = jnp.int32(0)
    for d in DIRS:
        ok = exists(d, 1)
        waits = waits + ok.astype(jnp.int32)

        @pl.when(ok)
        def _(d=d):
            greet(shifted(d, 1))

    met = set()
    for core, ring, rest, share in plans:
        for group in (core, ring, share, *rest):
            key = tuple(group.axes)
            if key not in met:
                met.add(key)
                waits = waits + (group.size - 1)
                for j in range(1, group.size):
                    greet(group.other(j))

    def rim_copy(r, start, rows, place):
        src, dst = rims[r][:2]
        return pltpu.make_async_remote_copy(
            src_ref=src.at[pl.ds(start, rows)],
            dst_ref=dst.at[pl.ds(start, rows)],
            send_sem=rim_sem.at[r, 0],
            recv_sem=rim_sem.at[r, 1],
            device_id=place,
            device_id_type=MESH,
        )

    def rim_start(r):
        for d in DIRS:

            @pl.when(exists(d, 1))
            def _(d=d):
                rim_copy(r, *rims[r][3][d], shifted(d, 1)).start()

    def rim_whole(r):
        return rim_copy(r, 0, rims[r][0].shape[0], pos)

    def rows_at(ref, index, rows):
        return ref.at[pl.ds(pl.multiple_of(index * rows, 8), rows)]

    sums = ((ng, cbn, rbn, exn, gn), (eg, cbe, rbe, exe, ge))

    def sum_copy(w, stage, src, dst, place):
        return pltpu.make_async_remote_copy(
            src_ref=src,
            dst_ref=dst,
            send_sem=sum_sem.at[w, stage, 0],
            recv_sem=sum_sem.at[w, stage, 1],
            device_id=place,
            device_id_type=MESH,
        )

    def core_copy(w):
        core, buf, got = plans[w][0], *sums[w][:2]
        return sum_copy(w, 0, rows_at(buf, 1 - core.rank, got.shape[0]), got, core.other(1))

    def core_start(w):
        if plans[w][0].size > 1:
            core_copy(w).start()

    def piece(w, ref, rank):
        core, ring = plans[w][:2]
        return rows_at(ref, core.rank * ring.size + rank, ref.shape[0] // (core.size * ring.size))

    def ring_copy(w, j):
        ring, buf, got = plans[w][1], sums[w][0], sums[w][2]
        to = lax.rem(ring.rank + j, ring.size)
        return sum_copy(w, 1, piece(w, buf, to), got.at[j - 1], ring.place(to))

    def ring_whole(w):
        got = sums[w][2]
        return sum_copy(w, 1, got, got, pos)

    def ring_start(w):
        core, ring = plans[w][:2]
        if core.size > 1:
            buf, got = sums[w][:2]
            half = rows_at(buf, core.rank, got.shape[0])
            core_copy(w).wait_recv()
            half[...] = half[...] + got[...]
        for j in range(1, ring.size):
            ring_copy(w, j).start()

    def ring_finish(w):
        ring, buf, got = plans[w][1], sums[w][0], sums[w][2]
        ring_whole(w).wait_recv()
        total = piece(w, buf, ring.rank)[...]
        for j in range(1, ring.size):
            total = total + got[j - 1]
        return total

    def ex_spots(w):
        base = 0
        for group in plans[w][2]:
            yield base, group
            base += group.size

    def ex_copy(w, e, j):
        base, group = list(ex_spots(w))[e]
        spot = sums[w][3].at[base + group.rank]
        return pltpu.make_async_remote_copy(
            src_ref=spot,
            dst_ref=spot,
            send_sem=ex_sem.at[w, base + j, 0],
            recv_sem=ex_sem.at[w, base + j, 1],
            device_id=group.other(j),
            device_id_type=MESH,
        )

    def ex_start(w, e, total):
        base, group = list(ex_spots(w))[e]
        sums[w][3][base + group.rank] = total
        for j in range(1, group.size):
            ex_copy(w, e, j).start()

    def ex_finish(w, e):
        base, group = list(ex_spots(w))[e]
        buf = sums[w][3]
        for j in range(1, group.size):
            ex_copy(w, e, j).wait_recv()
        total = buf[base]
        for r in range(1, group.size):
            total = total + buf[base + r]
        return total

    def ex_first(w):
        total = ring_finish(w)
        if len(plans[w][2]) > 0:
            ex_start(w, 0, total)
        return total

    def ex_all(w, total):
        for e in range(len(plans[w][2])):
            total = ex_finish(w, e)
            if e + 1 < len(plans[w][2]):
                ex_start(w, e + 1, total)
        return total

    def share_start(w, total):
        _, ring, _, share = plans[w]
        spot = piece(w, sums[w][4], ring.rank)
        spot[...] = total
        for j in range(1, share.size):
            sum_copy(w, 2, spot, spot, share.other(j)).start()

    def share_whole(w):
        ring, share, out = plans[w][1], plans[w][3], sums[w][4]
        core = plans[w][0].size
        rows = out.shape[0] // (core * ring.size) * (share.size - 1)
        some = out.at[pl.ds(0, rows)]
        return sum_copy(w, 2, some, some, pos)

    def passes(w):
        core, ring, _, share = plans[w]
        return core.size > 1 and share.size == ring.size

    def pass_copy(w):
        core, out = plans[w][0], sums[w][4]
        half = rows_at(out, core.rank, out.shape[0] // core.size)
        return sum_copy(w, 3, half, half, core.other(1))

    def share_finish(w):
        share_whole(w).wait_recv()
        if passes(w):
            pass_copy(w).start()

    def rows_of(ref, slices):
        return jnp.concatenate([ref[pl.ds(start, rows), :] for start, rows in slices], axis=0)

    order = list(reversed(DIRS))
    pad_a[...] = jnp.zeros_like(pad_a)
    pad_s[...] = jnp.zeros_like(pad_s)
    coords = [lax.broadcasted_iota(jnp.int32, cube, axis) for axis in range(3)]

    fetches[0].wait()
    scale_rows = lax.broadcasted_iota(jnp.int32, (count, brick * brick), 0) // brick
    scale_cols = lax.broadcasted_iota(jnp.int32, (count, brick * brick), 1)
    picked = dot(
        (scale_rows == scale_cols).astype(BF16), cop_ref[...].astype(F32).astype(BF16)
    )
    lane = lax.broadcasted_iota(jnp.int32, (count, brick), 1)
    row = lax.broadcasted_iota(jnp.int32, (count, brick), 0) % brick
    picked = jnp.where(lane == row, picked, 0.0).astype(BF16)
    quant[0] = dot(picked, jnp.ones((brick, width), BF16))
    rim_lane = lax.broadcasted_iota(jnp.int32, (rim, width), 1)
    rim_row = lax.broadcasted_iota(jnp.int32, (rim, width), 0) % TILE
    divisors = jnp.concatenate([rim_load(quant.at[0], d, 1, brick) for d in order], axis=0)
    divisors = jnp.where(rim_lane == rim_row, divisors, 0.0).astype(BF16)
    groups = -(-rim // (TILE * TILE)) * TILE
    gather = lax.broadcasted_iota(jnp.int32, (groups, rim), 1) // TILE
    gather = (gather == lax.broadcasted_iota(jnp.int32, (groups, rim), 0)).astype(BF16)
    compact = dot(gather, divisors)
    for d in order:
        start, rows = rims[0][3][d]
        first, n = spots[d][0] // TILE, rim_rows(d, brick) // TILE
        tile = compact[first : first + n]
        hst0[pl.ds(start + rows - TILE, TILE), :] = tile if n == TILE else jnp.broadcast_to(tile[:1], (TILE, width))

    for fetch in fetches[1:4]:
        fetch.wait()
    node = node_ref[...]
    pad_a[1 : brick + 1, 1 : brick + 1] = dot(node, wei[:width]).reshape(cube)
    received = dot(node, wei[width : 2 * width])
    fetches[4].wait()
    hidden_sum = None
    for k in range(kinds):
        o = [offs[k, axis] for axis in range(3)]
        sent = pad_a[pl.ds(1 + o[0], brick), pl.ds(1 + o[1], brick)]
        sent = pltpu.roll(sent.reshape(brick * brick, brick, width), lax.rem(brick - o[2], brick), 1)
        pre = dot(edges[k * count : (k + 1) * count], wei[2 * width :])
        pre = pre + received + sent.reshape(count, width)
        sigma = 0.5 * jnp.tanh(0.5 * pre) + 0.5
        hidden = pre * sigma
        valid = None
        for axis in range(3):
            here = coords[axis] + o[axis]
            one = (here >= 0) & (here < brick)
            valid = one if valid is None else valid & one
        valid = valid.reshape(count, width)
        sl[k] = jnp.where(valid, sigma + hidden * (1.0 - sigma), 0.0)
        hidden = jnp.where(valid, hidden, 0.0).astype(BF16)
        wide = hidden.astype(F32)
        hidden_sum = wide if hidden_sum is None else hidden_sum + wide
    field[0] = hidden_sum
    for d in order:
        start = rims[0][3][d][0]
        hst0[pl.ds(start, rim_rows(d, brick)), :] = rim_load(field.at[0], d, 1, brick)
    pl.semaphore_wait(barrier, waits)
    rim_start(0)

    for fetch in fetches[5:]:
        fetch.wait()
    cot = cot_ref[...]
    quant[1] = dot(node, wni[:width])
    quant[2] = dot_t(cot, wno[...])
    for d in order:
        start, n = rims[2][3][d][0], rim_rows(d, brick)
        for q in (1, 2):
            est[pl.ds(start + (q - 1) * n, n), :] = rim_load(quant.at[q], d, 1, brick)
    rim_start(2)

    w_out = weo[...]
    twice = jnp.concatenate([w_out, w_out], axis=0)
    tiles = TILE * len(order)
    faces = 6 * brick * brick
    place = lax.broadcasted_iota(jnp.int32, (rim, tiles), 0)
    place = jnp.where(place < faces, place // TILE, faces // TILE + (place - faces) // TILE * TILE)
    spread = (place == lax.broadcasted_iota(jnp.int32, (rim, tiles), 1)).astype(BF16)

    def node_step(summed, inverse, own, upstream):
        gathered = (summed * inverse).astype(BF16)
        pre = own + dot(gathered, wni[width:])
        sigma = 0.5 * jnp.tanh(0.5 * pre) + 0.5
        hidden = pre * sigma
        slope = (upstream * (sigma + hidden * (1.0 - sigma))).astype(BF16)
        return gathered, hidden, slope, dot_t(slope, wni[width:]) * inverse

    rim_whole(0).wait_recv()
    for d in order:
        rim_add(field.at[0], d, brick, hrc0[pl.ds(rims[0][3][d][0], rim_rows(d, brick)), :])
    total = field[0]
    big = total.astype(BF16)
    small = (total - big.astype(F32)).astype(BF16)
    summed = dot(jnp.concatenate([big, small], axis=1), twice)
    field[0] = summed
    gathered, hidden, slope, to_agg = node_step(summed, 1.0 / quant[0], quant[1], quant[2])
    field[1] = to_agg
    ng[:width] = outer(node, slope)
    ng[width : 2 * width] = outer(gathered, slope)
    ng[2 * width : 3 * width] = outer(hidden.astype(BF16), cot)
    ng[3 * width :] = outer(big, to_agg.astype(BF16))
    core_start(0)

    compact = rows_of(hrc0, [(sum(rims[0][3][d]) - TILE, TILE) for d in order]).astype(BF16)
    divisors = jnp.where(rim_lane == rim_row, dot(spread, compact), 0.0).astype(BF16)
    divisors = jnp.maximum(dot(divisors, jnp.ones((width, width), BF16)), 1.0)
    beyond = jnp.concatenate([rim_load(field.at[0], d, -1, brick) for d in order], axis=0)
    rim_whole(2).wait_recv()
    own = rows_of(erc, [(rims[2][3][d][0], rim_rows(d, brick)) for d in order])
    upstream = rows_of(erc, [(rims[2][3][d][0] + rim_rows(d, brick), rim_rows(d, brick)) for d in order])
    to_rim = node_step(beyond, 1.0 / divisors, own, upstream)[3]
    for d in order:
        start, rows = spots[d]
        rim_add(field.at[1], d, brick, to_rim[start : start + rows])

    arriving = field[1].astype(BF16)
    back = dot_t(arriving, w_out)
    slopes = []
    direct = None
    turned = None
    for k in range(kinds):
        o = [offs[k, axis] for axis in range(3)]
        slope_k = (back * sl[k]).astype(BF16)
        slopes.append(slope_k)
        wide = slope_k.astype(F32)
        direct = wide if direct is None else direct + wide
        pad_s[k, 1 : brick + 1, 1 : brick + 1] = wide.reshape(cube)
        moved = pad_s[k, pl.ds(1 - o[0], brick), pl.ds(1 - o[1], brick)]
        moved = pltpu.roll(moved.reshape(brick * brick, brick, width), lax.rem(brick + o[2], brick), 1)
        turned = moved if turned is None else turned + moved
    turned = turned.reshape(count, width).astype(BF16)
    direct = direct.astype(BF16)
    slope_all = jnp.concatenate(slopes, axis=0)
    ring_start(0)
    eg[:width] = outer(node, turned)
    eg[width : 2 * width] = outer(node, direct)
    eg[2 * width :] = outer(edges[...], slope_all)
    core_start(1)
    local = cot.astype(F32) + dot_t(slope, wni[:width])
    local = local + dot_t(turned, wei[:width]) + dot_t(direct, wei[width : 2 * width])
    field[1] = local
    ring_start(1)
    for d in order:
        hst1[pl.ds(*spots[d]), :] = rim_load(field.at[1], d, 1, brick)
    rim_start(1)
    o_edge[...] = dot_t(slope_all, wei[2 * width :]).astype(BF16)
    firsts = [ex_first(w) for w in range(2)]
    for w in range(2):
        share_start(w, ex_all(w, firsts[w]))
    rim_whole(1).wait_recv()
    for d in order:
        rim_add(field.at[1], d, brick, hrc1[pl.ds(*spots[d]), :])
    o_node[...] = field[1].astype(BF16)
    for w in range(2):
        share_finish(w)
    for w in range(2):
        if passes(w):
            pass_copy(w).wait_recv()

    for r in range(3):
        rim_whole(r).wait_send()
    for w in range(2):
        if plans[w][0].size > 1:
            core_copy(w).wait_send()
        ring_whole(w).wait_send()
        share_whole(w).wait_send()
        if passes(w):
            pass_copy(w).wait_send()
        for e, (base, group) in enumerate(ex_spots(w)):
            for j in range(1, group.size):
                ex_copy(w, e, j).wait_send()


def finish(node_in, edge_in, gn, ge, o_node, o_edge, o_ei, o_eo, o_ni, o_no, s_ei, s_n, sems):
    width = gn.shape[1]
    moves = [
        pltpu.make_async_copy(edge_in, o_edge, sems.at[0]),
        pltpu.make_async_copy(node_in, o_node, sems.at[1]),
    ]
    for move in moves:
        move.start()
    totals = [ref[...] for ref in (gn, ge)]
    squares = sum(jnp.sum(t * t, axis=0, keepdims=True) for t in totals)
    squares = jnp.sum(squares, axis=1, keepdims=True)
    entries = sum(t.shape[0] for t in totals) * width
    factor = math.sqrt(entries) / jnp.sqrt(squares)
    s_n[...] = totals[0] * factor
    outs = ((s_n.at[: 2 * width], o_ni), (s_n.at[2 * width : 3 * width], o_no), (s_n.at[3 * width :], o_eo), (s_ei, o_ei))
    for i, (src, dst) in enumerate(outs):
        if src is s_ei:
            s_ei[...] = totals[1] * factor
        moves.append(pltpu.make_async_copy(src, dst, sems.at[2 + i]))
        moves[-1].start()
    for move in moves:
        move.wait()


def on_device(
    sizes, node_feat, edge_feat, copies, offsets, w_edge_in, w_edge_out, w_node_in, w_node_out, node_cot
):
    brick = node_feat.shape[0]
    width = node_feat.shape[3]
    kinds = edge_feat.shape[0]
    count = brick**3
    rims = [rim_layout(brick, *how)[1] for how in ((1, TILE), (1, 0), (2, 0))]
    dims = [plan_sizes(sizes, plan) for plan in PLANS]
    others = [max(sum(axis_part(sizes, a, p)[1] for a, p in rest), 1) for _, _, rest in dims]
    vmem = pl.BlockSpec(memory_space=pltpu.VMEM)
    hbm = pl.BlockSpec(memory_space=pl.ANY)
    far = pl.BlockSpec(memory_space=pltpu.HBM)
    dma = pltpu.SemaphoreType.DMA
    b, w = brick, width
    rows = (4 * w, 3 * w)
    outs = pl.pallas_call(
        functools.partial(kernel, sizes),
        out_shape=(
            jax.ShapeDtypeStruct((count, w), BF16),
            jax.ShapeDtypeStruct((kinds * count, w), BF16),
            *[jax.ShapeDtypeStruct((r, w), F32) for r in rows],
        ),
        in_specs=[far] * 9,
        out_specs=(vmem, vmem, vmem, vmem),
        scratch_shapes=[
            pltpu.SMEM(offsets.shape, jnp.int32),
            pltpu.VMEM((count, w), BF16),
            pltpu.VMEM((kinds * count, w), BF16),
            pltpu.VMEM((b * b, b), jnp.int32),
            pltpu.VMEM((3 * w, w), BF16),
            pltpu.VMEM((w, w), BF16),
            pltpu.VMEM((2 * w, w), BF16),
            pltpu.VMEM((w, w), BF16),
            pltpu.VMEM((count, w), BF16),
            pltpu.VMEM((b + 2, b + 2, b, w), F32),
            pltpu.VMEM((kinds, b + 2, b + 2, b, w), F32),
            pltpu.VMEM((kinds, count, w), F32),
            pltpu.VMEM((2, count, w), F32),
            pltpu.VMEM((3, count, w), F32),
            *[pltpu.VMEM((r, w), F32) for r in (rims[0], rims[0], rims[1], rims[1], rims[2], rims[2])],
            pltpu.VMEM((2 * b * b + TILE, w), F32),
            *[pltpu.VMEM((r, w), F32) for r in rims],
            *[pltpu.VMEM((r, w), F32) for r in rows],
            *[pltpu.VMEM((r // c, w), F32) for r, (c, _, _) in zip(rows, dims)],
            *[pltpu.VMEM((m - 1, r // (c * m), w), F32) for r, (c, m, _) in zip(rows, dims)],
            *[pltpu.VMEM((n, r // (c * m), w), F32) for r, n, (c, m, _) in zip(rows, others, dims)],
            dma((9,)),
            dma((3, 2)),
            dma((2, 4, 2)),
            dma((2, max(others), 2)),
        ],
        compiler_params=pltpu.CompilerParams(
            collective_id=0, has_side_effects=True, vmem_limit_bytes=VMEM_MAIN
        ),
    )(
        pltpu.with_memory_space_constraint(offsets, pltpu.HBM),
        *[
            pltpu.with_memory_space_constraint(array, pltpu.HBM)
            for array in (
                node_feat.reshape(count, w),
                edge_feat.reshape(kinds * count, w),
                copies.reshape(b * b, b),
                w_edge_in,
                w_edge_out,
                w_node_in,
                w_node_out,
                node_cot.reshape(count, w),
            )
        ],
    )
    done = pl.pallas_call(
        finish,
        out_shape=(
            jax.ShapeDtypeStruct((count, w), BF16),
            jax.ShapeDtypeStruct((kinds * count, w), BF16),
            jax.ShapeDtypeStruct((3 * w, w), F32),
            jax.ShapeDtypeStruct((w, w), F32),
            jax.ShapeDtypeStruct((2 * w, w), F32),
            jax.ShapeDtypeStruct((w, w), F32),
        ),
        in_specs=[hbm, hbm, vmem, vmem],
        out_specs=(hbm,) * 6,
        scratch_shapes=[pltpu.VMEM((rows[1], w), F32), pltpu.VMEM((rows[0], w), F32), dma((6,))],
        compiler_params=pltpu.CompilerParams(vmem_limit_bytes=VMEM_FINISH),
    )(*outs)
    return (done[0].reshape(node_feat.shape), done[1].reshape(edge_feat.shape)) + tuple(done[2:])


def solution(mesh):
    sizes = {a: mesh.shape[a] for a in AXES}
    bricks, edges = P("gx", "gy", "gz", None), P(None, "gx", "gy", "gz", None)
    return jax.shard_map(
        functools.partial(on_device, sizes),
        mesh=mesh,
        in_specs=(bricks, edges, P("gx", "gy", "gz"), P(), P(), P(), P(), P(), bricks),
        out_specs=(bricks, edges, P(), P(), P(), P()),
        check_vma=False,
    )
```

```python
import functools
import math

import jax
import jax.numpy as jnp
from jax import lax
from jax.experimental import pallas as pl
from jax.experimental.pallas import tpu as pltpu
from jax.sharding import PartitionSpec as P

F32 = jnp.float32
BF16 = jnp.bfloat16
VMEM_MAIN = 28 * 2**20
VMEM_FINISH = 8 * 2**20
AXES = ("gx", "gy", "gz")
MESH = pl.DeviceIdType.MESH
TILE = 8
PLANS = (
    (True, (("gx", "low"), ("gy", "high"), ("gz", "low")), (("gx", "high"), ("gz", "high")), False),
    (True, (("gx", "low"), ("gy", "high"), ("gz", "low")), (("gx", "high"), ("gz", "high")), False),
)
DIRS = [
    (dx, dy, dz)
    for dx in (-1, 0, 1)
    for dy in (-1, 0, 1)
    for dz in (-1, 0, 1)
    if (dx, dy, dz) != (0, 0, 0)
]
DIRS.sort(key=lambda d: -sum(map(abs, d)))


def dot(left, right):
    return jnp.dot(left, right, preferred_element_type=F32)


def dot_t(left, right):
    return lax.dot_general(left, right, (((1,), (1,)), ((), ())), preferred_element_type=F32)


def outer(left, right):
    return lax.dot_general(left, right, (((0,), (0,)), ((), ())), preferred_element_type=F32)


def rim_layout(brick, times, extra):
    spots, base = {}, 0
    for d in reversed(DIRS):
        rows = times * rim_rows(d, brick) + extra
        spots[d] = (base, rows)
        base += rows
    return spots, base


def rim_rows(d, brick):
    return max(brick ** (3 - sum(map(abs, d))), TILE)


def rim_place(d, sign, brick):
    return [None if s == 0 else (brick - 1 if s * sign > 0 else 0) for s in d]


def rim_slices(d, sign, brick):
    x, y, z = rim_place(d, sign, brick)
    face = brick * brick
    if z is None:
        if y is None:
            return [pl.ds(x * face, face)]
        if x is None:
            return [pl.ds(i * face + y * brick, brick) for i in range(brick)]
        return [pl.ds(x * face + y * brick, brick)]
    if x is None and y is None:
        return [pl.ds(z, face, stride=brick)]
    if y is None:
        return [pl.ds(x * face + z, brick, stride=brick)]
    if x is None:
        return [pl.ds(y * brick + z, brick, stride=face)]
    return [pl.ds(x * face + y * brick + z, 1)]


def rim_load(ref, d, sign, brick):
    parts = [ref[s, :] for s in rim_slices(d, sign, brick)]
    if len(parts) > 1:
        return jnp.concatenate(parts, axis=0)
    if parts[0].shape[0] < 8:
        return jnp.broadcast_to(parts[0], (8, parts[0].shape[1]))
    return parts[0]


def rim_add(ref, d, brick, values):
    slices = rim_slices(d, -1, brick)
    for i, s in enumerate(slices):
        rows = s.size
        ref[s, :] = ref[s, :] + values[i * rows : (i + 1) * rows]


def axis_part(sizes, a, part):
    low = 2 if sizes[a] % 2 == 0 else 1
    return {"all": (1, sizes[a]), "low": (1, low), "high": (low, sizes[a] // low)}[part]


def plan_sizes(sizes, plan):
    pre, ring, rest, _ = plan
    cores = axis_part(sizes, "gy", "low")[1] if pre else 1
    members = math.prod(axis_part(sizes, a, p)[1] for a, p in ring)
    rest = [(a, p) for a, p in rest if axis_part(sizes, a, p)[1] > 1]
    return cores, members, rest


class Group:
    def __init__(self, sizes, pos, axes):
        self.pos, self.axes = pos, [(a, *axis_part(sizes, a, p)) for a, p in axes]
        self.size = math.prod(n for _, _, n in self.axes)
        self.rank = 0
        for a, f, n in self.axes:
            self.rank = self.rank * n + lax.rem(pos[a] // f, n)

    def place(self, rank):
        place = dict(self.pos)
        for a, f, n in reversed(self.axes):
            place[a] = place[a] + (lax.rem(rank, n) - lax.rem(self.pos[a] // f, n)) * f
            rank = rank // n
        return place

    def other(self, j):
        return self.place(lax.rem(self.rank + j, self.size))


def kernel(
    sizes,
    offs_hbm, node_hbm, edge_hbm, cop_hbm, wei_hbm, weo_hbm, wni_hbm, wno_hbm, cot_hbm,
    o_node, o_edge, gn, ge,
    offs, node_ref, edges, cop_ref, wei, weo, wni, wno, cot_ref, pad_a, pad_s, sl,
    field, quant, hst0, hrc0, hst1, hrc1, est, erc, zero, spill,
    ng, eg, cbn, cbe, rbn, rbe, exn, exe,
    in_sem, rim_sem, sum_sem, ex_sem,
):
    width = node_ref.shape[1]
    count = node_ref.shape[0]
    kinds = offs.shape[0]
    brick = pad_a.shape[2]
    cube = (brick, brick, brick, width)
    pos = {a: lax.axis_index(a) for a in AXES}
    spots, rim = rim_layout(brick, 1, 0)

    moves = (
        [(cop_hbm, cop_ref), (offs_hbm, offs), (node_hbm, node_ref), (wei_hbm, wei), (edge_hbm, edges)]
        + [(wni_hbm, wni), (cot_hbm, cot_ref), (wno_hbm, wno), (weo_hbm, weo)]
    )
    fetches = [pltpu.make_async_copy(src, dst, in_sem.at[i]) for i, (src, dst) in enumerate(moves)]
    for fetch in fetches[:5]:
        fetch.start()

    inside = {(a, s): (pos[a] + s >= 0) & (pos[a] + s < sizes[a]) for a in AXES for s in (-1, 1)}
    there = {d: functools.reduce(jnp.logical_and, [inside[a, s] for a, s in zip(AXES, d) if s != 0]) for d in DIRS}

    def shifted(d, sign):
        return {a: pos[a] + sign * step for a, step in zip(AXES, d)}

    plans = []
    for pre, ring, rest, direct in PLANS:
        rest = plan_sizes(sizes, (pre, ring, rest, direct))[2]
        core = Group(sizes, pos, (("gy", "low"),) if pre else ())
        share = Group(sizes, pos, ((("gy", "low"),) if pre and direct else ()) + ring)
        plans.append((core, Group(sizes, pos, ring), [Group(sizes, pos, (ap,)) for ap in rest], share))

    rims = (
        (hst0, hrc0, rim_layout(brick, 1, TILE)[0]),
        (hst1, hrc1, spots),
        (est, erc, rim_layout(brick, 2, 0)[0]),
    )
    unsent = rim_layout(brick, 4, TILE)[0]
    barrier = pltpu.get_barrier_semaphore()

    def greet(place):
        pl.semaphore_signal(barrier, inc=1, device_id=place, device_id_type=MESH)

    waits = jnp.int32(0)
    for d in DIRS:
        waits = waits + there[d].astype(jnp.int32)

        @pl.when(there[d])
        def _(d=d):
            greet(shifted(d, 1))

    met = set()
    for core, ring, rest, share in plans:
        for group in (core, ring, share, *rest):
            key = tuple(group.axes)
            if key not in met:
                met.add(key)
                waits = waits + (group.size - 1)
                for j in range(1, group.size):
                    greet(group.other(j))

    for fetch in fetches[5:]:
        fetch.start()
    def rim_copy(r, start, rows, place):
        src, dst = rims[r][:2]
        return pltpu.make_async_remote_copy(
            src_ref=src.at[pl.ds(start, rows)],
            dst_ref=dst.at[pl.ds(start, rows)],
            send_sem=rim_sem.at[3],
            recv_sem=rim_sem.at[r],
            device_id=place,
            device_id_type=MESH,
        )

    def rim_start(r):
        for d in DIRS:

            @pl.when(there[d])
            def _(d=d):
                rim_copy(r, *rims[r][2][d], shifted(d, 1)).start()

    def rim_whole(r):
        return rim_copy(r, 0, rims[r][0].shape[0], pos)

    def rows_at(ref, index, rows):
        return ref.at[pl.ds(pl.multiple_of(index * rows, 8), rows)]

    sums = ((ng, cbn, rbn, exn, gn), (eg, cbe, rbe, exe, ge))

    def sum_copy(w, stage, src, dst, place):
        return pltpu.make_async_remote_copy(
            src_ref=src,
            dst_ref=dst,
            send_sem=sum_sem.at[w, stage, 0],
            recv_sem=sum_sem.at[w, stage, 1],
            device_id=place,
            device_id_type=MESH,
        )

    def core_copy(w):
        core, buf, got = plans[w][0], *sums[w][:2]
        return sum_copy(w, 0, rows_at(buf, 1 - core.rank, got.shape[0]), got, core.other(1))

    def core_start(w):
        if plans[w][0].size > 1:
            core_copy(w).start()

    def piece(w, ref, rank):
        core, ring = plans[w][:2]
        return rows_at(ref, core.rank * ring.size + rank, ref.shape[0] // (core.size * ring.size))

    def ring_copy(w, j):
        ring, buf, got = plans[w][1], sums[w][0], sums[w][2]
        to = lax.rem(ring.rank + j, ring.size)
        return sum_copy(w, 1, piece(w, buf, to), got.at[j - 1], ring.place(to))

    def ring_whole(w):
        got = sums[w][2]
        return sum_copy(w, 1, got, got, pos)

    def ring_start(w):
        core, ring = plans[w][:2]
        if core.size > 1:
            buf, got = sums[w][:2]
            half = rows_at(buf, core.rank, got.shape[0])
            core_copy(w).wait_recv()
            half[...] = half[...] + got[...]
        for j in range(1, ring.size):
            ring_copy(w, j).start()

    def ring_finish(w):
        ring, buf, got = plans[w][1], sums[w][0], sums[w][2]
        ring_whole(w).wait_recv()
        total = piece(w, buf, ring.rank)[...]
        for j in range(1, ring.size):
            total = total + got[j - 1]
        return total

    def ex_spots(w):
        base = 0
        for group in plans[w][2]:
            yield base, group
            base += group.size

    def ex_copy(w, e, j):
        base, group = list(ex_spots(w))[e]
        spot = sums[w][3].at[base + group.rank]
        return pltpu.make_async_remote_copy(
            src_ref=spot,
            dst_ref=spot,
            send_sem=ex_sem.at[w, base + j, 0],
            recv_sem=ex_sem.at[w, base + j, 1],
            device_id=group.other(j),
            device_id_type=MESH,
        )

    def ex_start(w, e, total):
        base, group = list(ex_spots(w))[e]
        sums[w][3][base + group.rank] = total
        for j in range(1, group.size):
            ex_copy(w, e, j).start()

    def ex_finish(w, e):
        base, group = list(ex_spots(w))[e]
        buf = sums[w][3]
        for j in range(1, group.size):
            ex_copy(w, e, j).wait_recv()
        total = buf[base]
        for r in range(1, group.size):
            total = total + buf[base + r]
        return total

    def ex_first(w):
        total = ring_finish(w)
        if len(plans[w][2]) > 0:
            ex_start(w, 0, total)
        return total

    def ex_all(w, total):
        for e in range(len(plans[w][2])):
            total = ex_finish(w, e)
            if e + 1 < len(plans[w][2]):
                ex_start(w, e + 1, total)
        return total

    def share_start(w, total):
        _, ring, _, share = plans[w]
        spot = piece(w, sums[w][4], ring.rank)
        spot[...] = total
        for j in range(1, share.size):
            sum_copy(w, 2, spot, spot, share.other(j)).start()

    def share_whole(w):
        ring, share, out = plans[w][1], plans[w][3], sums[w][4]
        core = plans[w][0].size
        rows = out.shape[0] // (core * ring.size) * (share.size - 1)
        some = out.at[pl.ds(0, rows)]
        return sum_copy(w, 2, some, some, pos)

    def passes(w):
        core, ring, _, share = plans[w]
        return core.size > 1 and share.size == ring.size

    def pass_copy(w):
        core, out = plans[w][0], sums[w][4]
        half = rows_at(out, core.rank, out.shape[0] // core.size)
        return sum_copy(w, 3, half, half, core.other(1))

    def share_finish(w):
        share_whole(w).wait_recv()
        if passes(w):
            pass_copy(w).start()

    def rows_of(ref, slices):
        return jnp.concatenate([ref[pl.ds(start, rows), :] for start, rows in slices], axis=0)

    order = list(reversed(DIRS))
    pad_a[...] = jnp.zeros_like(pad_a)
    pad_s[...] = jnp.zeros_like(pad_s)
    coords = [lax.broadcasted_iota(jnp.int32, cube, axis) for axis in range(3)]

    fetches[0].wait()
    scale_rows = lax.broadcasted_iota(jnp.int32, (count, brick * brick), 0) // brick
    scale_cols = lax.broadcasted_iota(jnp.int32, (count, brick * brick), 1)
    picked = dot(
        (scale_rows == scale_cols).astype(BF16), cop_ref[...].astype(F32).astype(BF16)
    )
    lane = lax.broadcasted_iota(jnp.int32, (count, brick), 1)
    row = lax.broadcasted_iota(jnp.int32, (count, brick), 0) % brick
    picked = jnp.where(lane == row, picked, 0.0).astype(BF16)
    quant[0] = dot(picked, jnp.ones((brick, width), BF16))
    rim_lane = lax.broadcasted_iota(jnp.int32, (rim, width), 1)
    rim_row = lax.broadcasted_iota(jnp.int32, (rim, width), 0) % TILE
    divisors = jnp.concatenate([rim_load(quant.at[0], d, 1, brick) for d in order], axis=0)
    divisors = jnp.where(rim_lane == rim_row, divisors, 0.0).astype(BF16)
    groups = -(-rim // (TILE * TILE)) * TILE
    gather = lax.broadcasted_iota(jnp.int32, (groups, rim), 1) // TILE
    gather = (gather == lax.broadcasted_iota(jnp.int32, (groups, rim), 0)).astype(BF16)
    compact = dot(gather, divisors)
    for d in order:
        start, rows = rims[0][2][d]
        first, n = spots[d][0] // TILE, rim_rows(d, brick) // TILE
        tile = compact[first : first + n]
        hst0[pl.ds(start + rows - TILE, TILE), :] = tile if n == TILE else jnp.broadcast_to(tile[:1], (TILE, width))

    for fetch in fetches[1:4]:
        fetch.wait()
    node = node_ref[...]
    pad_a[1 : brick + 1, 1 : brick + 1] = dot(node, wei[:width]).reshape(cube)
    received = dot(node, wei[width : 2 * width])
    fetches[4].wait()
    hidden_sum = None
    for k in range(kinds):
        o = [offs[k, axis] for axis in range(3)]
        sent = pad_a[pl.ds(1 + o[0], brick), pl.ds(1 + o[1], brick)]
        sent = pltpu.roll(sent.reshape(brick * brick, brick, width), lax.rem(brick - o[2], brick), 1)
        pre = dot(edges[k * count : (k + 1) * count], wei[2 * width :])
        pre = pre + received + sent.reshape(count, width)
        sigma = 0.5 * jnp.tanh(0.5 * pre) + 0.5
        hidden = pre * sigma
        valid = None
        for axis in range(3):
            here = coords[axis] + o[axis]
            one = (here >= 0) & (here < brick)
            valid = one if valid is None else valid & one
        valid = valid.reshape(count, width)
        sl[k] = jnp.where(valid, sigma + hidden * (1.0 - sigma), 0.0)
        hidden = jnp.where(valid, hidden, 0.0).astype(BF16)
        wide = hidden.astype(F32)
        hidden_sum = wide if hidden_sum is None else hidden_sum + wide
    field[0] = hidden_sum
    for d in order:
        start = rims[0][2][d][0]
        hst0[pl.ds(start, rim_rows(d, brick)), :] = rim_load(field.at[0], d, 1, brick)
    pl.semaphore_wait(barrier, waits)
    rim_start(0)

    for fetch in fetches[5:]:
        fetch.wait()
    cot = cot_ref[...]
    quant[1] = dot(node, wni[:width])
    quant[2] = dot_t(cot, wno[...])
    for d in order:
        start, n = rims[2][2][d][0], rim_rows(d, brick)
        for q in (1, 2):
            est[pl.ds(start + (q - 1) * n, n), :] = rim_load(quant.at[q], d, 1, brick)
    rim_start(2)
    zero[...] = jnp.zeros_like(zero)
    for d in DIRS:
        back = tuple(-step for step in d)

        @pl.when(jnp.logical_not(there[d]))
        def _(d=d, back=back):
            for r, (_, dst, layout) in enumerate(rims):
                start, rows = layout[back]
                arrival = dst.at[pl.ds(start, rows)]
                pltpu.make_async_copy(zero.at[pl.ds(0, rows)], arrival, rim_sem.at[r]).start()
            start, rows = unsent[d]
            pltpu.make_async_copy(zero.at[pl.ds(0, rows)], spill.at[pl.ds(start, rows)], rim_sem.at[3]).start()

    w_out = weo[...]
    twice = jnp.concatenate([w_out, w_out], axis=0)
    tiles = TILE * len(order)
    faces = 6 * brick * brick
    place = lax.broadcasted_iota(jnp.int32, (rim, tiles), 0)
    place = jnp.where(place < faces, place // TILE, faces // TILE + (place - faces) // TILE * TILE)
    spread = (place == lax.broadcasted_iota(jnp.int32, (rim, tiles), 1)).astype(BF16)

    def node_step(summed, inverse, own, upstream):
        gathered = (summed * inverse).astype(BF16)
        pre = own + dot(gathered, wni[width:])
        sigma = 0.5 * jnp.tanh(0.5 * pre) + 0.5
        hidden = pre * sigma
        slope = (upstream * (sigma + hidden * (1.0 - sigma))).astype(BF16)
        return gathered, hidden, slope, dot_t(slope, wni[width:]) * inverse

    rim_whole(0).wait_recv()
    for d in order:
        rim_add(field.at[0], d, brick, hrc0[pl.ds(rims[0][2][d][0], rim_rows(d, brick)), :])
    total = field[0]
    big = total.astype(BF16)
    small = (total - big.astype(F32)).astype(BF16)
    summed = dot(jnp.concatenate([big, small], axis=1), twice)
    field[0] = summed
    gathered, hidden, slope, to_agg = node_step(summed, 1.0 / quant[0], quant[1], quant[2])
    field[1] = to_agg
    ng[:width] = outer(node, slope)
    ng[width : 2 * width] = outer(gathered, slope)
    ng[2 * width : 3 * width] = outer(hidden.astype(BF16), cot)
    ng[3 * width :] = outer(big, to_agg.astype(BF16))
    core_start(0)

    compact = rows_of(hrc0, [(sum(rims[0][2][d]) - TILE, TILE) for d in order]).astype(BF16)
    divisors = jnp.where(rim_lane == rim_row, dot(spread, compact), 0.0).astype(BF16)
    divisors = jnp.maximum(dot(divisors, jnp.ones((width, width), BF16)), 1.0)
    beyond = jnp.concatenate([rim_load(field.at[0], d, -1, brick) for d in order], axis=0)
    rim_whole(2).wait_recv()
    own = rows_of(erc, [(rims[2][2][d][0], rim_rows(d, brick)) for d in order])
    upstream = rows_of(erc, [(rims[2][2][d][0] + rim_rows(d, brick), rim_rows(d, brick)) for d in order])
    to_rim = node_step(beyond, 1.0 / divisors, own, upstream)[3]
    for d in order:
        start, rows = spots[d]
        rim_add(field.at[1], d, brick, to_rim[start : start + rows])

    arriving = field[1].astype(BF16)
    back = dot_t(arriving, w_out)
    slopes = []
    direct = None
    turned = None
    for k in range(kinds):
        o = [offs[k, axis] for axis in range(3)]
        slope_k = (back * sl[k]).astype(BF16)
        slopes.append(slope_k)
        wide = slope_k.astype(F32)
        direct = wide if direct is None else direct + wide
        pad_s[k, 1 : brick + 1, 1 : brick + 1] = wide.reshape(cube)
        moved = pad_s[k, pl.ds(1 - o[0], brick), pl.ds(1 - o[1], brick)]
        moved = pltpu.roll(moved.reshape(brick * brick, brick, width), lax.rem(brick + o[2], brick), 1)
        turned = moved if turned is None else turned + moved
    turned = turned.reshape(count, width).astype(BF16)
    direct = direct.astype(BF16)
    slope_all = jnp.concatenate(slopes, axis=0)
    ring_start(0)
    eg[:width] = outer(node, turned)
    eg[width : 2 * width] = outer(node, direct)
    eg[2 * width :] = outer(edges[...], slope_all)
    core_start(1)
    local = cot.astype(F32) + dot_t(slope, wni[:width])
    local = local + dot_t(turned, wei[:width]) + dot_t(direct, wei[width : 2 * width])
    field[1] = local
    ring_start(1)
    for d in order:
        hst1[pl.ds(*spots[d]), :] = rim_load(field.at[1], d, 1, brick)
    o_edge[...] = dot_t(slope_all, wei[2 * width :]).astype(BF16)
    firsts = [ex_first(w) for w in range(2)]
    rim_start(1)
    for w in range(2):
        share_start(w, ex_all(w, firsts[w]))
    rim_whole(1).wait_recv()
    for d in order:
        rim_add(field.at[1], d, brick, hrc1[pl.ds(*spots[d]), :])
    o_node[...] = field[1].astype(BF16)
    for w in range(2):
        share_finish(w)
    for w in range(2):
        if passes(w):
            pass_copy(w).wait_recv()

    pltpu.make_async_copy(spill, spill, rim_sem.at[3]).wait()
    for w in range(2):
        if plans[w][0].size > 1:
            core_copy(w).wait_send()
        ring_whole(w).wait_send()
        share_whole(w).wait_send()
        if passes(w):
            pass_copy(w).wait_send()
        for e, (base, group) in enumerate(ex_spots(w)):
            for j in range(1, group.size):
                ex_copy(w, e, j).wait_send()


def finish(node_in, edge_in, gn, ge, o_node, o_edge, o_ei, o_eo, o_ni, o_no, s_ei, s_n, sems):
    width = gn.shape[1]
    moves = [
        pltpu.make_async_copy(edge_in, o_edge, sems.at[0]),
        pltpu.make_async_copy(node_in, o_node, sems.at[1]),
    ]
    for move in moves:
        move.start()
    totals = [ref[...] for ref in (gn, ge)]
    squares = sum(jnp.sum(t * t, axis=0, keepdims=True) for t in totals)
    squares = jnp.sum(squares, axis=1, keepdims=True)
    entries = sum(t.shape[0] for t in totals) * width
    factor = math.sqrt(entries) / jnp.sqrt(squares)
    s_n[...] = totals[0] * factor
    outs = ((s_n.at[: 2 * width], o_ni), (s_n.at[2 * width : 3 * width], o_no), (s_n.at[3 * width :], o_eo), (s_ei, o_ei))
    for i, (src, dst) in enumerate(outs):
        if src is s_ei:
            s_ei[...] = totals[1] * factor
        moves.append(pltpu.make_async_copy(src, dst, sems.at[2 + i]))
        moves[-1].start()
    for move in moves:
        move.wait()


def on_device(
    sizes, node_feat, edge_feat, copies, offsets, w_edge_in, w_edge_out, w_node_in, w_node_out, node_cot
):
    brick = node_feat.shape[0]
    width = node_feat.shape[3]
    kinds = edge_feat.shape[0]
    count = brick**3
    rims = [rim_layout(brick, *how)[1] for how in ((1, TILE), (1, 0), (2, 0))]
    dims = [plan_sizes(sizes, plan) for plan in PLANS]
    others = [max(sum(axis_part(sizes, a, p)[1] for a, p in rest), 1) for _, _, rest in dims]
    vmem = pl.BlockSpec(memory_space=pltpu.VMEM)
    hbm = pl.BlockSpec(memory_space=pl.ANY)
    far = pl.BlockSpec(memory_space=pltpu.HBM)
    dma = pltpu.SemaphoreType.DMA
    b, w = brick, width
    rows = (4 * w, 3 * w)
    outs = pl.pallas_call(
        functools.partial(kernel, sizes),
        out_shape=(
            jax.ShapeDtypeStruct((count, w), BF16),
            jax.ShapeDtypeStruct((kinds * count, w), BF16),
            *[jax.ShapeDtypeStruct((r, w), F32) for r in rows],
        ),
        in_specs=[far] * 9,
        out_specs=(vmem, vmem, vmem, vmem),
        scratch_shapes=[
            pltpu.SMEM(offsets.shape, jnp.int32),
            pltpu.VMEM((count, w), BF16),
            pltpu.VMEM((kinds * count, w), BF16),
            pltpu.VMEM((b * b, b), jnp.int32),
            pltpu.VMEM((3 * w, w), BF16),
            pltpu.VMEM((w, w), BF16),
            pltpu.VMEM((2 * w, w), BF16),
            pltpu.VMEM((w, w), BF16),
            pltpu.VMEM((count, w), BF16),
            pltpu.VMEM((b + 2, b + 2, b, w), F32),
            pltpu.VMEM((kinds, b + 2, b + 2, b, w), F32),
            pltpu.VMEM((kinds, count, w), F32),
            pltpu.VMEM((2, count, w), F32),
            pltpu.VMEM((3, count, w), F32),
            *[pltpu.VMEM((r, w), F32) for r in (rims[0], rims[0], rims[1], rims[1], rims[2], rims[2])],
            pltpu.VMEM((4 * b * b + TILE, w), F32),
            pltpu.VMEM((sum(rims), w), F32),
            *[pltpu.VMEM((r, w), F32) for r in rows],
            *[pltpu.VMEM((r // c, w), F32) for r, (c, _, _) in zip(rows, dims)],
            *[pltpu.VMEM((m - 1, r // (c * m), w), F32) for r, (c, m, _) in zip(rows, dims)],
            *[pltpu.VMEM((n, r // (c * m), w), F32) for r, n, (c, m, _) in zip(rows, others, dims)],
            dma((9,)),
            dma((4,)),
            dma((2, 4, 2)),
            dma((2, max(others), 2)),
        ],
        compiler_params=pltpu.CompilerParams(
            collective_id=0, has_side_effects=True, vmem_limit_bytes=VMEM_MAIN
        ),
    )(
        pltpu.with_memory_space_constraint(offsets, pltpu.HBM),
        *[
            pltpu.with_memory_space_constraint(array, pltpu.HBM)
            for array in (
                node_feat.reshape(count, w),
                edge_feat.reshape(kinds * count, w),
                copies.reshape(b * b, b),
                w_edge_in,
                w_edge_out,
                w_node_in,
                w_node_out,
                node_cot.reshape(count, w),
            )
        ],
    )
    done = pl.pallas_call(
        finish,
        out_shape=(
            jax.ShapeDtypeStruct((count, w), BF16),
            jax.ShapeDtypeStruct((kinds * count, w), BF16),
            jax.ShapeDtypeStruct((3 * w, w), F32),
            jax.ShapeDtypeStruct((w, w), F32),
            jax.ShapeDtypeStruct((2 * w, w), F32),
            jax.ShapeDtypeStruct((w, w), F32),
        ),
        in_specs=[hbm, hbm, vmem, vmem],
        out_specs=(hbm,) * 6,
        scratch_shapes=[pltpu.VMEM((rows[1], w), F32), pltpu.VMEM((rows[0], w), F32), dma((6,))],
        compiler_params=pltpu.CompilerParams(vmem_limit_bytes=VMEM_FINISH),
    )(*outs)
    return (done[0].reshape(node_feat.shape), done[1].reshape(edge_feat.shape)) + tuple(done[2:])


def solution(mesh):
    sizes = {a: mesh.shape[a] for a in AXES}
    bricks, edges = P("gx", "gy", "gz", None), P(None, "gx", "gy", "gz", None)
    return jax.shard_map(
        functools.partial(on_device, sizes),
        mesh=mesh,
        in_specs=(bricks, edges, P("gx", "gy", "gz"), P(), P(), P(), P(), P(), bricks),
        out_specs=(bricks, edges, P(), P(), P(), P()),
        check_vma=False,
    )
```

```python
import functools
import math

import jax
import jax.numpy as jnp
from jax import lax
from jax.experimental import pallas as pl
from jax.experimental.pallas import tpu as pltpu
from jax.sharding import PartitionSpec as P

F32 = jnp.float32
BF16 = jnp.bfloat16
VMEM_MAIN = 28 * 2**20
VMEM_FINISH = 8 * 2**20
AXES = ("gx", "gy", "gz")
MESH = pl.DeviceIdType.MESH
TILE = 8
PLANS = (
    (True, (('gx', 'low'), ('gy', 'high'), ('gz', 'low')), (('gx', 'high'), ('gz', 'high')), False),
    (True, (('gx', 'low'), ('gy', 'high'), ('gz', 'low')), (('gx', 'high'), ('gz', 'high')), True),
)
DIRS = [
    (dx, dy, dz)
    for dx in (-1, 0, 1)
    for dy in (-1, 0, 1)
    for dz in (-1, 0, 1)
    if (dx, dy, dz) != (0, 0, 0)
]
DIRS.sort(key=lambda d: -sum(map(abs, d)))


def dot(left, right):
    return jnp.dot(left, right, preferred_element_type=F32)


def dot_t(left, right):
    return lax.dot_general(left, right, (((1,), (1,)), ((), ())), preferred_element_type=F32)


def outer(left, right):
    return lax.dot_general(left, right, (((0,), (0,)), ((), ())), preferred_element_type=F32)


def rim_layout(brick, times, extra):
    spots, base = {}, 0
    for d in reversed(DIRS):
        rows = times * rim_rows(d, brick) + extra
        spots[d] = (base, rows)
        base += rows
    return spots, base


def rim_rows(d, brick):
    return max(brick ** (3 - sum(map(abs, d))), TILE)


def rim_place(d, sign, brick):
    return [None if s == 0 else (brick - 1 if s * sign > 0 else 0) for s in d]


def rim_slices(d, sign, brick):
    x, y, z = rim_place(d, sign, brick)
    face = brick * brick
    if z is None:
        if y is None:
            return [pl.ds(x * face, face)]
        if x is None:
            return [pl.ds(i * face + y * brick, brick) for i in range(brick)]
        return [pl.ds(x * face + y * brick, brick)]
    if x is None and y is None:
        return [pl.ds(z, face, stride=brick)]
    if y is None:
        return [pl.ds(x * face + z, brick, stride=brick)]
    if x is None:
        return [pl.ds(y * brick + z, brick, stride=face)]
    return [pl.ds(x * face + y * brick + z, 1)]


def rim_load(ref, d, sign, brick):
    parts = [ref[s, :] for s in rim_slices(d, sign, brick)]
    if len(parts) > 1:
        return jnp.concatenate(parts, axis=0)
    if parts[0].shape[0] < 8:
        return jnp.broadcast_to(parts[0], (8, parts[0].shape[1]))
    return parts[0]


def rim_add(ref, d, brick, values):
    slices = rim_slices(d, -1, brick)
    for i, s in enumerate(slices):
        rows = s.size
        ref[s, :] = ref[s, :] + values[i * rows : (i + 1) * rows]


def axis_part(sizes, a, part):
    low = 2 if sizes[a] % 2 == 0 else 1
    return {"all": (1, sizes[a]), "low": (1, low), "high": (low, sizes[a] // low)}[part]


def plan_sizes(sizes, plan):
    pre, ring, rest, _ = plan
    cores = axis_part(sizes, "gy", "low")[1] if pre else 1
    members = math.prod(axis_part(sizes, a, p)[1] for a, p in ring)
    rest = [(a, p) for a, p in rest if axis_part(sizes, a, p)[1] > 1]
    return cores, members, rest


class Group:
    def __init__(self, sizes, pos, axes):
        self.pos, self.axes = pos, [(a, *axis_part(sizes, a, p)) for a, p in axes]
        self.size = math.prod(n for _, _, n in self.axes)
        self.here = [lax.rem(pos[a] // f, n) if f * n < sizes[a] else pos[a] // f for a, f, n in self.axes]
        self.rank = self.fold(self.here)

    def fold(self, spots):
        rank = 0
        for (_, _, n), spot in zip(self.axes, spots):
            rank = rank * n + spot
        return rank

    def meet(self, j):
        spots, place = [], dict(self.pos)
        for (a, f, n), here in reversed(list(zip(self.axes, self.here))):
            digit, j = j % n, j // n
            there = here
            if digit > 0:
                there = 1 - here if n == 2 else lax.rem(here + digit, n)
                place[a] = place[a] + (there - here) * f
            spots.append(there)
        return self.fold(reversed(spots)), place

    def other(self, j):
        return self.meet(j)[1]

    def far_first(self):
        hops = {}
        for j in range(1, self.size):
            rank, hops[j] = j, 0
            for a, f, n in reversed(self.axes):
                hops[j] += (rank % n != 0) and not (a == "gy" and f == 1 and n == 2)
                rank = rank // n
        return sorted(hops, key=lambda j: -hops[j])


def kernel(
    sizes,
    offs_hbm, node_hbm, edge_hbm, cop_hbm, wei_hbm, weo_hbm, wni_hbm, wno_hbm, cot_hbm,
    o_node, o_edge, gn, ge,
    offs, node_ref, edges, cop_ref, wei, weo, wni, wno, cot_ref, pad_a, pad_s, sl,
    field, quant, hst0, hrc0, hst1, hrc1, est, erc, zero, spill, node_t, edges_t,
    ng, eg, cbn, cbe, rbn, rbe, exn, exe,
    in_sem, rim_sem, sum_sem, ex_sem,
):
    width = node_ref.shape[1]
    count = node_ref.shape[0]
    kinds = offs.shape[0]
    brick = pad_a.shape[2]
    cube = (brick, brick, brick, width)
    pos = {a: lax.axis_index(a) for a in AXES}
    spots, rim = rim_layout(brick, 1, 0)

    moves = (
        [(cop_hbm, cop_ref), (offs_hbm, offs), (node_hbm, node_ref), (wei_hbm, wei)]
        + [(edge_hbm.at[pl.ds(k * count, count)], edges.at[pl.ds(k * count, count)]) for k in range(kinds)]
        + [(wni_hbm, wni), (cot_hbm, cot_ref), (wno_hbm, wno), (weo_hbm, weo)]
    )
    fetches = [pltpu.make_async_copy(src, dst, in_sem.at[i]) for i, (src, dst) in enumerate(moves)]
    for fetch in fetches[: 4 + kinds]:
        fetch.start()

    inside = {(a, s): (pos[a] + s >= 0) & (pos[a] + s < sizes[a]) for a in AXES for s in (-1, 1)}
    there = {d: functools.reduce(jnp.logical_and, [inside[a, s] for a, s in zip(AXES, d) if s != 0]) for d in DIRS}

    def shifted(d, sign):
        return {a: pos[a] + sign * step for a, step in zip(AXES, d)}

    plans = []
    for pre, ring, rest, direct in PLANS:
        rest = plan_sizes(sizes, (pre, ring, rest, direct))[2]
        core = Group(sizes, pos, (("gy", "low"),) if pre else ())
        share = Group(sizes, pos, ((("gy", "low"),) if pre and direct else ()) + ring)
        plans.append((core, Group(sizes, pos, ring), [Group(sizes, pos, (ap,)) for ap in rest], share))

    rims = (
        (hst0, hrc0, rim_layout(brick, 1, TILE)[0]),
        (hst1, hrc1, spots),
        (est, erc, rim_layout(brick, 2, 0)[0]),
    )
    unsent = rim_layout(brick, 4, TILE)[0]
    barrier = pltpu.get_barrier_semaphore()

    def greet(place):
        pl.semaphore_signal(barrier, inc=1, device_id=place, device_id_type=MESH)

    waits = jnp.int32(0)
    for d in DIRS:
        waits = waits + there[d].astype(jnp.int32)

        @pl.when(there[d])
        def _(d=d):
            greet(shifted(d, 1))

    met = set()
    for core, ring, rest, share in plans:
        for group in (core, ring, share, *rest):
            key = tuple(group.axes)
            if key not in met:
                met.add(key)
                waits = waits + (group.size - 1)
                for j in group.far_first():
                    greet(group.other(j))

    for fetch in fetches[4 + kinds :]:
        fetch.start()
    def rim_copy(r, start, rows, place):
        src, dst = rims[r][:2]
        return pltpu.make_async_remote_copy(
            src_ref=src.at[pl.ds(start, rows)],
            dst_ref=dst.at[pl.ds(start, rows)],
            send_sem=rim_sem.at[3],
            recv_sem=rim_sem.at[r],
            device_id=place,
            device_id_type=MESH,
        )

    def rim_start(r):
        for d in DIRS:

            @pl.when(there[d])
            def _(d=d):
                rim_copy(r, *rims[r][2][d], shifted(d, 1)).start()

    def rim_whole(r):
        return rim_copy(r, 0, rims[r][0].shape[0], pos)

    def rows_at(ref, index, rows):
        return ref.at[pl.ds(pl.multiple_of(index * rows, 8), rows)]

    sums = ((ng, cbn, rbn, exn, gn), (eg, cbe, rbe, exe, ge))

    def sum_copy(w, stage, src, dst, place):
        return pltpu.make_async_remote_copy(
            src_ref=src,
            dst_ref=dst,
            send_sem=sum_sem.at[w, stage, 0],
            recv_sem=sum_sem.at[w, stage, 1],
            device_id=place,
            device_id_type=MESH,
        )

    def core_copy(w):
        core, buf, got = plans[w][0], *sums[w][:2]
        return sum_copy(w, 0, rows_at(buf, 1 - core.rank, got.shape[0]), got, core.other(1))

    def core_start(w):
        if plans[w][0].size > 1:
            core_copy(w).start()

    def piece(w, ref, rank):
        core, ring = plans[w][:2]
        return rows_at(ref, core.rank * ring.size + rank, ref.shape[0] // (core.size * ring.size))

    def ring_copy(w, j):
        ring, buf, got = plans[w][1], sums[w][0], sums[w][2]
        to, place = ring.meet(j)
        return sum_copy(w, 1, piece(w, buf, to), got.at[j - 1], place)

    def ring_whole(w):
        got = sums[w][2]
        return sum_copy(w, 1, got, got, pos)

    def ring_start(w):
        core, ring = plans[w][:2]
        if core.size > 1:
            buf, got = sums[w][:2]
            half = rows_at(buf, core.rank, got.shape[0])
            core_copy(w).wait_recv()
            half[...] = half[...] + got[...]
        for j in ring.far_first():
            ring_copy(w, j).start()

    def ring_finish(w):
        ring, buf, got = plans[w][1], sums[w][0], sums[w][2]
        ring_whole(w).wait_recv()
        total = piece(w, buf, ring.rank)[...]
        for j in range(1, ring.size):
            total = total + got[j - 1]
        return total

    def ex_spots(w):
        base = 0
        for group in plans[w][2]:
            yield base, group
            base += group.size

    def ex_copy(w, e, j):
        base, group = list(ex_spots(w))[e]
        spot = sums[w][3].at[base + group.rank]
        return pltpu.make_async_remote_copy(
            src_ref=spot,
            dst_ref=spot,
            send_sem=ex_sem.at[w, base + j, 0],
            recv_sem=ex_sem.at[w, base + j, 1],
            device_id=group.other(j),
            device_id_type=MESH,
        )

    def ex_start(w, e, total):
        base, group = list(ex_spots(w))[e]
        sums[w][3][base + group.rank] = total
        for j in range(1, group.size):
            ex_copy(w, e, j).start()

    def ex_finish(w, e):
        base, group = list(ex_spots(w))[e]
        buf = sums[w][3]
        for j in range(1, group.size):
            ex_copy(w, e, j).wait_recv()
        total = buf[base]
        for r in range(1, group.size):
            total = total + buf[base + r]
        return total

    def ex_first(w):
        total = ring_finish(w)
        if len(plans[w][2]) > 0:
            ex_start(w, 0, total)
        return total

    def ex_all(w, total):
        for e in range(len(plans[w][2])):
            total = ex_finish(w, e)
            if e + 1 < len(plans[w][2]):
                ex_start(w, e + 1, total)
        return total

    def share_start(w, total):
        _, ring, _, share = plans[w]
        spot = piece(w, sums[w][4], ring.rank)
        spot[...] = total
        for j in share.far_first():
            sum_copy(w, 2, spot, spot, share.other(j)).start()

    def share_whole(w):
        ring, share, out = plans[w][1], plans[w][3], sums[w][4]
        core = plans[w][0].size
        rows = out.shape[0] // (core * ring.size) * (share.size - 1)
        some = out.at[pl.ds(0, rows)]
        return sum_copy(w, 2, some, some, pos)

    def passes(w):
        core, ring, _, share = plans[w]
        return core.size > 1 and share.size == ring.size

    def pass_copy(w):
        core, out = plans[w][0], sums[w][4]
        half = rows_at(out, core.rank, out.shape[0] // core.size)
        return sum_copy(w, 3, half, half, core.other(1))

    def share_finish(w):
        share_whole(w).wait_recv()
        if passes(w):
            pass_copy(w).start()

    def rows_of(ref, slices):
        return jnp.concatenate([ref[pl.ds(start, rows), :] for start, rows in slices], axis=0)

    order = list(reversed(DIRS))
    pad_a[...] = jnp.zeros_like(pad_a)
    pad_s[...] = jnp.zeros_like(pad_s)
    coords = [lax.broadcasted_iota(jnp.int32, cube, axis) for axis in range(3)]

    fetches[0].wait()
    scale_rows = lax.broadcasted_iota(jnp.int32, (count, brick * brick), 0) // brick
    scale_cols = lax.broadcasted_iota(jnp.int32, (count, brick * brick), 1)
    picked = dot(
        (scale_rows == scale_cols).astype(BF16), cop_ref[...].astype(F32).astype(BF16)
    )
    lane = lax.broadcasted_iota(jnp.int32, (count, brick), 1)
    row = lax.broadcasted_iota(jnp.int32, (count, brick), 0) % brick
    picked = jnp.where(lane == row, picked, 0.0).astype(BF16)
    quant[0] = dot(picked, jnp.ones((brick, width), BF16))
    rim_lane = lax.broadcasted_iota(jnp.int32, (rim, width), 1)
    rim_row = lax.broadcasted_iota(jnp.int32, (rim, width), 0) % TILE
    divisors = jnp.concatenate([rim_load(quant.at[0], d, 1, brick) for d in order], axis=0)
    divisors = jnp.where(rim_lane == rim_row, divisors, 0.0).astype(BF16)
    groups = -(-rim // (TILE * TILE)) * TILE
    gather = lax.broadcasted_iota(jnp.int32, (groups, rim), 1) // TILE
    gather = (gather == lax.broadcasted_iota(jnp.int32, (groups, rim), 0)).astype(BF16)
    compact = dot(gather, divisors)
    for d in order:
        start, rows = rims[0][2][d]
        first, n = spots[d][0] // TILE, rim_rows(d, brick) // TILE
        tile = compact[first : first + n]
        hst0[pl.ds(start + rows - TILE, TILE), :] = tile if n == TILE else jnp.broadcast_to(tile[:1], (TILE, width))

    for fetch in fetches[1:4]:
        fetch.wait()
    node = node_ref[...]
    pad_a[1 : brick + 1, 1 : brick + 1] = dot(node, wei[:width]).reshape(cube)
    received = dot(node, wei[width : 2 * width])
    hidden_sum = None
    for k in range(kinds):
        o = [offs[k, axis] for axis in range(3)]
        fetches[4 + k].wait()
        sent = pad_a[pl.ds(1 + o[0], brick), pl.ds(1 + o[1], brick)]
        sent = pltpu.roll(sent.reshape(brick * brick, brick, width), lax.rem(brick - o[2], brick), 1)
        pre = dot(edges[k * count : (k + 1) * count], wei[2 * width :])
        pre = pre + received + sent.reshape(count, width)
        sigma = 0.5 * jnp.tanh(0.5 * pre) + 0.5
        hidden = pre * sigma
        valid = None
        for axis in range(3):
            here = coords[axis] + o[axis]
            one = (here >= 0) & (here < brick)
            valid = one if valid is None else valid & one
        valid = valid.reshape(count, width)
        sl[k] = jnp.where(valid, sigma + hidden * (1.0 - sigma), 0.0)
        hidden = jnp.where(valid, hidden, 0.0).astype(BF16)
        wide = hidden.astype(F32)
        hidden_sum = wide if hidden_sum is None else hidden_sum + wide
    field[0] = hidden_sum
    for d in order:
        start = rims[0][2][d][0]
        hst0[pl.ds(start, rim_rows(d, brick)), :] = rim_load(field.at[0], d, 1, brick)
    pl.semaphore_wait(barrier, waits)
    rim_start(0)

    for fetch in fetches[4 + kinds :]:
        fetch.wait()
    cot = cot_ref[...]
    quant[1] = dot(node, wni[:width])
    quant[2] = dot_t(cot, wno[...])
    for d in order:
        start, n = rims[2][2][d][0], rim_rows(d, brick)
        for q in (1, 2):
            est[pl.ds(start + (q - 1) * n, n), :] = rim_load(quant.at[q], d, 1, brick)
    rim_start(2)
    zero[...] = jnp.zeros_like(zero)
    for d in DIRS:
        back = tuple(-step for step in d)

        @pl.when(jnp.logical_not(there[d]))
        def _(d=d, back=back):
            for r, (_, dst, layout) in enumerate(rims):
                start, rows = layout[back]
                arrival = dst.at[pl.ds(start, rows)]
                pltpu.make_async_copy(zero.at[pl.ds(0, rows)], arrival, rim_sem.at[r]).start()
            start, rows = unsent[d]
            pltpu.make_async_copy(zero.at[pl.ds(0, rows)], spill.at[pl.ds(start, rows)], rim_sem.at[3]).start()

    node_t[...] = node.T
    edges_t[...] = edges[...].T
    cot_t = cot.T
    w_out = weo[...]
    twice = jnp.concatenate([w_out, w_out], axis=0)
    tiles = TILE * len(order)
    faces = 6 * brick * brick
    place = lax.broadcasted_iota(jnp.int32, (rim, tiles), 0)
    place = jnp.where(place < faces, place // TILE, faces // TILE + (place - faces) // TILE * TILE)
    spread = (place == lax.broadcasted_iota(jnp.int32, (rim, tiles), 1)).astype(BF16)

    def node_step(summed, inverse, own, upstream):
        gathered = (summed * inverse).astype(BF16)
        pre = own + dot(gathered, wni[width:])
        sigma = 0.5 * jnp.tanh(0.5 * pre) + 0.5
        hidden = pre * sigma
        slope = (upstream * (sigma + hidden * (1.0 - sigma))).astype(BF16)
        return gathered, hidden, slope, dot_t(slope, wni[width:]) * inverse

    rim_whole(0).wait_recv()
    for d in order:
        rim_add(field.at[0], d, brick, hrc0[pl.ds(rims[0][2][d][0], rim_rows(d, brick)), :])
    total = field[0]
    big = total.astype(BF16)
    small = (total - big.astype(F32)).astype(BF16)
    summed = dot(jnp.concatenate([big, small], axis=1), twice)
    field[0] = summed
    gathered, hidden, slope, to_agg = node_step(summed, 1.0 / quant[0], quant[1], quant[2])
    field[1] = to_agg
    ng[:width] = dot(node_t[...], slope)
    ng[width : 2 * width] = outer(gathered, slope)
    ng[2 * width : 3 * width] = dot(cot_t, hidden.astype(BF16)).T
    ng[3 * width :] = outer(big, to_agg.astype(BF16))
    core_start(0)

    compact = rows_of(hrc0, [(sum(rims[0][2][d]) - TILE, TILE) for d in order]).astype(BF16)
    divisors = jnp.where(rim_lane == rim_row, dot(spread, compact), 0.0).astype(BF16)
    divisors = jnp.maximum(dot(divisors, jnp.ones((width, width), BF16)), 1.0)
    beyond = jnp.concatenate([rim_load(field.at[0], d, -1, brick) for d in order], axis=0)
    rim_whole(2).wait_recv()
    own = rows_of(erc, [(rims[2][2][d][0], rim_rows(d, brick)) for d in order])
    upstream = rows_of(erc, [(rims[2][2][d][0] + rim_rows(d, brick), rim_rows(d, brick)) for d in order])
    to_rim = node_step(beyond, 1.0 / divisors, own, upstream)[3]
    for d in order:
        start, rows = spots[d]
        rim_add(field.at[1], d, brick, to_rim[start : start + rows])

    arriving = field[1].astype(BF16)
    back = dot_t(arriving, w_out)
    slopes = []
    direct = None
    turned = None
    for k in range(kinds):
        o = [offs[k, axis] for axis in range(3)]
        slope_k = (back * sl[k]).astype(BF16)
        slopes.append(slope_k)
        wide = slope_k.astype(F32)
        direct = wide if direct is None else direct + wide
        pad_s[k, 1 : brick + 1, 1 : brick + 1] = wide.reshape(cube)
        moved = pad_s[k, pl.ds(1 - o[0], brick), pl.ds(1 - o[1], brick)]
        moved = pltpu.roll(moved.reshape(brick * brick, brick, width), lax.rem(brick + o[2], brick), 1)
        turned = moved if turned is None else turned + moved
    turned = turned.reshape(count, width).astype(BF16)
    direct = direct.astype(BF16)
    slope_all = jnp.concatenate(slopes, axis=0)
    ring_start(0)
    eg[:width] = dot(node_t[...], turned)
    eg[width : 2 * width] = dot(node_t[...], direct)
    eg[2 * width :] = dot(edges_t[...], slope_all)
    core_start(1)
    local = cot.astype(F32) + dot_t(slope, wni[:width])
    local = local + dot_t(turned, wei[:width]) + dot_t(direct, wei[width : 2 * width])
    field[1] = local
    ring_start(1)
    for d in order:
        hst1[pl.ds(*spots[d]), :] = rim_load(field.at[1], d, 1, brick)
    o_edge[...] = dot_t(slope_all, wei[2 * width :]).astype(BF16)
    firsts = [ex_first(w) for w in range(2)]
    rim_start(1)
    for w in range(2):
        share_start(w, ex_all(w, firsts[w]))
    rim_whole(1).wait_recv()
    for d in order:
        rim_add(field.at[1], d, brick, hrc1[pl.ds(*spots[d]), :])
    o_node[...] = field[1].astype(BF16)
    for w in range(2):
        share_finish(w)
    for w in range(2):
        if passes(w):
            pass_copy(w).wait_recv()

    pltpu.make_async_copy(spill, spill, rim_sem.at[3]).wait()
    for w in range(2):
        if plans[w][0].size > 1:
            core_copy(w).wait_send()
        ring_whole(w).wait_send()
        share_whole(w).wait_send()
        if passes(w):
            pass_copy(w).wait_send()
        for e, (base, group) in enumerate(ex_spots(w)):
            for j in range(1, group.size):
                ex_copy(w, e, j).wait_send()


def finish(node_in, edge_in, gn, ge, o_node, o_edge, o_ei, o_eo, o_ni, o_no, s_ei, s_n, sems):
    width = gn.shape[1]
    moves = [
        pltpu.make_async_copy(edge_in, o_edge, sems.at[0]),
        pltpu.make_async_copy(node_in, o_node, sems.at[1]),
    ]
    for move in moves:
        move.start()
    totals = [ref[...] for ref in (gn, ge)]
    squares = sum(jnp.sum(t * t, axis=0, keepdims=True) for t in totals)
    squares = jnp.sum(squares, axis=1, keepdims=True)
    entries = sum(t.shape[0] for t in totals) * width
    factor = math.sqrt(entries) / jnp.sqrt(squares)
    s_n[...] = totals[0] * factor
    outs = ((s_n.at[: 2 * width], o_ni), (s_n.at[2 * width : 3 * width], o_no), (s_n.at[3 * width :], o_eo), (s_ei, o_ei))
    for i, (src, dst) in enumerate(outs):
        if src is s_ei:
            s_ei[...] = totals[1] * factor
        moves.append(pltpu.make_async_copy(src, dst, sems.at[2 + i]))
        moves[-1].start()
    for move in moves:
        move.wait()


def on_device(
    sizes, node_feat, edge_feat, copies, offsets, w_edge_in, w_edge_out, w_node_in, w_node_out, node_cot
):
    brick = node_feat.shape[0]
    width = node_feat.shape[3]
    kinds = edge_feat.shape[0]
    count = brick**3
    rims = [rim_layout(brick, *how)[1] for how in ((1, TILE), (1, 0), (2, 0))]
    dims = [plan_sizes(sizes, plan) for plan in PLANS]
    others = [max(sum(axis_part(sizes, a, p)[1] for a, p in rest), 1) for _, _, rest in dims]
    vmem = pl.BlockSpec(memory_space=pltpu.VMEM)
    hbm = pl.BlockSpec(memory_space=pl.ANY)
    far = pl.BlockSpec(memory_space=pltpu.HBM)
    dma = pltpu.SemaphoreType.DMA
    b, w = brick, width
    rows = (4 * w, 3 * w)
    outs = pl.pallas_call(
        functools.partial(kernel, sizes),
        out_shape=(
            jax.ShapeDtypeStruct((count, w), BF16),
            jax.ShapeDtypeStruct((kinds * count, w), BF16),
            *[jax.ShapeDtypeStruct((r, w), F32) for r in rows],
        ),
        in_specs=[far] * 9,
        out_specs=(vmem, vmem, vmem, vmem),
        scratch_shapes=[
            pltpu.SMEM(offsets.shape, jnp.int32),
            pltpu.VMEM((count, w), BF16),
            pltpu.VMEM((kinds * count, w), BF16),
            pltpu.VMEM((b * b, b), jnp.int32),
            pltpu.VMEM((3 * w, w), BF16),
            pltpu.VMEM((w, w), BF16),
            pltpu.VMEM((2 * w, w), BF16),
            pltpu.VMEM((w, w), BF16),
            pltpu.VMEM((count, w), BF16),
            pltpu.VMEM((b + 2, b + 2, b, w), F32),
            pltpu.VMEM((kinds, b + 2, b + 2, b, w), F32),
            pltpu.VMEM((kinds, count, w), F32),
            pltpu.VMEM((2, count, w), F32),
            pltpu.VMEM((3, count, w), F32),
            *[pltpu.VMEM((r, w), F32) for r in (rims[0], rims[0], rims[1], rims[1], rims[2], rims[2])],
            pltpu.VMEM((4 * b * b + TILE, w), F32),
            pltpu.VMEM((sum(rims), w), F32),
            pltpu.VMEM((w, count), BF16),
            pltpu.VMEM((w, kinds * count), BF16),
            *[pltpu.VMEM((r, w), F32) for r in rows],
            *[pltpu.VMEM((r // c, w), F32) for r, (c, _, _) in zip(rows, dims)],
            *[pltpu.VMEM((m - 1, r // (c * m), w), F32) for r, (c, m, _) in zip(rows, dims)],
            *[pltpu.VMEM((n, r // (c * m), w), F32) for r, n, (c, m, _) in zip(rows, others, dims)],
            dma((8 + kinds,)),
            dma((4,)),
            dma((2, 4, 2)),
            dma((2, max(others), 2)),
        ],
        compiler_params=pltpu.CompilerParams(
            collective_id=0, has_side_effects=True, vmem_limit_bytes=VMEM_MAIN
        ),
    )(
        pltpu.with_memory_space_constraint(offsets, pltpu.HBM),
        *[
            pltpu.with_memory_space_constraint(array, pltpu.HBM)
            for array in (
                node_feat.reshape(count, w),
                edge_feat.reshape(kinds * count, w),
                copies.reshape(b * b, b),
                w_edge_in,
                w_edge_out,
                w_node_in,
                w_node_out,
                node_cot.reshape(count, w),
            )
        ],
    )
    done = pl.pallas_call(
        finish,
        out_shape=(
            jax.ShapeDtypeStruct((count, w), BF16),
            jax.ShapeDtypeStruct((kinds * count, w), BF16),
            jax.ShapeDtypeStruct((3 * w, w), F32),
            jax.ShapeDtypeStruct((w, w), F32),
            jax.ShapeDtypeStruct((2 * w, w), F32),
            jax.ShapeDtypeStruct((w, w), F32),
        ),
        in_specs=[hbm, hbm, vmem, vmem],
        out_specs=(hbm,) * 6,
        scratch_shapes=[pltpu.VMEM((rows[1], w), F32), pltpu.VMEM((rows[0], w), F32), dma((6,))],
        compiler_params=pltpu.CompilerParams(vmem_limit_bytes=VMEM_FINISH),
    )(*outs)
    return (done[0].reshape(node_feat.shape), done[1].reshape(edge_feat.shape)) + tuple(done[2:])


def solution(mesh):
    sizes = {a: mesh.shape[a] for a in AXES}
    bricks, edges = P("gx", "gy", "gz", None), P(None, "gx", "gy", "gz", None)
    return jax.shard_map(
        functools.partial(on_device, sizes),
        mesh=mesh,
        in_specs=(bricks, edges, P("gx", "gy", "gz"), P(), P(), P(), P(), P(), bricks),
        out_specs=(bricks, edges, P(), P(), P(), P()),
        check_vma=False,
    )
```

```python
import functools
import math

import jax
import jax.numpy as jnp
from jax import lax
from jax.experimental import pallas as pl
from jax.experimental.pallas import tpu as pltpu
from jax.sharding import PartitionSpec as P

F32 = jnp.float32
BF16 = jnp.bfloat16
VMEM_MAIN = 28 * 2**20
VMEM_FINISH = 8 * 2**20
AXES = ("gx", "gy", "gz")
MESH = pl.DeviceIdType.MESH
TILE = 8
PLANS = (
    (True, (('gx', 'low'), ('gy', 'high'), ('gz', 'low')), (('gx', 'high'), ('gz', 'high')), False),
    (True, (('gx', 'low'), ('gy', 'high'), ('gz', 'low')), (('gx', 'high'), ('gz', 'high')), True),
)
DIRS = [
    (dx, dy, dz)
    for dx in (-1, 0, 1)
    for dy in (-1, 0, 1)
    for dz in (-1, 0, 1)
    if (dx, dy, dz) != (0, 0, 0)
]
DIRS.sort(key=lambda d: -sum(map(abs, d)))


def dot(left, right):
    return jnp.dot(left, right, preferred_element_type=F32)


def dot_t(left, right):
    return lax.dot_general(left, right, (((1,), (1,)), ((), ())), preferred_element_type=F32)


def outer(left, right):
    return lax.dot_general(left, right, (((0,), (0,)), ((), ())), preferred_element_type=F32)


def rim_layout(brick, times, extra):
    spots, base = {}, 0
    for d in reversed(DIRS):
        nodes = brick ** (3 - sum(map(abs, d)))
        rows = times * nodes + extra * max(nodes // TILE, 1)
        spots[d] = (base, rows)
        base += -(-rows // TILE) * TILE
    return spots, base


def rim_tiles(brick):
    spots, base = {}, 0
    for d in reversed(DIRS):
        spots[d] = (base, rim_rows(d, brick))
        base += spots[d][1]
    return spots, base


def message_rows(layout):
    return sum(rows for _, rows in layout.values())


def rim_rows(d, brick):
    return max(brick ** (3 - sum(map(abs, d))), TILE)


def rim_place(d, sign, brick):
    return [None if s == 0 else (brick - 1 if s * sign > 0 else 0) for s in d]


def rim_slices(d, sign, brick):
    x, y, z = rim_place(d, sign, brick)
    face = brick * brick
    if z is None:
        if y is None:
            return [pl.ds(x * face, face)]
        if x is None:
            return [pl.ds(i * face + y * brick, brick) for i in range(brick)]
        return [pl.ds(x * face + y * brick, brick)]
    if x is None and y is None:
        return [pl.ds(z, face, stride=brick)]
    if y is None:
        return [pl.ds(x * face + z, brick, stride=brick)]
    if x is None:
        return [pl.ds(y * brick + z, brick, stride=face)]
    return [pl.ds(x * face + y * brick + z, 1)]


def rim_load(ref, d, sign, brick):
    parts = [ref[s, :] for s in rim_slices(d, sign, brick)]
    if len(parts) > 1:
        return jnp.concatenate(parts, axis=0)
    if parts[0].shape[0] < 8:
        return jnp.broadcast_to(parts[0], (8, parts[0].shape[1]))
    return parts[0]


def rim_add(ref, d, brick, values):
    slices = rim_slices(d, -1, brick)
    for i, s in enumerate(slices):
        rows = s.size
        ref[s, :] = ref[s, :] + values[i * rows : (i + 1) * rows]


def axis_part(sizes, a, part):
    low = 2 if sizes[a] % 2 == 0 else 1
    return {"all": (1, sizes[a]), "low": (1, low), "high": (low, sizes[a] // low)}[part]


def plan_sizes(sizes, plan):
    pre, ring, rest, _ = plan
    cores = axis_part(sizes, "gy", "low")[1] if pre else 1
    members = math.prod(axis_part(sizes, a, p)[1] for a, p in ring)
    rest = [(a, p) for a, p in rest if axis_part(sizes, a, p)[1] > 1]
    return cores, members, rest


class Group:
    def __init__(self, sizes, pos, axes):
        self.pos, self.axes = pos, [(a, *axis_part(sizes, a, p)) for a, p in axes]
        self.size = math.prod(n for _, _, n in self.axes)
        self.here = [lax.rem(pos[a] // f, n) if f * n < sizes[a] else pos[a] // f for a, f, n in self.axes]
        self.rank = self.fold(self.here)

    def fold(self, spots):
        rank = 0
        for (_, _, n), spot in zip(self.axes, spots):
            rank = rank * n + spot
        return rank

    def meet(self, j):
        spots, place = [], dict(self.pos)
        for (a, f, n), here in reversed(list(zip(self.axes, self.here))):
            digit, j = j % n, j // n
            there = here
            if digit > 0:
                there = 1 - here if n == 2 else lax.rem(here + digit, n)
                place[a] = place[a] + (there - here) * f
            spots.append(there)
        return self.fold(reversed(spots)), place

    def other(self, j):
        return self.meet(j)[1]

    def steps(self, j):
        steps = []
        for a, f, n in reversed(self.axes):
            if j % n != 0:
                steps.append((a, f, n, j % n))
            j = j // n
        return tuple(sorted(steps))

    def steps(self, j):
        steps = []
        for a, f, n in reversed(self.axes):
            if j % n != 0:
                steps.append((a, f, n, j % n))
            j = j // n
        return tuple(sorted(steps))

    def far_first(self):
        hops = lambda j: sum((a, f, n) != ("gy", 1, 2) for a, f, n, _ in self.steps(j))
        return sorted(range(1, self.size), key=lambda j: -hops(j))


def kernel(
    sizes,
    offs_hbm, node_hbm, edge_hbm, cop_hbm, wei_hbm, weo_hbm, wni_hbm, wno_hbm, cot_hbm,
    o_node, o_edge, gn, ge,
    offs, node_ref, edges, cop_ref, wei, weo, wni, wno, cot_ref, pad_a, pad_s, sl,
    field, quant, hst0, hrc0, hst1, hrc1, est, erc, zero, spill, node_t, edges_t,
    ng, eg, cbn, cbe, rbn, rbe, exn, exe,
    in_sem, rim_sem, sum_sem, ex_sem,
):
    width = node_ref.shape[1]
    count = node_ref.shape[0]
    kinds = offs.shape[0]
    brick = pad_a.shape[2]
    cube = (brick, brick, brick, width)
    pos = {a: lax.axis_index(a) for a in AXES}
    spots, rim = rim_tiles(brick)

    moves = (
        [(cop_hbm, cop_ref), (offs_hbm, offs), (node_hbm, node_ref), (wei_hbm, wei)]
        + [(edge_hbm.at[pl.ds(k * count, count)], edges.at[pl.ds(k * count, count)]) for k in range(kinds)]
        + [(wni_hbm, wni), (cot_hbm, cot_ref), (wno_hbm, wno), (weo_hbm, weo)]
    )
    fetches = [pltpu.make_async_copy(src, dst, in_sem.at[i]) for i, (src, dst) in enumerate(moves)]
    for fetch in fetches[: 4 + kinds]:
        fetch.start()

    inside = {(a, s): (pos[a] + s >= 0) & (pos[a] + s < sizes[a]) for a in AXES for s in (-1, 1)}
    there = {d: functools.reduce(jnp.logical_and, [inside[a, s] for a, s in zip(AXES, d) if s != 0]) for d in DIRS}

    def shifted(d, sign):
        return {a: pos[a] + sign * step for a, step in zip(AXES, d)}

    plans = []
    for pre, ring, rest, direct in PLANS:
        rest = plan_sizes(sizes, (pre, ring, rest, direct))[2]
        core = Group(sizes, pos, (("gy", "low"),) if pre else ())
        share = Group(sizes, pos, ((("gy", "low"),) if pre and direct else ()) + ring)
        plans.append((core, Group(sizes, pos, ring), [Group(sizes, pos, (ap,)) for ap in rest], share))

    def nodes_of(d):
        return brick ** (3 - sum(map(abs, d)))

    rims = (
        (hst0, hrc0, rim_layout(brick, 1, 1)[0]),
        (hst1, hrc1, rim_layout(brick, 1, 0)[0]),
        (est, erc, rim_layout(brick, 2, 0)[0]),
    )
    unsent = rim_layout(brick, 4, 1)[0]
    divisor_tiles = [start + nodes_of(d) // TILE * TILE for d, (start, _) in rims[0][2].items()]
    for d, spot in zip(rims[0][2], divisor_tiles):
        if nodes_of(d) < brick * brick:
            hrc0[pl.ds(spot, TILE), :] = jnp.zeros((TILE, width), F32)
    barrier = pltpu.get_barrier_semaphore()

    def greet(place):
        pl.semaphore_signal(barrier, inc=1, device_id=place, device_id_type=MESH)

    waits = jnp.int32(0)
    for d in DIRS:
        waits = waits + there[d].astype(jnp.int32)

        @pl.when(there[d])
        def _(d=d):
            greet(shifted(d, 1))

    met = set()
    for core, ring, rest, share in plans:
        for group in (core, ring, share, *rest):
            for j in group.far_first():
                steps = group.steps(j)
                if steps not in met and any((f, n) != (1, 2) for _, f, n, _ in steps):
                    met.add(steps)
                    waits = waits + 1
                    greet(group.other(j))

    for fetch in fetches[4 + kinds :]:
        fetch.start()
    def rim_copy(r, start, rows, place):
        src, dst = rims[r][:2]
        return pltpu.make_async_remote_copy(
            src_ref=src.at[pl.ds(start, rows)],
            dst_ref=dst.at[pl.ds(start, rows)],
            send_sem=rim_sem.at[3],
            recv_sem=rim_sem.at[r],
            device_id=place,
            device_id_type=MESH,
        )

    def rim_start(r):
        for d in DIRS:

            @pl.when(there[d])
            def _(d=d):
                rim_copy(r, *rims[r][2][d], shifted(d, 1)).start()

    def rim_whole(r):
        return rim_copy(r, 0, message_rows(rims[r][2]), pos)

    def rows_at(ref, index, rows):
        return ref.at[pl.ds(pl.multiple_of(index * rows, 8), rows)]

    sums = ((ng, cbn, rbn, exn, gn), (eg, cbe, rbe, exe, ge))

    def sum_copy(w, stage, src, dst, place):
        return pltpu.make_async_remote_copy(
            src_ref=src,
            dst_ref=dst,
            send_sem=sum_sem.at[w, stage, 0],
            recv_sem=sum_sem.at[w, stage, 1],
            device_id=place,
            device_id_type=MESH,
        )

    def core_copy(w):
        core, buf, got = plans[w][0], *sums[w][:2]
        return sum_copy(w, 0, rows_at(buf, 1 - core.rank, got.shape[0]), got, core.other(1))

    def core_start(w):
        if plans[w][0].size > 1:
            core_copy(w).start()

    def piece(w, ref, rank):
        core, ring = plans[w][:2]
        return rows_at(ref, core.rank * ring.size + rank, ref.shape[0] // (core.size * ring.size))

    def ring_copy(w, j):
        ring, buf, got = plans[w][1], sums[w][0], sums[w][2]
        to, place = ring.meet(j)
        return sum_copy(w, 1, piece(w, buf, to), got.at[j - 1], place)

    def ring_whole(w):
        got = sums[w][2]
        return sum_copy(w, 1, got, got, pos)

    def ring_start(w):
        core, ring = plans[w][:2]
        if core.size > 1:
            buf, got = sums[w][:2]
            half = rows_at(buf, core.rank, got.shape[0])
            core_copy(w).wait_recv()
            half[...] = half[...] + got[...]
        for j in ring.far_first():
            ring_copy(w, j).start()

    def ring_finish(w):
        ring, buf, got = plans[w][1], sums[w][0], sums[w][2]
        ring_whole(w).wait_recv()
        total = piece(w, buf, ring.rank)[...]
        for j in range(1, ring.size):
            total = total + got[j - 1]
        return total

    def ex_spots(w):
        base = 0
        for group in plans[w][2]:
            yield base, group
            base += group.size

    def ex_copy(w, e, j):
        base, group = list(ex_spots(w))[e]
        spot = sums[w][3].at[base + group.rank]
        return pltpu.make_async_remote_copy(
            src_ref=spot,
            dst_ref=spot,
            send_sem=ex_sem.at[w, base + j, 0],
            recv_sem=ex_sem.at[w, base + j, 1],
            device_id=group.other(j),
            device_id_type=MESH,
        )

    def ex_start(w, e, total):
        base, group = list(ex_spots(w))[e]
        sums[w][3][base + group.rank] = total
        for j in range(1, group.size):
            ex_copy(w, e, j).start()

    def ex_finish(w, e):
        base, group = list(ex_spots(w))[e]
        buf = sums[w][3]
        for j in range(1, group.size):
            ex_copy(w, e, j).wait_recv()
        total = buf[base]
        for r in range(1, group.size):
            total = total + buf[base + r]
        return total

    def ex_first(w):
        total = ring_finish(w)
        if len(plans[w][2]) > 0:
            ex_start(w, 0, total)
        return total

    def ex_all(w, total):
        for e in range(len(plans[w][2])):
            total = ex_finish(w, e)
            if e + 1 < len(plans[w][2]):
                ex_start(w, e + 1, total)
        return total

    def share_start(w, total):
        _, ring, _, share = plans[w]
        spot = piece(w, sums[w][4], ring.rank)
        spot[...] = total
        for j in share.far_first():
            sum_copy(w, 2, spot, spot, share.other(j)).start()

    def share_whole(w):
        ring, share, out = plans[w][1], plans[w][3], sums[w][4]
        core = plans[w][0].size
        rows = out.shape[0] // (core * ring.size) * (share.size - 1)
        some = out.at[pl.ds(0, rows)]
        return sum_copy(w, 2, some, some, pos)

    def passes(w):
        core, ring, _, share = plans[w]
        return core.size > 1 and share.size == ring.size

    def pass_copy(w):
        core, out = plans[w][0], sums[w][4]
        half = rows_at(out, core.rank, out.shape[0] // core.size)
        return sum_copy(w, 3, half, half, core.other(1))

    def share_finish(w):
        share_whole(w).wait_recv()
        if passes(w):
            pass_copy(w).start()

    def put(ref, start, d, source):
        ref[pl.ds(start, nodes_of(d)), :] = rim_load(source, d, 1, brick)[: nodes_of(d)]

    def get(ref, start, d):
        values = ref[pl.ds(start, nodes_of(d)), :]
        return values if nodes_of(d) >= TILE else jnp.broadcast_to(values, (TILE, width))

    order = list(reversed(DIRS))
    pad_a[...] = jnp.zeros_like(pad_a)
    pad_s[...] = jnp.zeros_like(pad_s)
    coords = []
    for axis in range(3):
        shape = [brick if i in (axis, 2) else 1 for i in range(3)] + [width]
        coords.append(lax.broadcasted_iota(jnp.int32, shape, axis))

    fetches[0].wait()
    scale_rows = lax.broadcasted_iota(jnp.int32, (count, brick * brick), 0) // brick
    scale_cols = lax.broadcasted_iota(jnp.int32, (count, brick * brick), 1)
    picked = dot(
        (scale_rows == scale_cols).astype(BF16), cop_ref[...].astype(F32).astype(BF16)
    )
    lane = lax.broadcasted_iota(jnp.int32, (count, brick), 1)
    row = lax.broadcasted_iota(jnp.int32, (count, brick), 0) % brick
    picked = jnp.where(lane == row, picked, 0.0).astype(BF16)
    quant[0] = dot(picked, jnp.ones((brick, width), BF16))
    rim_lane = lax.broadcasted_iota(jnp.int32, (rim, width), 1)
    rim_row = lax.broadcasted_iota(jnp.int32, (rim, width), 0) % TILE
    divisors = jnp.concatenate([rim_load(quant.at[0], d, 1, brick) for d in order], axis=0)
    divisors = jnp.where(rim_lane == rim_row, divisors, 0.0).astype(BF16)
    groups = -(-rim // (TILE * TILE)) * TILE
    gather = lax.broadcasted_iota(jnp.int32, (groups, rim), 1) // TILE
    gather = (gather == lax.broadcasted_iota(jnp.int32, (groups, rim), 0)).astype(BF16)
    compact = dot(gather, divisors)
    for d in order:
        start, rows = rims[0][2][d]
        first, n = spots[d][0] // TILE, rim_rows(d, brick) // TILE
        hst0[pl.ds(start + rows - n, n), :] = compact[first : first + n]

    for fetch in fetches[1:4]:
        fetch.wait()
    node = node_ref[...]
    pad_a[1 : brick + 1, 1 : brick + 1] = dot(node, wei[:width]).reshape(cube)
    received = dot(node, wei[width : 2 * width])
    hidden_sum = None
    for k in range(kinds):
        o = [offs[k, axis] for axis in range(3)]
        fetches[4 + k].wait()
        sent = pad_a[pl.ds(1 + o[0], brick), pl.ds(1 + o[1], brick)]
        sent = pltpu.roll(sent.reshape(brick * brick, brick, width), lax.rem(brick - o[2], brick), 1)
        pre = dot(edges[k * count : (k + 1) * count], wei[2 * width :])
        pre = pre + received + sent.reshape(count, width)
        sigma = 0.5 * jnp.tanh(0.5 * pre) + 0.5
        hidden = pre * sigma
        valid = None
        for axis in range(3):
            here = coords[axis] + o[axis]
            one = jnp.where((here >= 0) & (here < brick), 1.0, 0.0)
            valid = one if valid is None else valid * one
        valid = valid.reshape(count, width) > 0.0
        sl[k] = jnp.where(valid, sigma + hidden * (1.0 - sigma), 0.0)
        hidden = jnp.where(valid, hidden, 0.0).astype(BF16)
        wide = hidden.astype(F32)
        hidden_sum = wide if hidden_sum is None else hidden_sum + wide
    field[0] = hidden_sum
    for d in order:
        put(hst0, rims[0][2][d][0], d, field.at[0])
    pl.semaphore_wait(barrier, waits)
    rim_start(0)

    for fetch in fetches[4 + kinds :]:
        fetch.wait()
    cot = cot_ref[...]
    quant[1] = dot(node, wni[:width])
    quant[2] = dot_t(cot, wno[...])
    for d in order:
        start, rows = rims[2][2][d]
        put(est, start, d, quant.at[1])
        put(est, start + rows // 2, d, quant.at[2])
    rim_start(2)
    zero[...] = jnp.zeros_like(zero)
    for d in DIRS:
        back = tuple(-step for step in d)

        @pl.when(jnp.logical_not(there[d]))
        def _(d=d, back=back):
            for r, (_, dst, layout) in enumerate(rims):
                start, rows = layout[back]
                arrival = dst.at[pl.ds(start, rows)]
                pltpu.make_async_copy(zero.at[pl.ds(0, rows)], arrival, rim_sem.at[r]).start()
            start, rows = unsent[d]
            pltpu.make_async_copy(zero.at[pl.ds(0, rows)], spill.at[pl.ds(start, rows)], rim_sem.at[3]).start()

    node_t[...] = node.T
    pad_s[0, 1 : brick + 1, 1 : brick + 1] = node.astype(F32).reshape(cube)
    for k in range(kinds):
        o = [offs[k, axis] for axis in range(3)]
        sent = pad_s[0, pl.ds(1 + o[0], brick), pl.ds(1 + o[1], brick)]
        sent = pltpu.roll(sent.reshape(brick * brick, brick, width), lax.rem(brick - o[2], brick), 1)
        columns = pl.ds(k * count, count)
        edges_t[:width, columns] = sent.reshape(count, width).astype(BF16).T
        edges_t[width:, columns] = edges[columns, :].T
    cot_t = cot.T
    quant[0] = 1.0 / quant[0]
    w_out = weo[...]
    twice = jnp.concatenate([w_out, w_out], axis=0)
    tiles = TILE * len(order)
    faces = 6 * brick * brick
    place = lax.broadcasted_iota(jnp.int32, (rim, tiles), 0)
    corners = faces + 12 * brick
    second = jnp.where(place < corners, 0, 1)
    place = jnp.where(place < faces, place // TILE, faces // TILE + (place - faces) // TILE * TILE + second)
    spread = (place == lax.broadcasted_iota(jnp.int32, (rim, tiles), 1)).astype(BF16)

    def node_step(summed, inverse, own, upstream):
        gathered = (summed * inverse).astype(BF16)
        pre = own + dot(gathered, wni[width:])
        sigma = 0.5 * jnp.tanh(0.5 * pre) + 0.5
        hidden = pre * sigma
        slope = (upstream * (sigma + hidden * (1.0 - sigma))).astype(BF16)
        return gathered, hidden, slope, dot_t(slope, wni[width:]) * inverse

    rim_whole(0).wait_recv()
    for d in order:
        rim_add(field.at[0], d, brick, get(hrc0, rims[0][2][d][0], d))
    total = field[0]
    big = total.astype(BF16)
    small = (total - big.astype(F32)).astype(BF16)
    summed = dot(jnp.concatenate([big, small], axis=1), twice)
    field[0] = summed
    gathered, hidden, slope, to_agg = node_step(summed, quant[0], quant[1], quant[2])
    field[1] = to_agg
    ng[:width] = dot(node_t[...], slope)
    ng[width : 2 * width] = outer(gathered, slope)
    ng[2 * width : 3 * width] = dot(cot_t, hidden.astype(BF16)).T
    ng[3 * width :] = outer(big, to_agg.astype(BF16))
    core_start(0)

    compact = jnp.concatenate([hrc0[pl.ds(spot, TILE), :] for spot in divisor_tiles], axis=0).astype(BF16)
    divisors = jnp.where(rim_lane == rim_row, dot(spread, compact), 0.0).astype(BF16)
    divisors = 1.0 / jnp.maximum(dot(divisors, jnp.ones((width, width), BF16)), 1.0)
    beyond = jnp.concatenate([rim_load(field.at[0], d, -1, brick) for d in order], axis=0)
    rim_whole(2).wait_recv()
    own = jnp.concatenate([get(erc, rims[2][2][d][0], d) for d in order], axis=0)
    upstream = jnp.concatenate([get(erc, rims[2][2][d][0] + rims[2][2][d][1] // 2, d) for d in order], axis=0)
    to_rim = node_step(beyond, divisors, own, upstream)[3]
    for d in order:
        start, rows = spots[d]
        rim_add(field.at[1], d, brick, to_rim[start : start + rows])

    ring_start(0)
    arriving = field[1].astype(BF16)
    back = dot_t(arriving, w_out)
    slopes = []
    direct = None
    for k in range(kinds):
        slope_k = (back * sl[k]).astype(BF16)
        slopes.append(slope_k)
        wide = slope_k.astype(F32)
        direct = wide if direct is None else direct + wide
    direct = direct.astype(BF16)
    slope_all = jnp.concatenate(slopes, axis=0)
    both = dot(edges_t[...], slope_all)
    eg[:width] = both[:width]
    eg[width : 2 * width] = dot(node_t[...], direct)
    eg[2 * width :] = both[width:]
    core_start(1)
    turned = None
    for k in range(kinds):
        o = [offs[k, axis] for axis in range(3)]
        pad_s[k, 1 : brick + 1, 1 : brick + 1] = slopes[k].astype(F32).reshape(cube)
        moved = pad_s[k, pl.ds(1 - o[0], brick), pl.ds(1 - o[1], brick)]
        moved = pltpu.roll(moved.reshape(brick * brick, brick, width), lax.rem(brick + o[2], brick), 1)
        turned = moved if turned is None else turned + moved
    turned = turned.reshape(count, width).astype(BF16)
    local = cot.astype(F32) + dot_t(slope, wni[:width])
    local = local + dot_t(turned, wei[:width]) + dot_t(direct, wei[width : 2 * width])
    field[1] = local
    ring_start(1)
    for d in order:
        put(hst1, rims[1][2][d][0], d, field.at[1])
    o_edge[...] = dot_t(slope_all, wei[2 * width :]).astype(BF16)
    firsts = [ex_first(w) for w in range(2)]
    rim_start(1)
    for w in range(2):
        share_start(w, ex_all(w, firsts[w]))
    rim_whole(1).wait_recv()
    for d in order:
        rim_add(field.at[1], d, brick, get(hrc1, rims[1][2][d][0], d))
    o_node[...] = field[1].astype(BF16)
    for w in range(2):
        share_finish(w)
    for w in range(2):
        if passes(w):
            pass_copy(w).wait_recv()

    all_sent = spill.at[pl.ds(0, message_rows(unsent))]
    pltpu.make_async_copy(all_sent, all_sent, rim_sem.at[3]).wait()
    for w in range(2):
        if plans[w][0].size > 1:
            core_copy(w).wait_send()
        ring_whole(w).wait_send()
        share_whole(w).wait_send()
        if passes(w):
            pass_copy(w).wait_send()
        for e, (base, group) in enumerate(ex_spots(w)):
            for j in range(1, group.size):
                ex_copy(w, e, j).wait_send()


def finish(node_in, edge_in, gn, ge, o_node, o_edge, o_ei, o_eo, o_ni, o_no, s_ei, s_n, sems):
    width = gn.shape[1]
    moves = [
        pltpu.make_async_copy(edge_in, o_edge, sems.at[0]),
        pltpu.make_async_copy(node_in, o_node, sems.at[1]),
    ]
    for move in moves:
        move.start()
    totals = [ref[...] for ref in (gn, ge)]
    squares = sum(jnp.sum(t * t, axis=0, keepdims=True) for t in totals)
    squares = jnp.sum(squares, axis=1, keepdims=True)
    entries = sum(t.shape[0] for t in totals) * width
    factor = math.sqrt(entries) / jnp.sqrt(squares)
    s_n[...] = totals[0] * factor
    outs = ((s_n.at[: 2 * width], o_ni), (s_n.at[2 * width : 3 * width], o_no), (s_n.at[3 * width :], o_eo), (s_ei, o_ei))
    for i, (src, dst) in enumerate(outs):
        if src is s_ei:
            s_ei[...] = totals[1] * factor
        moves.append(pltpu.make_async_copy(src, dst, sems.at[2 + i]))
        moves[-1].start()
    for move in moves:
        move.wait()


def on_device(
    sizes, node_feat, edge_feat, copies, offsets, w_edge_in, w_edge_out, w_node_in, w_node_out, node_cot
):
    brick = node_feat.shape[0]
    width = node_feat.shape[3]
    kinds = edge_feat.shape[0]
    count = brick**3
    rims = [rim_layout(brick, *how)[1] for how in ((1, 1), (1, 0), (2, 0), (4, 1))]
    dims = [plan_sizes(sizes, plan) for plan in PLANS]
    others = [max(sum(axis_part(sizes, a, p)[1] for a, p in rest), 1) for _, _, rest in dims]
    vmem = pl.BlockSpec(memory_space=pltpu.VMEM)
    hbm = pl.BlockSpec(memory_space=pl.ANY)
    far = pl.BlockSpec(memory_space=pltpu.HBM)
    dma = pltpu.SemaphoreType.DMA
    b, w = brick, width
    rows = (4 * w, 3 * w)
    outs = pl.pallas_call(
        functools.partial(kernel, sizes),
        out_shape=(
            jax.ShapeDtypeStruct((count, w), BF16),
            jax.ShapeDtypeStruct((kinds * count, w), BF16),
            *[jax.ShapeDtypeStruct((r, w), F32) for r in rows],
        ),
        in_specs=[far] * 9,
        out_specs=(vmem, vmem, vmem, vmem),
        scratch_shapes=[
            pltpu.SMEM(offsets.shape, jnp.int32),
            pltpu.VMEM((count, w), BF16),
            pltpu.VMEM((kinds * count, w), BF16),
            pltpu.VMEM((b * b, b), jnp.int32),
            pltpu.VMEM((3 * w, w), BF16),
            pltpu.VMEM((w, w), BF16),
            pltpu.VMEM((2 * w, w), BF16),
            pltpu.VMEM((w, w), BF16),
            pltpu.VMEM((count, w), BF16),
            pltpu.VMEM((b + 2, b + 2, b, w), F32),
            pltpu.VMEM((kinds, b + 2, b + 2, b, w), F32),
            pltpu.VMEM((kinds, count, w), F32),
            pltpu.VMEM((2, count, w), F32),
            pltpu.VMEM((3, count, w), F32),
            *[pltpu.VMEM((r, w), F32) for r in (rims[0], rims[0], rims[1], rims[1], rims[2], rims[2])],
            pltpu.VMEM((4 * b * b + TILE, w), F32),
            pltpu.VMEM((rims[3], w), F32),
            pltpu.VMEM((w, count), BF16),
            pltpu.VMEM((2 * w, kinds * count), BF16),
            *[pltpu.VMEM((r, w), F32) for r in rows],
            *[pltpu.VMEM((r // c, w), F32) for r, (c, _, _) in zip(rows, dims)],
            *[pltpu.VMEM((m - 1, r // (c * m), w), F32) for r, (c, m, _) in zip(rows, dims)],
            *[pltpu.VMEM((n, r // (c * m), w), F32) for r, n, (c, m, _) in zip(rows, others, dims)],
            dma((8 + kinds,)),
            dma((4,)),
            dma((2, 4, 2)),
            dma((2, max(others), 2)),
        ],
        compiler_params=pltpu.CompilerParams(
            collective_id=0, has_side_effects=True, vmem_limit_bytes=VMEM_MAIN
        ),
    )(
        pltpu.with_memory_space_constraint(offsets, pltpu.HBM),
        *[
            pltpu.with_memory_space_constraint(array, pltpu.HBM)
            for array in (
                node_feat.reshape(count, w),
                edge_feat.reshape(kinds * count, w),
                copies.reshape(b * b, b),
                w_edge_in,
                w_edge_out,
                w_node_in,
                w_node_out,
                node_cot.reshape(count, w),
            )
        ],
    )
    done = pl.pallas_call(
        finish,
        out_shape=(
            jax.ShapeDtypeStruct((count, w), BF16),
            jax.ShapeDtypeStruct((kinds * count, w), BF16),
            jax.ShapeDtypeStruct((3 * w, w), F32),
            jax.ShapeDtypeStruct((w, w), F32),
            jax.ShapeDtypeStruct((2 * w, w), F32),
            jax.ShapeDtypeStruct((w, w), F32),
        ),
        in_specs=[hbm, hbm, vmem, vmem],
        out_specs=(hbm,) * 6,
        scratch_shapes=[pltpu.VMEM((rows[1], w), F32), pltpu.VMEM((rows[0], w), F32), dma((6,))],
        compiler_params=pltpu.CompilerParams(vmem_limit_bytes=VMEM_FINISH),
    )(*outs)
    return (done[0].reshape(node_feat.shape), done[1].reshape(edge_feat.shape)) + tuple(done[2:])


def solution(mesh):
    sizes = {a: mesh.shape[a] for a in AXES}
    bricks, edges = P("gx", "gy", "gz", None), P(None, "gx", "gy", "gz", None)
    return jax.shard_map(
        functools.partial(on_device, sizes),
        mesh=mesh,
        in_specs=(bricks, edges, P("gx", "gy", "gz"), P(), P(), P(), P(), P(), bricks),
        out_specs=(bricks, edges, P(), P(), P(), P()),
        check_vma=False,
    )
```

```python
import functools
import math

import jax
import jax.numpy as jnp
from jax import lax
from jax.experimental import pallas as pl
from jax.experimental.pallas import tpu as pltpu
from jax.sharding import PartitionSpec as P

F32 = jnp.float32
BF16 = jnp.bfloat16
VMEM_MAIN = 28 * 2**20
VMEM_FINISH = 8 * 2**20
AXES = ("gx", "gy", "gz")
MESH = pl.DeviceIdType.MESH
TILE = 8
PLANS = (
    (True, (('gx', 'low'), ('gy', 'high'), ('gz', 'low')), (('gx', 'high'), ('gz', 'high')), False),
    (True, (('gx', 'low'), ('gy', 'high'), ('gz', 'low')), (('gx', 'high'), ('gz', 'high')), True),
)
DIRS = [
    (dx, dy, dz)
    for dx in (-1, 0, 1)
    for dy in (-1, 0, 1)
    for dz in (-1, 0, 1)
    if (dx, dy, dz) != (0, 0, 0)
]
DIRS.sort(key=lambda d: -sum(map(abs, d)))


def dot(left, right):
    return jnp.dot(left, right, preferred_element_type=F32)


def dot_t(left, right):
    return lax.dot_general(left, right, (((1,), (1,)), ((), ())), preferred_element_type=F32)


def outer(left, right):
    return lax.dot_general(left, right, (((0,), (0,)), ((), ())), preferred_element_type=F32)


def rim_layout(brick, times, extra):
    spots, base = {}, 0
    for d in reversed(DIRS):
        nodes = brick ** (3 - sum(map(abs, d)))
        rows = times * nodes + extra * max(nodes // TILE, 1)
        spots[d] = (base, rows)
        base += -(-rows // TILE) * TILE
    return spots, base


def rim_tiles(brick):
    spots, base = {}, 0
    for d in reversed(DIRS):
        spots[d] = (base, rim_rows(d, brick))
        base += spots[d][1]
    return spots, base


def message_rows(layout):
    return sum(rows for _, rows in layout.values())


def rim_rows(d, brick):
    return max(brick ** (3 - sum(map(abs, d))), TILE)


def rim_place(d, sign, brick):
    return [None if s == 0 else (brick - 1 if s * sign > 0 else 0) for s in d]


def rim_slices(d, sign, brick):
    x, y, z = rim_place(d, sign, brick)
    face = brick * brick
    if z is None:
        if y is None:
            return [pl.ds(x * face, face)]
        if x is None:
            return [pl.ds(i * face + y * brick, brick) for i in range(brick)]
        return [pl.ds(x * face + y * brick, brick)]
    if x is None and y is None:
        return [pl.ds(z, face, stride=brick)]
    if y is None:
        return [pl.ds(x * face + z, brick, stride=brick)]
    if x is None:
        return [pl.ds(y * brick + z, brick, stride=face)]
    return [pl.ds(x * face + y * brick + z, 1)]


def rim_load(ref, d, sign, brick):
    parts = [ref[s, :] for s in rim_slices(d, sign, brick)]
    if len(parts) > 1:
        return jnp.concatenate(parts, axis=0)
    if parts[0].shape[0] < 8:
        return jnp.broadcast_to(parts[0], (8, parts[0].shape[1]))
    return parts[0]


def rim_add(ref, d, brick, values):
    slices = rim_slices(d, -1, brick)
    for i, s in enumerate(slices):
        rows = s.size
        ref[s, :] = ref[s, :] + values[i * rows : (i + 1) * rows]


def axis_part(sizes, a, part):
    low = 2 if sizes[a] % 2 == 0 else 1
    return {"all": (1, sizes[a]), "low": (1, low), "high": (low, sizes[a] // low)}[part]


def plan_sizes(sizes, plan):
    pre, ring, rest, _ = plan
    cores = axis_part(sizes, "gy", "low")[1] if pre else 1
    members = math.prod(axis_part(sizes, a, p)[1] for a, p in ring)
    rest = [(a, p) for a, p in rest if axis_part(sizes, a, p)[1] > 1]
    return cores, members, rest


def sent_rows(sizes, plan, rows):
    cores, members, rest = plan_sizes(sizes, plan)
    piece = rows // (cores * members)
    total = (members - 1) * piece + sum(axis_part(sizes, a, p)[1] - 1 for a, p in rest) * piece
    if plan[0] and plan[3]:
        total += (cores * members - 1) * piece
    else:
        total += (members - 1) * piece + (cores > 1) * rows // cores
    return total + (cores > 1) * rows // cores


class Group:
    def __init__(self, sizes, pos, axes):
        self.pos, self.axes = pos, [(a, *axis_part(sizes, a, p)) for a, p in axes]
        self.size = math.prod(n for _, _, n in self.axes)
        self.here = [lax.rem(pos[a] // f, n) if f * n < sizes[a] else pos[a] // f for a, f, n in self.axes]
        self.rank = self.fold(self.here)

    def fold(self, spots):
        rank = 0
        for (_, _, n), spot in zip(self.axes, spots):
            rank = rank * n + spot
        return rank

    def meet(self, j):
        spots, place = [], dict(self.pos)
        for (a, f, n), here in reversed(list(zip(self.axes, self.here))):
            digit, j = j % n, j // n
            there = here
            if digit > 0:
                there = 1 - here if n == 2 else lax.rem(here + digit, n)
                place[a] = place[a] + (there - here) * f
            spots.append(there)
        return self.fold(reversed(spots)), place

    def other(self, j):
        return self.meet(j)[1]

    def steps(self, j):
        steps = []
        for a, f, n in reversed(self.axes):
            if j % n != 0:
                steps.append((a, f, n, j % n))
            j = j // n
        return tuple(sorted(steps))

    def steps(self, j):
        steps = []
        for a, f, n in reversed(self.axes):
            if j % n != 0:
                steps.append((a, f, n, j % n))
            j = j // n
        return tuple(sorted(steps))

    def far_first(self):
        hops = lambda j: sum((a, f, n) != ("gy", 1, 2) for a, f, n, _ in self.steps(j))
        return sorted(range(1, self.size), key=lambda j: -hops(j))


def kernel(
    sizes,
    offs_hbm, node_hbm, edge_hbm, cop_hbm, wei_hbm, weo_hbm, wni_hbm, wno_hbm, cot_hbm,
    o_node, o_edge, gn, ge,
    offs, node_ref, edges, cop_ref, wei, weo, wni, wno, cot_ref, pad_a, pad_s, sl,
    field, quant, hst0, hrc0, hst1, hrc1, est, erc, zero, spill, node_t, edges_t,
    ng, eg, cbn, cbe, rbn, rbe, exn, exe,
    in_sem, rim_sem, sum_sem, ex_sem,
):
    width = node_ref.shape[1]
    count = node_ref.shape[0]
    kinds = offs.shape[0]
    brick = pad_a.shape[2]
    cube = (brick, brick, brick, width)
    pos = {a: lax.axis_index(a) for a in AXES}
    spots, rim = rim_tiles(brick)

    moves = (
        [(cop_hbm, cop_ref), (offs_hbm, offs), (node_hbm, node_ref), (wei_hbm, wei), (edge_hbm, edges)]
        + [(wni_hbm, wni), (cot_hbm, cot_ref), (wno_hbm, wno), (weo_hbm, weo)]
    )
    fetches = [
        pltpu.make_async_copy(src, dst, in_sem.at[i]) for i, (src, dst) in zip((0, 1, 2, 2, 3, 4, 4, 4, 4), moves)
    ]

    def landed(i, refs):
        rows = edges.at[pl.ds(0, sum(ref.shape[0] for ref in refs))]
        pltpu.make_async_copy(rows, rows, in_sem.at[i]).wait()

    for fetch in fetches[:5]:
        fetch.start()

    inside = {(a, s): (pos[a] + s >= 0) & (pos[a] + s < sizes[a]) for a in AXES for s in (-1, 1)}
    there = {d: functools.reduce(jnp.logical_and, [inside[a, s] for a, s in zip(AXES, d) if s != 0]) for d in DIRS}

    def shifted(d, sign):
        return {a: pos[a] + sign * step for a, step in zip(AXES, d)}

    plans = []
    for pre, ring, rest, direct in PLANS:
        rest = plan_sizes(sizes, (pre, ring, rest, direct))[2]
        core = Group(sizes, pos, (("gy", "low"),) if pre else ())
        share = Group(sizes, pos, ((("gy", "low"),) if pre and direct else ()) + ring)
        plans.append((core, Group(sizes, pos, ring), [Group(sizes, pos, (ap,)) for ap in rest], share))

    def nodes_of(d):
        return brick ** (3 - sum(map(abs, d)))

    rims = (
        (hst0, hrc0, rim_layout(brick, 1, 1)[0]),
        (hst1, hrc1, rim_layout(brick, 1, 0)[0]),
        (est, erc, rim_layout(brick, 2, 0)[0]),
    )
    unsent = rim_layout(brick, 4, 1)[0]
    divisor_tiles = [start + nodes_of(d) // TILE * TILE for d, (start, _) in rims[0][2].items()]
    for d, spot in zip(rims[0][2], divisor_tiles):
        if nodes_of(d) < brick * brick:
            hrc0[pl.ds(spot, TILE), :] = jnp.zeros((TILE, width), F32)
    barrier = pltpu.get_barrier_semaphore()

    def greet(place):
        pl.semaphore_signal(barrier, inc=1, device_id=place, device_id_type=MESH)

    waits = jnp.int32(0)
    for d in DIRS:
        waits = waits + there[d].astype(jnp.int32)

        @pl.when(there[d])
        def _(d=d):
            greet(shifted(d, 1))

    met = set()
    for core, ring, rest, share in plans:
        for group in (core, ring, share, *rest):
            for j in group.far_first():
                steps = group.steps(j)
                if steps not in met and any((f, n) != (1, 2) for _, f, n, _ in steps):
                    met.add(steps)
                    waits = waits + 1
                    greet(group.other(j))

    for fetch in fetches[5:]:
        fetch.start()
    def rim_copy(r, start, rows, place):
        src, dst = rims[r][:2]
        return pltpu.make_async_remote_copy(
            src_ref=src.at[pl.ds(start, rows)],
            dst_ref=dst.at[pl.ds(start, rows)],
            send_sem=rim_sem.at[3],
            recv_sem=rim_sem.at[r],
            device_id=place,
            device_id_type=MESH,
        )

    def rim_start(r):
        for d in reversed(DIRS) if r == 1 else DIRS:

            @pl.when(there[d])
            def _(d=d):
                rim_copy(r, *rims[r][2][d], shifted(d, 1)).start()

    def rim_whole(r):
        return rim_copy(r, 0, message_rows(rims[r][2]), pos)

    def rows_at(ref, index, rows):
        return ref.at[pl.ds(pl.multiple_of(index * rows, 8), rows)]

    sums = ((ng, cbn, rbn, exn, gn), (eg, cbe, rbe, exe, ge))

    def sum_copy(w, stage, src, dst, place):
        return pltpu.make_async_remote_copy(
            src_ref=src,
            dst_ref=dst,
            send_sem=rim_sem.at[3],
            recv_sem=sum_sem.at[w, stage],
            device_id=place,
            device_id_type=MESH,
        )

    def core_copy(w):
        core, buf, got = plans[w][0], *sums[w][:2]
        return sum_copy(w, 0, rows_at(buf, 1 - core.rank, got.shape[0]), got, core.other(1))

    def core_start(w):
        if plans[w][0].size > 1:
            core_copy(w).start()

    def piece(w, ref, rank):
        core, ring = plans[w][:2]
        return rows_at(ref, core.rank * ring.size + rank, ref.shape[0] // (core.size * ring.size))

    def ring_copy(w, j):
        ring, buf, got = plans[w][1], sums[w][0], sums[w][2]
        to, place = ring.meet(j)
        return sum_copy(w, 1, piece(w, buf, to), got.at[j - 1], place)

    def ring_whole(w):
        got = sums[w][2]
        return sum_copy(w, 1, got, got, pos)

    def ring_start(w):
        core, ring = plans[w][:2]
        if core.size > 1:
            buf, got = sums[w][:2]
            half = rows_at(buf, core.rank, got.shape[0])
            core_copy(w).wait_recv()
            half[...] = half[...] + got[...]
        for j in ring.far_first():
            ring_copy(w, j).start()

    def ring_finish(w):
        ring, buf, got = plans[w][1], sums[w][0], sums[w][2]
        ring_whole(w).wait_recv()
        total = piece(w, buf, ring.rank)[...]
        for j in range(1, ring.size):
            total = total + got[j - 1]
        return total

    def ex_spots(w):
        base = 0
        for group in plans[w][2]:
            yield base, group
            base += group.size

    def ex_copy(w, e, j):
        base, group = list(ex_spots(w))[e]
        spot = sums[w][3].at[base + group.rank]
        return pltpu.make_async_remote_copy(
            src_ref=spot,
            dst_ref=spot,
            send_sem=rim_sem.at[3],
            recv_sem=ex_sem.at[w, base - e + j - 1],
            device_id=group.other(j),
            device_id_type=MESH,
        )

    def ex_start(w, e, total):
        base, group = list(ex_spots(w))[e]
        sums[w][3][base + group.rank] = total
        for j in range(1, group.size):
            ex_copy(w, e, j).start()

    def ex_finish(w, e):
        base, group = list(ex_spots(w))[e]
        buf = sums[w][3]
        for j in range(1, group.size):
            ex_copy(w, e, j).wait_recv()
        total = buf[base]
        for r in range(1, group.size):
            total = total + buf[base + r]
        return total

    def ex_first(w):
        total = ring_finish(w)
        if len(plans[w][2]) > 0:
            ex_start(w, 0, total)
        return total

    def ex_all(w, total):
        for e in range(len(plans[w][2])):
            total = ex_finish(w, e)
            if e + 1 < len(plans[w][2]):
                ex_start(w, e + 1, total)
        return total

    def share_start(w, total):
        _, ring, _, share = plans[w]
        spot = piece(w, sums[w][4], ring.rank)
        spot[...] = total
        for j in share.far_first():
            sum_copy(w, 2, spot, spot, share.other(j)).start()

    def share_whole(w):
        ring, share, out = plans[w][1], plans[w][3], sums[w][4]
        core = plans[w][0].size
        rows = out.shape[0] // (core * ring.size) * (share.size - 1)
        some = out.at[pl.ds(0, rows)]
        return sum_copy(w, 2, some, some, pos)

    def passes(w):
        core, ring, _, share = plans[w]
        return core.size > 1 and share.size == ring.size

    def pass_copy(w):
        core, out = plans[w][0], sums[w][4]
        half = rows_at(out, core.rank, out.shape[0] // core.size)
        return sum_copy(w, 3, half, half, core.other(1))

    def share_finish(w):
        share_whole(w).wait_recv()
        if passes(w):
            pass_copy(w).start()

    def put(ref, start, d, source):
        ref[pl.ds(start, nodes_of(d)), :] = rim_load(source, d, 1, brick)[: nodes_of(d)]

    def get(ref, start, d):
        values = ref[pl.ds(start, nodes_of(d)), :]
        return values if nodes_of(d) >= TILE else jnp.broadcast_to(values, (TILE, width))

    order = list(reversed(DIRS))
    pad_a[...] = jnp.zeros_like(pad_a)
    pad_s[...] = jnp.zeros_like(pad_s)
    coords = []
    for axis in range(3):
        shape = [brick if i in (axis, 2) else 1 for i in range(3)] + [width]
        coords.append(lax.broadcasted_iota(jnp.int32, shape, axis))

    fetches[0].wait()
    scale_rows = lax.broadcasted_iota(jnp.int32, (count, brick * brick), 0) // brick
    scale_cols = lax.broadcasted_iota(jnp.int32, (count, brick * brick), 1)
    picked = dot(
        (scale_rows == scale_cols).astype(BF16), cop_ref[...].astype(F32).astype(BF16)
    )
    lane = lax.broadcasted_iota(jnp.int32, (count, brick), 1)
    row = lax.broadcasted_iota(jnp.int32, (count, brick), 0) % brick
    picked = jnp.where(lane == row, picked, 0.0).astype(BF16)
    quant[0] = dot(picked, jnp.ones((brick, width), BF16))
    rim_lane = lax.broadcasted_iota(jnp.int32, (rim, width), 1)
    rim_row = lax.broadcasted_iota(jnp.int32, (rim, width), 0) % TILE
    divisors = jnp.concatenate([rim_load(quant.at[0], d, 1, brick) for d in order], axis=0)
    divisors = jnp.where(rim_lane == rim_row, divisors, 0.0).astype(BF16)
    groups = -(-rim // (TILE * TILE)) * TILE
    gather = lax.broadcasted_iota(jnp.int32, (groups, rim), 1) // TILE
    gather = (gather == lax.broadcasted_iota(jnp.int32, (groups, rim), 0)).astype(BF16)
    compact = dot(gather, divisors)
    for d in order:
        start, rows = rims[0][2][d]
        first, n = spots[d][0] // TILE, rim_rows(d, brick) // TILE
        hst0[pl.ds(start + rows - n, n), :] = compact[first : first + n]

    fetches[1].wait()
    landed(2, (node_ref, wei))
    node = node_ref[...]
    pad_a[1 : brick + 1, 1 : brick + 1] = dot(node, wei[:width]).reshape(cube)
    received = dot(node, wei[width : 2 * width])
    fetches[4].wait()
    hidden_sum = None
    for k in range(kinds):
        o = [offs[k, axis] for axis in range(3)]
        sent = pad_a[pl.ds(1 + o[0], brick), pl.ds(1 + o[1], brick)]
        sent = pltpu.roll(sent.reshape(brick * brick, brick, width), lax.rem(brick - o[2], brick), 1)
        pre = dot(edges[k * count : (k + 1) * count], wei[2 * width :])
        pre = pre + received + sent.reshape(count, width)
        sigma = 0.5 * jnp.tanh(0.5 * pre) + 0.5
        hidden = pre * sigma
        valid = None
        for axis in range(3):
            here = coords[axis] + o[axis]
            one = jnp.where((here >= 0) & (here < brick), 1.0, 0.0)
            valid = one if valid is None else valid * one
        valid = valid.reshape(count, width) > 0.0
        sl[k] = jnp.where(valid, sigma + hidden * (1.0 - sigma), 0.0)
        hidden = jnp.where(valid, hidden, 0.0).astype(BF16)
        wide = hidden.astype(F32)
        hidden_sum = wide if hidden_sum is None else hidden_sum + wide
    field[0] = hidden_sum
    for d in order:
        put(hst0, rims[0][2][d][0], d, field.at[0])
    pl.semaphore_wait(barrier, waits)
    rim_start(0)

    landed(4, (wni, cot_ref, wno, weo))
    cot = cot_ref[...]
    quant[1] = dot(node, wni[:width])
    quant[2] = dot_t(cot, wno[...])
    for d in order:
        start, rows = rims[2][2][d]
        put(est, start, d, quant.at[1])
        put(est, start + rows // 2, d, quant.at[2])
    rim_start(2)
    zero[...] = jnp.zeros_like(zero)
    for d in DIRS:
        back = tuple(-step for step in d)

        @pl.when(jnp.logical_not(there[d]))
        def _(d=d, back=back):
            for r, (_, dst, layout) in enumerate(rims):
                start, rows = layout[back]
                arrival = dst.at[pl.ds(start, rows)]
                pltpu.make_async_copy(zero.at[pl.ds(0, rows)], arrival, rim_sem.at[r]).start()
            start, rows = unsent[d]
            pltpu.make_async_copy(zero.at[pl.ds(0, rows)], spill.at[pl.ds(start, rows)], rim_sem.at[3]).start()

    node_t[...] = node.T
    pad_s[0, 1 : brick + 1, 1 : brick + 1] = node.astype(F32).reshape(cube)
    for k in range(kinds):
        o = [offs[k, axis] for axis in range(3)]
        sent = pad_s[0, pl.ds(1 + o[0], brick), pl.ds(1 + o[1], brick)]
        sent = pltpu.roll(sent.reshape(brick * brick, brick, width), lax.rem(brick - o[2], brick), 1)
        columns = pl.ds(k * count, count)
        edges_t[:width, columns] = sent.reshape(count, width).astype(BF16).T
        edges_t[width:, columns] = edges[columns, :].T
    cot_t = cot.T
    quant[0] = 1.0 / quant[0]
    w_out = weo[...]
    twice = jnp.concatenate([w_out, w_out], axis=0)
    tiles = TILE * len(order)
    faces = 6 * brick * brick
    place = lax.broadcasted_iota(jnp.int32, (rim, tiles), 0)
    corners = faces + 12 * brick
    second = jnp.where(place < corners, 0, 1)
    place = jnp.where(place < faces, place // TILE, faces // TILE + (place - faces) // TILE * TILE + second)
    spread = (place == lax.broadcasted_iota(jnp.int32, (rim, tiles), 1)).astype(BF16)

    def node_step(summed, inverse, own, upstream):
        gathered = (summed * inverse).astype(BF16)
        pre = own + dot(gathered, wni[width:])
        sigma = 0.5 * jnp.tanh(0.5 * pre) + 0.5
        hidden = pre * sigma
        slope = (upstream * (sigma + hidden * (1.0 - sigma))).astype(BF16)
        return gathered, hidden, slope, dot_t(slope, wni[width:]) * inverse

    rim_whole(0).wait_recv()
    for d in order:
        rim_add(field.at[0], d, brick, get(hrc0, rims[0][2][d][0], d))
    total = field[0]
    big = total.astype(BF16)
    small = (total - big.astype(F32)).astype(BF16)
    summed = dot(jnp.concatenate([big, small], axis=1), twice)
    field[0] = summed
    gathered, hidden, slope, to_agg = node_step(summed, quant[0], quant[1], quant[2])
    field[1] = to_agg
    ng[:width] = dot(node_t[...], slope)
    ng[width : 2 * width] = outer(gathered, slope)
    ng[2 * width : 3 * width] = dot(cot_t, hidden.astype(BF16)).T
    ng[3 * width :] = outer(big, to_agg.astype(BF16))
    core_start(0)

    compact = jnp.concatenate([hrc0[pl.ds(spot, TILE), :] for spot in divisor_tiles], axis=0).astype(BF16)
    divisors = jnp.where(rim_lane == rim_row, dot(spread, compact), 0.0).astype(BF16)
    divisors = 1.0 / jnp.maximum(dot(divisors, jnp.ones((width, width), BF16)), 1.0)
    beyond = jnp.concatenate([rim_load(field.at[0], d, -1, brick) for d in order], axis=0)
    rim_whole(2).wait_recv()
    own = jnp.concatenate([get(erc, rims[2][2][d][0], d) for d in order], axis=0)
    upstream = jnp.concatenate([get(erc, rims[2][2][d][0] + rims[2][2][d][1] // 2, d) for d in order], axis=0)
    to_rim = node_step(beyond, divisors, own, upstream)[3]
    for d in order:
        start, rows = spots[d]
        rim_add(field.at[1], d, brick, to_rim[start : start + rows])

    ring_start(0)
    arriving = field[1].astype(BF16)
    back = dot_t(arriving, w_out)
    slopes = []
    direct = None
    for k in range(kinds):
        slope_k = (back * sl[k]).astype(BF16)
        slopes.append(slope_k)
        wide = slope_k.astype(F32)
        direct = wide if direct is None else direct + wide
    direct = direct.astype(BF16)
    slope_all = jnp.concatenate(slopes, axis=0)
    both = dot(edges_t[...], slope_all)
    eg[:width] = both[:width]
    eg[width : 2 * width] = dot(node_t[...], direct)
    eg[2 * width :] = both[width:]
    core_start(1)
    turned = None
    for k in range(kinds):
        o = [offs[k, axis] for axis in range(3)]
        pad_s[k, 1 : brick + 1, 1 : brick + 1] = slopes[k].astype(F32).reshape(cube)
        moved = pad_s[k, pl.ds(1 - o[0], brick), pl.ds(1 - o[1], brick)]
        moved = pltpu.roll(moved.reshape(brick * brick, brick, width), lax.rem(brick + o[2], brick), 1)
        turned = moved if turned is None else turned + moved
    turned = turned.reshape(count, width).astype(BF16)
    local = cot.astype(F32) + dot_t(slope, wni[:width])
    local = local + dot_t(turned, wei[:width]) + dot_t(direct, wei[width : 2 * width])
    field[1] = local
    ring_start(1)
    for d in order:
        put(hst1, rims[1][2][d][0], d, field.at[1])
    o_edge[...] = dot_t(slope_all, wei[2 * width :]).astype(BF16)
    firsts = [ex_first(w) for w in range(2)]
    rim_start(1)
    for w in range(2):
        share_start(w, ex_all(w, firsts[w]))
    rim_whole(1).wait_recv()
    for d in order:
        rim_add(field.at[1], d, brick, get(hrc1, rims[1][2][d][0], d))
    o_node[...] = field[1].astype(BF16)
    for w in range(2):
        share_finish(w)
    for w in range(2):
        if passes(w):
            pass_copy(w).wait_recv()

    pltpu.make_async_copy(spill, spill, rim_sem.at[3]).wait()


def finish(node_in, edge_in, gn, ge, o_node, o_edge, o_ei, o_eo, o_ni, o_no, s_ei, s_n, sems):
    width = gn.shape[1]
    moves = [
        pltpu.make_async_copy(edge_in, o_edge, sems.at[0]),
        pltpu.make_async_copy(node_in, o_node, sems.at[1]),
    ]
    for move in moves:
        move.start()
    totals = [ref[...] for ref in (gn, ge)]
    squares = sum(jnp.sum(t * t, axis=0, keepdims=True) for t in totals)
    squares = jnp.sum(squares, axis=1, keepdims=True)
    entries = sum(t.shape[0] for t in totals) * width
    factor = math.sqrt(entries) / jnp.sqrt(squares)
    s_n[...] = totals[0] * factor
    outs = ((s_n.at[: 2 * width], o_ni), (s_n.at[2 * width : 3 * width], o_no), (s_n.at[3 * width :], o_eo), (s_ei, o_ei))
    for i, (src, dst) in enumerate(outs):
        if src is s_ei:
            s_ei[...] = totals[1] * factor
        moves.append(pltpu.make_async_copy(src, dst, sems.at[2 + i]))
        moves[-1].start()
    for move in moves:
        move.wait()


def on_device(
    sizes, node_feat, edge_feat, copies, offsets, w_edge_in, w_edge_out, w_node_in, w_node_out, node_cot
):
    brick = node_feat.shape[0]
    width = node_feat.shape[3]
    kinds = edge_feat.shape[0]
    count = brick**3
    rims = [rim_layout(brick, *how)[1] for how in ((1, 1), (1, 0), (2, 0))]
    dims = [plan_sizes(sizes, plan) for plan in PLANS]
    others = [max(sum(axis_part(sizes, a, p)[1] for a, p in rest), 1) for _, _, rest in dims]
    sent = message_rows(rim_layout(brick, 4, 1)[0])
    sent += sum(sent_rows(sizes, plan, n * width) for plan, n in zip(PLANS, (4, 3)))
    vmem = pl.BlockSpec(memory_space=pltpu.VMEM)
    hbm = pl.BlockSpec(memory_space=pl.ANY)
    far = pl.BlockSpec(memory_space=pltpu.HBM)
    dma = pltpu.SemaphoreType.DMA
    b, w = brick, width
    rows = (4 * w, 3 * w)
    outs = pl.pallas_call(
        functools.partial(kernel, sizes),
        out_shape=(
            jax.ShapeDtypeStruct((count, w), BF16),
            jax.ShapeDtypeStruct((kinds * count, w), BF16),
            *[jax.ShapeDtypeStruct((r, w), F32) for r in rows],
        ),
        in_specs=[far] * 9,
        out_specs=(vmem, vmem, vmem, vmem),
        scratch_shapes=[
            pltpu.SMEM(offsets.shape, jnp.int32),
            pltpu.VMEM((count, w), BF16),
            pltpu.VMEM((kinds * count, w), BF16),
            pltpu.VMEM((b * b, b), jnp.int32),
            pltpu.VMEM((3 * w, w), BF16),
            pltpu.VMEM((w, w), BF16),
            pltpu.VMEM((2 * w, w), BF16),
            pltpu.VMEM((w, w), BF16),
            pltpu.VMEM((count, w), BF16),
            pltpu.VMEM((b + 2, b + 2, b, w), F32),
            pltpu.VMEM((kinds, b + 2, b + 2, b, w), F32),
            pltpu.VMEM((kinds, count, w), F32),
            pltpu.VMEM((2, count, w), F32),
            pltpu.VMEM((3, count, w), F32),
            *[pltpu.VMEM((r, w), F32) for r in (rims[0], rims[0], rims[1], rims[1], rims[2], rims[2])],
            pltpu.VMEM((4 * b * b + TILE, w), F32),
            pltpu.VMEM((sent, w), F32),
            pltpu.VMEM((w, count), BF16),
            pltpu.VMEM((2 * w, kinds * count), BF16),
            *[pltpu.VMEM((r, w), F32) for r in rows],
            *[pltpu.VMEM((r // c, w), F32) for r, (c, _, _) in zip(rows, dims)],
            *[pltpu.VMEM((m - 1, r // (c * m), w), F32) for r, (c, m, _) in zip(rows, dims)],
            *[pltpu.VMEM((n, r // (c * m), w), F32) for r, n, (c, m, _) in zip(rows, others, dims)],
            dma((5,)),
            dma((4,)),
            dma((2, 4)),
            dma((2, max(max(n - len(rest) for n, (_, _, rest) in zip(others, dims)), 1))),
        ],
        compiler_params=pltpu.CompilerParams(
            collective_id=0, has_side_effects=True, vmem_limit_bytes=VMEM_MAIN
        ),
    )(
        pltpu.with_memory_space_constraint(offsets, pltpu.HBM),
        *[
            pltpu.with_memory_space_constraint(array, pltpu.HBM)
            for array in (
                node_feat.reshape(count, w),
                edge_feat.reshape(kinds * count, w),
                copies.reshape(b * b, b),
                w_edge_in,
                w_edge_out,
                w_node_in,
                w_node_out,
                node_cot.reshape(count, w),
            )
        ],
    )
    done = pl.pallas_call(
        finish,
        out_shape=(
            jax.ShapeDtypeStruct((count, w), BF16),
            jax.ShapeDtypeStruct((kinds * count, w), BF16),
            jax.ShapeDtypeStruct((3 * w, w), F32),
            jax.ShapeDtypeStruct((w, w), F32),
            jax.ShapeDtypeStruct((2 * w, w), F32),
            jax.ShapeDtypeStruct((w, w), F32),
        ),
        in_specs=[hbm, hbm, vmem, vmem],
        out_specs=(hbm,) * 6,
        scratch_shapes=[pltpu.VMEM((rows[1], w), F32), pltpu.VMEM((rows[0], w), F32), dma((6,))],
        compiler_params=pltpu.CompilerParams(vmem_limit_bytes=VMEM_FINISH),
    )(*outs)
    return (done[0].reshape(node_feat.shape), done[1].reshape(edge_feat.shape)) + tuple(done[2:])


def solution(mesh):
    sizes = {a: mesh.shape[a] for a in AXES}
    bricks, edges = P("gx", "gy", "gz", None), P(None, "gx", "gy", "gz", None)
    return jax.shard_map(
        functools.partial(on_device, sizes),
        mesh=mesh,
        in_specs=(bricks, edges, P("gx", "gy", "gz"), P(), P(), P(), P(), P(), bricks),
        out_specs=(bricks, edges, P(), P(), P(), P()),
        check_vma=False,
    )
```

```python
import functools
import math

import jax
import jax.numpy as jnp
from jax import lax
from jax.experimental import pallas as pl
from jax.experimental.pallas import tpu as pltpu
from jax.sharding import PartitionSpec as P

F32 = jnp.float32
BF16 = jnp.bfloat16
VMEM_MAIN = 28 * 2**20
VMEM_FINISH = 8 * 2**20
AXES = ("gx", "gy", "gz")
MESH = pl.DeviceIdType.MESH
TILE = 8
PLANS = (
    (True, (('gx', 'low'), ('gy', 'high'), ('gz', 'low')), (('gx', 'high'), ('gz', 'high')), False),
    (True, (('gx', 'low'), ('gy', 'high'), ('gz', 'low')), (('gx', 'high'), ('gz', 'high')), True),
)
DIRS = [
    (dx, dy, dz)
    for dx in (-1, 0, 1)
    for dy in (-1, 0, 1)
    for dz in (-1, 0, 1)
    if (dx, dy, dz) != (0, 0, 0)
]
DIRS.sort(key=lambda d: -sum(map(abs, d)))


def dot(left, right):
    return jnp.dot(left, right, preferred_element_type=F32)


def dot_t(left, right):
    return lax.dot_general(left, right, (((1,), (1,)), ((), ())), preferred_element_type=F32)


def outer(left, right):
    return lax.dot_general(left, right, (((0,), (0,)), ((), ())), preferred_element_type=F32)


def rim_layout(brick, times, extra):
    spots, base = {}, 0
    for d in reversed(DIRS):
        nodes = brick ** (3 - sum(map(abs, d)))
        rows = times * nodes + extra * max(nodes // TILE, 1)
        spots[d] = (base, rows)
        base += -(-rows // TILE) * TILE
    return spots, base


def rim_tiles(brick):
    spots, base = {}, 0
    for d in reversed(DIRS):
        spots[d] = (base, rim_rows(d, brick))
        base += spots[d][1]
    return spots, base


def message_rows(layout):
    return sum(rows for _, rows in layout.values())


def rim_rows(d, brick):
    return max(brick ** (3 - sum(map(abs, d))), TILE)


def rim_place(d, sign, brick):
    return [None if s == 0 else (brick - 1 if s * sign > 0 else 0) for s in d]


def rim_slices(d, sign, brick):
    x, y, z = rim_place(d, sign, brick)
    face = brick * brick
    if z is None:
        if y is None:
            return [pl.ds(x * face, face)]
        if x is None:
            return [pl.ds(i * face + y * brick, brick) for i in range(brick)]
        return [pl.ds(x * face + y * brick, brick)]
    if x is None and y is None:
        return [pl.ds(z, face, stride=brick)]
    if y is None:
        return [pl.ds(x * face + z, brick, stride=brick)]
    if x is None:
        return [pl.ds(y * brick + z, brick, stride=face)]
    return [pl.ds(x * face + y * brick + z, 1)]


def rim_load(ref, d, sign, brick):
    parts = [ref[s, :] for s in rim_slices(d, sign, brick)]
    if len(parts) > 1:
        return jnp.concatenate(parts, axis=0)
    if parts[0].shape[0] < 8:
        return jnp.broadcast_to(parts[0], (8, parts[0].shape[1]))
    return parts[0]


def rim_add(ref, d, brick, values):
    slices = rim_slices(d, -1, brick)
    for i, s in enumerate(slices):
        rows = s.size
        ref[s, :] = ref[s, :] + values[i * rows : (i + 1) * rows]


def axis_part(sizes, a, part):
    low = 2 if sizes[a] % 2 == 0 else 1
    return {"all": (1, sizes[a]), "low": (1, low), "high": (low, sizes[a] // low)}[part]


def plan_sizes(sizes, plan):
    pre, ring, rest, _ = plan
    cores = axis_part(sizes, "gy", "low")[1] if pre else 1
    members = math.prod(axis_part(sizes, a, p)[1] for a, p in ring)
    rest = [(a, p) for a, p in rest if axis_part(sizes, a, p)[1] > 1]
    return cores, members, rest


def sent_rows(sizes, plan, rows):
    cores, members, rest = plan_sizes(sizes, plan)
    piece = rows // (cores * members)
    total = (members - 1) * piece + sum(axis_part(sizes, a, p)[1] - 1 for a, p in rest) * piece
    if plan[0] and plan[3]:
        total += (cores * members - 1) * piece
    else:
        total += (members - 1) * piece + (cores > 1) * rows // cores
    return total + (cores > 1) * rows // cores


class Group:
    def __init__(self, sizes, pos, axes):
        self.pos, self.axes = pos, [(a, *axis_part(sizes, a, p)) for a, p in axes]
        self.size = math.prod(n for _, _, n in self.axes)
        self.here = [lax.rem(pos[a] // f, n) if f * n < sizes[a] else pos[a] // f for a, f, n in self.axes]
        self.rank = self.fold(self.here)

    def fold(self, spots):
        rank = 0
        for (_, _, n), spot in zip(self.axes, spots):
            rank = rank * n + spot
        return rank

    def meet(self, j):
        spots, place = [], dict(self.pos)
        for (a, f, n), here in reversed(list(zip(self.axes, self.here))):
            digit, j = j % n, j // n
            there = here
            if digit > 0:
                there = 1 - here if n == 2 else lax.rem(here + digit, n)
                place[a] = place[a] + (there - here) * f
            spots.append(there)
        return self.fold(reversed(spots)), place

    def other(self, j):
        return self.meet(j)[1]

    def steps(self, j):
        steps = []
        for a, f, n in reversed(self.axes):
            if j % n != 0:
                steps.append((a, f, n, j % n))
            j = j // n
        return tuple(sorted(steps))

    def steps(self, j):
        steps = []
        for a, f, n in reversed(self.axes):
            if j % n != 0:
                steps.append((a, f, n, j % n))
            j = j // n
        return tuple(sorted(steps))

    def far_first(self):
        hops = lambda j: sum((a, f, n) != ("gy", 1, 2) for a, f, n, _ in self.steps(j))
        return sorted(range(1, self.size), key=lambda j: -hops(j))


def kernel(
    sizes,
    offs_hbm, node_hbm, edge_hbm, cop_hbm, wei_hbm, weo_hbm, wni_hbm, wno_hbm, cot_hbm,
    o_node, o_edge, gn, ge,
    offs, node_ref, edges, cop_ref, wei, weo, wni, wno, cot_ref, pad_a, pad_s, sl,
    field, quant, hst0, hrc0, hst1, hrc1, est, erc, zero, spill, node_t, edges_t,
    ng, eg, cbn, cbe, rbn, rbe, exn, exe,
    in_sem, rim_sem, sum_sem, ex_sem,
):
    width = node_ref.shape[1]
    count = node_ref.shape[0]
    kinds = offs.shape[0]
    brick = pad_a.shape[2]
    cube = (brick, brick, brick, width)
    pos = {a: lax.axis_index(a) for a in AXES}
    spots, rim = rim_tiles(brick)

    moves = (
        [(cop_hbm, cop_ref), (offs_hbm, offs), (node_hbm, node_ref), (wei_hbm, wei), (edge_hbm, edges)]
        + [(wni_hbm, wni), (cot_hbm, cot_ref), (wno_hbm, wno), (weo_hbm, weo)]
    )
    fetches = [
        pltpu.make_async_copy(src, dst, in_sem.at[i]) for i, (src, dst) in zip((0, 1, 2, 2, 3, 4, 4, 4, 4), moves)
    ]

    def landed(i, refs):
        rows = edges.at[pl.ds(0, sum(ref.shape[0] for ref in refs))]
        pltpu.make_async_copy(rows, rows, in_sem.at[i]).wait()

    for fetch in fetches[:5]:
        fetch.start()

    inside = {(a, s): (pos[a] + s >= 0) & (pos[a] + s < sizes[a]) for a in AXES for s in (-1, 1)}
    there = {d: functools.reduce(jnp.logical_and, [inside[a, s] for a, s in zip(AXES, d) if s != 0]) for d in DIRS}

    def shifted(d, sign):
        return {a: pos[a] + sign * step for a, step in zip(AXES, d)}

    plans = []
    for pre, ring, rest, direct in PLANS:
        rest = plan_sizes(sizes, (pre, ring, rest, direct))[2]
        core = Group(sizes, pos, (("gy", "low"),) if pre else ())
        share = Group(sizes, pos, ((("gy", "low"),) if pre and direct else ()) + ring)
        plans.append((core, Group(sizes, pos, ring), [Group(sizes, pos, (ap,)) for ap in rest], share))

    def nodes_of(d):
        return brick ** (3 - sum(map(abs, d)))

    rims = (
        (hst0, hrc0, rim_layout(brick, 1, 1)[0]),
        (hst1, hrc1, rim_layout(brick, 1, 0)[0]),
        (est, erc, rim_layout(brick, 2, 0)[0]),
    )
    unsent = rim_layout(brick, 4, 1)[0]
    divisor_tiles = [start + nodes_of(d) // TILE * TILE for d, (start, _) in rims[0][2].items()]
    for d, spot in zip(rims[0][2], divisor_tiles):
        if nodes_of(d) < brick * brick:
            hrc0[pl.ds(spot, TILE), :] = jnp.zeros((TILE, width), F32)
    barrier = pltpu.get_barrier_semaphore()

    def greet(place):
        pl.semaphore_signal(barrier, inc=1, device_id=place, device_id_type=MESH)

    waits = jnp.int32(0)
    for d in DIRS:
        waits = waits + there[d].astype(jnp.int32)

        @pl.when(there[d])
        def _(d=d):
            greet(shifted(d, 1))

    met = set()
    for core, ring, rest, share in plans:
        for group in (core, ring, share, *rest):
            for j in group.far_first():
                steps = group.steps(j)
                if steps not in met and any((f, n) != (1, 2) for _, f, n, _ in steps):
                    met.add(steps)
                    waits = waits + 1
                    greet(group.other(j))

    for fetch in fetches[5:]:
        fetch.start()
    def rim_copy(r, start, rows, place):
        src, dst = rims[r][:2]
        return pltpu.make_async_remote_copy(
            src_ref=src.at[pl.ds(start, rows)],
            dst_ref=dst.at[pl.ds(start, rows)],
            send_sem=rim_sem.at[3],
            recv_sem=rim_sem.at[r],
            device_id=place,
            device_id_type=MESH,
        )

    def rim_start(r):
        for d in reversed(DIRS) if r == 1 else DIRS:

            @pl.when(there[d])
            def _(d=d):
                rim_copy(r, *rims[r][2][d], shifted(d, 1)).start()

    def rim_whole(r):
        return rim_copy(r, 0, message_rows(rims[r][2]), pos)

    def rows_at(ref, index, rows):
        return ref.at[pl.ds(pl.multiple_of(index * rows, 8), rows)]

    sums = ((ng, cbn, rbn, exn, gn), (eg, cbe, rbe, exe, ge))

    def sum_copy(w, stage, src, dst, place):
        return pltpu.make_async_remote_copy(
            src_ref=src,
            dst_ref=dst,
            send_sem=rim_sem.at[3],
            recv_sem=sum_sem.at[w, stage],
            device_id=place,
            device_id_type=MESH,
        )

    def core_copy(w):
        core, buf, got = plans[w][0], *sums[w][:2]
        return sum_copy(w, 0, rows_at(buf, 1 - core.rank, got.shape[0]), got, core.other(1))

    def core_start(w):
        if plans[w][0].size > 1:
            core_copy(w).start()

    def piece(w, ref, rank):
        core, ring = plans[w][:2]
        return rows_at(ref, core.rank * ring.size + rank, ref.shape[0] // (core.size * ring.size))

    def ring_copy(w, j):
        ring, buf, got = plans[w][1], sums[w][0], sums[w][2]
        to, place = ring.meet(j)
        return sum_copy(w, 1, piece(w, buf, to), got.at[j - 1], place)

    def ring_whole(w):
        got = sums[w][2]
        return sum_copy(w, 1, got, got, pos)

    def ring_start(w):
        core, ring = plans[w][:2]
        if core.size > 1:
            buf, got = sums[w][:2]
            half = rows_at(buf, core.rank, got.shape[0])
            core_copy(w).wait_recv()
            half[...] = half[...] + got[...]
        for j in ring.far_first():
            ring_copy(w, j).start()

    def ring_finish(w):
        ring, buf, got = plans[w][1], sums[w][0], sums[w][2]
        ring_whole(w).wait_recv()
        total = piece(w, buf, ring.rank)[...]
        for j in range(1, ring.size):
            total = total + got[j - 1]
        return total

    def ex_spots(w):
        base = 0
        for group in plans[w][2]:
            yield base, group
            base += group.size

    def ex_copy(w, e, j):
        base, group = list(ex_spots(w))[e]
        spot = sums[w][3].at[base + group.rank]
        return pltpu.make_async_remote_copy(
            src_ref=spot,
            dst_ref=spot,
            send_sem=rim_sem.at[3],
            recv_sem=ex_sem.at[w, base - e + j - 1],
            device_id=group.other(j),
            device_id_type=MESH,
        )

    def ex_start(w, e, total):
        base, group = list(ex_spots(w))[e]
        sums[w][3][base + group.rank] = total
        for j in range(1, group.size):
            ex_copy(w, e, j).start()

    def ex_finish(w, e):
        base, group = list(ex_spots(w))[e]
        buf = sums[w][3]
        for j in range(1, group.size):
            ex_copy(w, e, j).wait_recv()
        total = buf[base]
        for r in range(1, group.size):
            total = total + buf[base + r]
        return total

    def ex_first(w):
        total = ring_finish(w)
        if len(plans[w][2]) > 0:
            ex_start(w, 0, total)
        return total

    def ex_all(w, total):
        for e in range(len(plans[w][2])):
            total = ex_finish(w, e)
            if e + 1 < len(plans[w][2]):
                ex_start(w, e + 1, total)
        return total

    def share_start(w, total):
        _, ring, _, share = plans[w]
        spot = piece(w, sums[w][4], ring.rank)
        spot[...] = total
        for j in share.far_first():
            sum_copy(w, 2, spot, spot, share.other(j)).start()

    def share_whole(w):
        ring, share, out = plans[w][1], plans[w][3], sums[w][4]
        core = plans[w][0].size
        rows = out.shape[0] // (core * ring.size) * (share.size - 1)
        some = out.at[pl.ds(0, rows)]
        return sum_copy(w, 2, some, some, pos)

    def passes(w):
        core, ring, _, share = plans[w]
        return core.size > 1 and share.size == ring.size

    def pass_copy(w):
        core, out = plans[w][0], sums[w][4]
        half = rows_at(out, core.rank, out.shape[0] // core.size)
        return sum_copy(w, 3, half, half, core.other(1))

    def share_finish(w):
        share_whole(w).wait_recv()
        if passes(w):
            pass_copy(w).start()

    def put(ref, start, d, source):
        ref[pl.ds(start, nodes_of(d)), :] = rim_load(source, d, 1, brick)[: nodes_of(d)]

    def get(ref, start, d):
        values = ref[pl.ds(start, nodes_of(d)), :]
        return values if nodes_of(d) >= TILE else jnp.broadcast_to(values, (TILE, width))

    order = list(reversed(DIRS))
    pad_a[...] = jnp.zeros_like(pad_a)
    pad_s[...] = jnp.zeros_like(pad_s)
    coords = []
    for axis in range(3):
        shape = [brick if i in (axis, 2) else 1 for i in range(3)] + [width]
        coords.append(lax.broadcasted_iota(jnp.int32, shape, axis))

    fetches[0].wait()
    scale_rows = lax.broadcasted_iota(jnp.int32, (count, brick * brick), 0) // brick
    scale_cols = lax.broadcasted_iota(jnp.int32, (count, brick * brick), 1)
    picked = dot(
        (scale_rows == scale_cols).astype(BF16), cop_ref[...].astype(F32).astype(BF16)
    )
    lane = lax.broadcasted_iota(jnp.int32, (count, brick), 1)
    row = lax.broadcasted_iota(jnp.int32, (count, brick), 0) % brick
    picked = jnp.where(lane == row, picked, 0.0).astype(BF16)
    quant[0] = dot(picked, jnp.ones((brick, width), BF16))
    rim_lane = lax.broadcasted_iota(jnp.int32, (rim, width), 1)
    rim_row = lax.broadcasted_iota(jnp.int32, (rim, width), 0) % TILE
    divisors = jnp.concatenate([rim_load(quant.at[0], d, 1, brick) for d in order], axis=0)
    divisors = jnp.where(rim_lane == rim_row, divisors, 0.0).astype(BF16)
    groups = -(-rim // (TILE * TILE)) * TILE
    gather = lax.broadcasted_iota(jnp.int32, (groups, rim), 1) // TILE
    gather = (gather == lax.broadcasted_iota(jnp.int32, (groups, rim), 0)).astype(BF16)
    compact = dot(gather, divisors)
    for d in order:
        start, rows = rims[0][2][d]
        first, n = spots[d][0] // TILE, rim_rows(d, brick) // TILE
        hst0[pl.ds(start + rows - n, n), :] = compact[first : first + n]

    fetches[1].wait()
    landed(2, (node_ref, wei))
    node = node_ref[...]
    pad_a[1 : brick + 1, 1 : brick + 1] = dot(node, wei[:width]).reshape(cube)
    received = dot(node, wei[width : 2 * width])
    fetches[4].wait()
    hidden_sum = None
    for k in range(kinds):
        o = [offs[k, axis] for axis in range(3)]
        sent = pad_a[pl.ds(1 + o[0], brick), pl.ds(1 + o[1], brick)]
        sent = pltpu.roll(sent.reshape(brick * brick, brick, width), lax.rem(brick - o[2], brick), 1)
        pre = dot(edges[k * count : (k + 1) * count], wei[2 * width :])
        pre = pre + received + sent.reshape(count, width)
        sigma = 0.5 * jnp.tanh(0.5 * pre) + 0.5
        hidden = pre * sigma
        valid = None
        for axis in range(3):
            here = coords[axis] + o[axis]
            one = jnp.where((here >= 0) & (here < brick), 1.0, 0.0)
            valid = one if valid is None else valid * one
        valid = valid.reshape(count, width) > 0.0
        sl[k] = jnp.where(valid, sigma + hidden * (1.0 - sigma), 0.0)
        hidden = jnp.where(valid, hidden, 0.0).astype(BF16)
        wide = hidden.astype(F32)
        hidden_sum = wide if hidden_sum is None else hidden_sum + wide
    field[0] = hidden_sum
    for d in order:
        put(hst0, rims[0][2][d][0], d, field.at[0])
    pl.semaphore_wait(barrier, waits)
    rim_start(0)

    landed(4, (wni, cot_ref, wno, weo))
    cot = cot_ref[...]
    quant[1] = dot(node, wni[:width])
    quant[2] = dot_t(cot, wno[...])
    for d in order:
        start, rows = rims[2][2][d]
        put(est, start, d, quant.at[1])
        put(est, start + rows // 2, d, quant.at[2])
    rim_start(2)
    zero[...] = jnp.zeros_like(zero)
    def fill(exchanges, leaving):
        for d in DIRS:
            back = tuple(-step for step in d)

            @pl.when(jnp.logical_not(there[d]))
            def _(d=d, back=back):
                for r in exchanges:
                    _, dst, layout = rims[r]
                    start, rows = layout[back]
                    arrival = dst.at[pl.ds(start, rows)]
                    pltpu.make_async_copy(zero.at[pl.ds(0, rows)], arrival, rim_sem.at[r]).start()
                if leaving:
                    start, rows = unsent[d]
                    pltpu.make_async_copy(zero.at[pl.ds(0, rows)], spill.at[pl.ds(start, rows)], rim_sem.at[3]).start()

    fill((0, 2), False)
    node_t[...] = node.T
    pad_s[0, 1 : brick + 1, 1 : brick + 1] = node.astype(F32).reshape(cube)
    for k in range(kinds):
        o = [offs[k, axis] for axis in range(3)]
        sent = pad_s[0, pl.ds(1 + o[0], brick), pl.ds(1 + o[1], brick)]
        sent = pltpu.roll(sent.reshape(brick * brick, brick, width), lax.rem(brick - o[2], brick), 1)
        columns = pl.ds(k * count, count)
        edges_t[:width, columns] = sent.reshape(count, width).astype(BF16).T
        edges_t[width:, columns] = edges[columns, :].T
    cot_t = cot.T
    quant[0] = 1.0 / quant[0]
    w_out = weo[...]
    twice = jnp.concatenate([w_out, w_out], axis=0)
    tiles = TILE * len(order)
    faces = 6 * brick * brick
    place = lax.broadcasted_iota(jnp.int32, (rim, tiles), 0)
    corners = faces + 12 * brick
    second = jnp.where(place < corners, 0, 1)
    place = jnp.where(place < faces, place // TILE, faces // TILE + (place - faces) // TILE * TILE + second)
    spread = (place == lax.broadcasted_iota(jnp.int32, (rim, tiles), 1)).astype(BF16)

    def node_step(summed, inverse, own, upstream):
        gathered = (summed * inverse).astype(BF16)
        pre = own + dot(gathered, wni[width:])
        sigma = 0.5 * jnp.tanh(0.5 * pre) + 0.5
        hidden = pre * sigma
        slope = (upstream * (sigma + hidden * (1.0 - sigma))).astype(BF16)
        return gathered, hidden, slope, dot_t(slope, wni[width:]) * inverse

    rim_whole(0).wait_recv()
    for d in order:
        rim_add(field.at[0], d, brick, get(hrc0, rims[0][2][d][0], d))
    total = field[0]
    big = total.astype(BF16)
    small = (total - big.astype(F32)).astype(BF16)
    summed = dot(jnp.concatenate([big, small], axis=1), twice)
    field[0] = summed
    gathered, hidden, slope, to_agg = node_step(summed, quant[0], quant[1], quant[2])
    field[1] = to_agg
    ng[:width] = dot(node_t[...], slope)
    ng[width : 2 * width] = outer(gathered, slope)
    ng[2 * width : 3 * width] = dot(cot_t, hidden.astype(BF16)).T
    ng[3 * width :] = outer(big, to_agg.astype(BF16))
    core_start(0)

    compact = jnp.concatenate([hrc0[pl.ds(spot, TILE), :] for spot in divisor_tiles], axis=0).astype(BF16)
    divisors = jnp.where(rim_lane == rim_row, dot(spread, compact), 0.0).astype(BF16)
    divisors = 1.0 / jnp.maximum(dot(divisors, jnp.ones((width, width), BF16)), 1.0)
    beyond = jnp.concatenate([rim_load(field.at[0], d, -1, brick) for d in order], axis=0)
    rim_whole(2).wait_recv()
    own = jnp.concatenate([get(erc, rims[2][2][d][0], d) for d in order], axis=0)
    upstream = jnp.concatenate([get(erc, rims[2][2][d][0] + rims[2][2][d][1] // 2, d) for d in order], axis=0)
    to_rim = node_step(beyond, divisors, own, upstream)[3]
    for d in order:
        start, rows = spots[d]
        rim_add(field.at[1], d, brick, to_rim[start : start + rows])

    ring_start(0)
    arriving = field[1].astype(BF16)
    back = dot_t(arriving, w_out)
    slopes = []
    direct = None
    for k in range(kinds):
        slope_k = (back * sl[k]).astype(BF16)
        slopes.append(slope_k)
        wide = slope_k.astype(F32)
        direct = wide if direct is None else direct + wide
    direct = direct.astype(BF16)
    slope_all = jnp.concatenate(slopes, axis=0)
    both = dot(edges_t[...], slope_all)
    eg[:width] = both[:width]
    eg[width : 2 * width] = dot(node_t[...], direct)
    eg[2 * width :] = both[width:]
    core_start(1)
    turned = None
    for k in range(kinds):
        o = [offs[k, axis] for axis in range(3)]
        pad_s[k, 1 : brick + 1, 1 : brick + 1] = slopes[k].astype(F32).reshape(cube)
        moved = pad_s[k, pl.ds(1 - o[0], brick), pl.ds(1 - o[1], brick)]
        moved = pltpu.roll(moved.reshape(brick * brick, brick, width), lax.rem(brick + o[2], brick), 1)
        turned = moved if turned is None else turned + moved
    turned = turned.reshape(count, width).astype(BF16)
    local = cot.astype(F32) + dot_t(slope, wni[:width])
    local = local + dot_t(turned, wei[:width]) + dot_t(direct, wei[width : 2 * width])
    field[1] = local
    ring_start(1)
    for d in order:
        put(hst1, rims[1][2][d][0], d, field.at[1])
    o_edge[...] = dot_t(slope_all, wei[2 * width :]).astype(BF16)
    fill((1,), True)
    firsts = [ex_first(w) for w in range(2)]
    rim_start(1)
    for w in range(2):
        share_start(w, ex_all(w, firsts[w]))
    rim_whole(1).wait_recv()
    for d in order:
        rim_add(field.at[1], d, brick, get(hrc1, rims[1][2][d][0], d))
    o_node[...] = field[1].astype(BF16)
    for w in range(2):
        share_finish(w)
    for w in range(2):
        if passes(w):
            pass_copy(w).wait_recv()

    pltpu.make_async_copy(spill, spill, rim_sem.at[3]).wait()


def finish(node_in, edge_in, gn, ge, o_node, o_edge, o_ei, o_eo, o_ni, o_no, s_ei, s_n, sems):
    width = gn.shape[1]
    moves = [
        pltpu.make_async_copy(edge_in, o_edge, sems.at[0]),
        pltpu.make_async_copy(node_in, o_node, sems.at[1]),
    ]
    for move in moves:
        move.start()
    totals = [ref[...] for ref in (gn, ge)]
    squares = sum(jnp.sum(t * t, axis=0, keepdims=True) for t in totals)
    squares = jnp.sum(squares, axis=1, keepdims=True)
    entries = sum(t.shape[0] for t in totals) * width
    factor = math.sqrt(entries) / jnp.sqrt(squares)
    s_n[...] = totals[0] * factor
    outs = ((s_n.at[: 2 * width], o_ni), (s_n.at[2 * width : 3 * width], o_no), (s_n.at[3 * width :], o_eo), (s_ei, o_ei))
    for i, (src, dst) in enumerate(outs):
        if src is s_ei:
            s_ei[...] = totals[1] * factor
        moves.append(pltpu.make_async_copy(src, dst, sems.at[2 + i]))
        moves[-1].start()
    for move in moves:
        move.wait()


def on_device(
    sizes, node_feat, edge_feat, copies, offsets, w_edge_in, w_edge_out, w_node_in, w_node_out, node_cot
):
    brick = node_feat.shape[0]
    width = node_feat.shape[3]
    kinds = edge_feat.shape[0]
    count = brick**3
    rims = [rim_layout(brick, *how)[1] for how in ((1, 1), (1, 0), (2, 0))]
    dims = [plan_sizes(sizes, plan) for plan in PLANS]
    others = [max(sum(axis_part(sizes, a, p)[1] for a, p in rest), 1) for _, _, rest in dims]
    sent = message_rows(rim_layout(brick, 4, 1)[0])
    sent += sum(sent_rows(sizes, plan, n * width) for plan, n in zip(PLANS, (4, 3)))
    vmem = pl.BlockSpec(memory_space=pltpu.VMEM)
    hbm = pl.BlockSpec(memory_space=pl.ANY)
    far = pl.BlockSpec(memory_space=pltpu.HBM)
    dma = pltpu.SemaphoreType.DMA
    b, w = brick, width
    rows = (4 * w, 3 * w)
    outs = pl.pallas_call(
        functools.partial(kernel, sizes),
        out_shape=(
            jax.ShapeDtypeStruct((count, w), BF16),
            jax.ShapeDtypeStruct((kinds * count, w), BF16),
            *[jax.ShapeDtypeStruct((r, w), F32) for r in rows],
        ),
        in_specs=[far] * 9,
        out_specs=(vmem, vmem, vmem, vmem),
        scratch_shapes=[
            pltpu.SMEM(offsets.shape, jnp.int32),
            pltpu.VMEM((count, w), BF16),
            pltpu.VMEM((kinds * count, w), BF16),
            pltpu.VMEM((b * b, b), jnp.int32),
            pltpu.VMEM((3 * w, w), BF16),
            pltpu.VMEM((w, w), BF16),
            pltpu.VMEM((2 * w, w), BF16),
            pltpu.VMEM((w, w), BF16),
            pltpu.VMEM((count, w), BF16),
            pltpu.VMEM((b + 2, b + 2, b, w), F32),
            pltpu.VMEM((kinds, b + 2, b + 2, b, w), F32),
            pltpu.VMEM((kinds, count, w), F32),
            pltpu.VMEM((2, count, w), F32),
            pltpu.VMEM((3, count, w), F32),
            *[pltpu.VMEM((r, w), F32) for r in (rims[0], rims[0], rims[1], rims[1], rims[2], rims[2])],
            pltpu.VMEM((4 * b * b + TILE, w), F32),
            pltpu.VMEM((sent, w), F32),
            pltpu.VMEM((w, count), BF16),
            pltpu.VMEM((2 * w, kinds * count), BF16),
            *[pltpu.VMEM((r, w), F32) for r in rows],
            *[pltpu.VMEM((r // c, w), F32) for r, (c, _, _) in zip(rows, dims)],
            *[pltpu.VMEM((m - 1, r // (c * m), w), F32) for r, (c, m, _) in zip(rows, dims)],
            *[pltpu.VMEM((n, r // (c * m), w), F32) for r, n, (c, m, _) in zip(rows, others, dims)],
            dma((5,)),
            dma((4,)),
            dma((2, 4)),
            dma((2, max(max(n - len(rest) for n, (_, _, rest) in zip(others, dims)), 1))),
        ],
        compiler_params=pltpu.CompilerParams(
            collective_id=0, has_side_effects=True, vmem_limit_bytes=VMEM_MAIN
        ),
    )(
        pltpu.with_memory_space_constraint(offsets, pltpu.HBM),
        *[
            pltpu.with_memory_space_constraint(array, pltpu.HBM)
            for array in (
                node_feat.reshape(count, w),
                edge_feat.reshape(kinds * count, w),
                copies.reshape(b * b, b),
                w_edge_in,
                w_edge_out,
                w_node_in,
                w_node_out,
                node_cot.reshape(count, w),
            )
        ],
    )
    done = pl.pallas_call(
        finish,
        out_shape=(
            jax.ShapeDtypeStruct((count, w), BF16),
            jax.ShapeDtypeStruct((kinds * count, w), BF16),
            jax.ShapeDtypeStruct((3 * w, w), F32),
            jax.ShapeDtypeStruct((w, w), F32),
            jax.ShapeDtypeStruct((2 * w, w), F32),
            jax.ShapeDtypeStruct((w, w), F32),
        ),
        in_specs=[hbm, hbm, vmem, vmem],
        out_specs=(hbm,) * 6,
        scratch_shapes=[pltpu.VMEM((rows[1], w), F32), pltpu.VMEM((rows[0], w), F32), dma((6,))],
        compiler_params=pltpu.CompilerParams(vmem_limit_bytes=VMEM_FINISH),
    )(*outs)
    return (done[0].reshape(node_feat.shape), done[1].reshape(edge_feat.shape)) + tuple(done[2:])


def solution(mesh):
    sizes = {a: mesh.shape[a] for a in AXES}
    bricks, edges = P("gx", "gy", "gz", None), P(None, "gx", "gy", "gz", None)
    return jax.shard_map(
        functools.partial(on_device, sizes),
        mesh=mesh,
        in_specs=(bricks, edges, P("gx", "gy", "gz"), P(), P(), P(), P(), P(), bricks),
        out_specs=(bricks, edges, P(), P(), P(), P()),
        check_vma=False,
    )
```
